512 devices in a mesh: grp: 16 (over y, core), path: 32 (over z, x).
Axes of the slice: x: 4, y: 8, z: 8, core: 2. Of those that a mesh axis runs over, the one named last changes fastest.
Arguments:
- link_state: bfloat16 [16, 16384, 256], P('grp', 'path'), may hold values from -6 to 6
- path_state: bfloat16 [16, 4096, 256], P('grp', 'path'), may hold values from -6 to 6
- path_links: int32 [4096, 8], P('path'), may hold values from -1 to 16383, as said below
- w_path_in: bfloat16 [256, 768], replicated, may hold values from -0.375 to 0.375
- w_path_hid: bfloat16 [256, 768], replicated, may hold values from -0.375 to 0.375
- w_link_in: bfloat16 [256, 768], replicated, may hold values from -0.375 to 0.375
- w_link_hid: bfloat16 [256, 768], replicated, may hold values from -0.375 to 0.375
- cotangent: bfloat16 [16, 4096, 128], P('grp', 'path'), may hold values from -0.0234375 to 0.0234375
Outputs:
- link_next: bfloat16 [16, 16384, 256], P('grp', 'path')
- path_final: bfloat16 [16, 4096, 256], P('grp', 'path')
- read_grad: float32 [128, 256], P('path')
The draws below stay inside these ranges and needn't reach their ends.
Inputs may be any that keep to these rules, and one draw needn't show every extreme that they name: `path_links`: entry -1 marks no hop; each path's live entries come first and number two or more. In the rows of one device, at most 32 live entries name links of the block of 512 link ids held by any one index of path, and some block takes exactly 32.
All inputs are finite; a program needn't handle non-finite values.
Results may differ from the reference program's by a relative error of at most 0.0035.
Values may be sent and summed in bfloat16 or wider, within the bound.
A program may use at most 64 MiB of HBM per device.

```python
import jax
import jax.numpy as jnp
from jax import lax

H = 256
RD = 128
HOPS = 8
PATH_DEV = 128
LINK_DEV = 512
CAP = 32
PATHS = 4096
LINKS = 16384
SAMPLES = 16


def draw_block(key, blocks):
    keys = jax.random.split(key, 5)
    entries = PATH_DEV * HOPS
    lengths = jax.random.randint(keys[0], (PATH_DEV,), 2, HOPS + 1)
    live = (jnp.arange(HOPS)[None, :] < lengths[:, None]).reshape(-1)
    ranks = jax.random.permutation(keys[1], entries).astype(jnp.int32)
    entry_keys = jnp.where(live, 0, entries) + ranks
    sorted_pos = jnp.argsort(entry_keys, stable=True)
    forced = jax.random.randint(keys[2], (), 0, blocks)
    slot_ids = jnp.arange(blocks * CAP)
    slot_keys = jnp.where(slot_ids // CAP == forced, 0, blocks * CAP) + jax.random.permutation(keys[3], blocks * CAP).astype(jnp.int32)
    slot_order = jnp.argsort(slot_keys, stable=True)
    owners_sorted = (slot_order[:entries] // CAP).astype(jnp.int32)
    live_total = jnp.sum(live.astype(jnp.int32))
    owners_sorted = jnp.where(jnp.arange(entries) < live_total, owners_sorted, -1)
    owner_entry = jnp.zeros((entries,), jnp.int32).at[sorted_pos].set(owners_sorted)
    link_ids = owner_entry * LINK_DEV + jax.random.randint(keys[4], (entries,), 0, LINK_DEV)
    return jnp.where(owner_entry >= 0, link_ids, -1).astype(jnp.int32).reshape(PATH_DEV, HOPS)


def draw_path_links(key, part):
    blocks = PATHS // PATH_DEV
    every = jax.vmap(lambda index: draw_block(jax.random.fold_in(key, index), blocks))(jnp.arange(blocks))
    return every.reshape(PATHS, HOPS)


def spiked(values, stream_key, source, target, blocks, factor):
    def block_of(axis_at):
        return (jnp.arange(values.shape[axis_at]) // (values.shape[axis_at] // blocks)).reshape((-1,) + (1,) * (values.ndim - 1 - axis_at))

    first = jax.random.permutation(stream_key, blocks)[block_of(target)]
    other_side = (block_of(target) + blocks // 2) % blocks
    return jnp.where((block_of(source) == first) | (block_of(source) == other_side), factor * values, values)


def block_levels(own_key, dims, cuts, least, top_value):
    factor_of = 1.0
    for position, parts in cuts:
        heights = jax.random.uniform(jax.random.fold_in(jax.random.fold_in(own_key, 6), position), (parts,), jnp.float32, least / len(cuts), top_value / len(cuts))
        factor_of = factor_of * jnp.repeat(jnp.exp(heights), dims[position] // parts).reshape((-1,) + (1,) * (len(dims) - 1 - position))
    return factor_of


def normal_values(own_key, extent, spread, bound, cuts=(), dtype=jnp.bfloat16):
    values = spread * jax.random.normal(own_key, extent, jnp.float32)
    if cuts:
        values = values * block_levels(own_key, extent, cuts, -0.22, 0.18)
    return jnp.clip(values, -bound, bound).astype(dtype)


def noise_with(own_key, extent, deviation, limit, pieces, heavy, kind=jnp.bfloat16):
    result = deviation * jax.random.normal(own_key, extent, jnp.float32)
    if pieces:
        result = result * block_levels(own_key, extent, pieces, -0.22, 0.18)
    return jnp.clip(spiked(result, jax.random.fold_in(own_key, 3), *heavy), -limit, limit).astype(kind)


def setup_inputs(seed: int = 0) -> dict:
    streams_of = jax.random.split(jax.random.key(seed), 9)
    return {
        "link_state": normal_values(streams_of[0], (SAMPLES, LINKS, H), 1.0, 6.0, ((0, 16), (1, 32))),
        "path_state": normal_values(streams_of[1], (SAMPLES, PATHS, H), 1.0, 6.0, ((0, 16), (1, 32))),
        "path_links": draw_path_links(jax.random.fold_in(streams_of[8], 71), 0),
        "w_path_in": normal_values(streams_of[3], (H, 3 * H), H ** -0.5, 0.375),
        "w_path_hid": normal_values(streams_of[4], (H, 3 * H), H ** -0.5, 0.375),
        "w_link_in": normal_values(streams_of[5], (H, 3 * H), H ** -0.5, 0.375),
        "w_link_hid": normal_values(streams_of[6], (H, 3 * H), H ** -0.5, 0.375),
        "cotangent": noise_with(streams_of[7], (SAMPLES, PATHS, RD), (1.0 / (SAMPLES * PATHS) ** 0.5), 0.0234375, ((0, 16), (1, 32)), (1, 2, 32, 2.75)),
    }


def gated_update(projected, carried, w_hidden):
    width = carried.shape[1]
    recur = jnp.dot(carried.astype(jnp.bfloat16), w_hidden, preferred_element_type=jnp.float32)
    reset = jax.nn.sigmoid(projected[:, :width] + recur[:, :width])
    update = jax.nn.sigmoid(projected[:, width:2 * width] + recur[:, width:2 * width])
    candidate = jnp.tanh(projected[:, 2 * width:] + reset * recur[:, 2 * width:])
    return (1.0 - update) * candidate + update * carried


def one_sample(sample_pair, path_links, w_path_in, w_path_hid, w_link_in, w_link_hid):
    link_state, path_state = sample_pair
    is_live = path_links >= 0
    safe_ids = jnp.where(is_live, path_links, 0)
    fetched = jnp.where(is_live[:, :, None], link_state[safe_ids], jnp.zeros((), jnp.bfloat16))
    width = link_state.shape[1]
    path_count = path_links.shape[0]
    hop_count = path_links.shape[1]
    projected = jnp.dot(fetched.reshape(-1, width), w_path_in, preferred_element_type=jnp.float32)
    projected = projected.reshape(path_count, hop_count, 3 * width)
    carried = path_state.astype(jnp.float32)
    messages = []
    for hop_index in range(hop_count):
        renewed = gated_update(projected[:, hop_index], carried, w_path_hid)
        carried = jnp.where(is_live[:, hop_index, None], renewed, carried)
        messages.append(carried.astype(jnp.bfloat16))
    stacked = jnp.stack(messages, axis=1).reshape(-1, width).astype(jnp.float32)
    targets = jnp.where(is_live, path_links, link_state.shape[0]).reshape(-1)
    link_sum = jnp.zeros(link_state.shape, jnp.float32).at[targets].add(stacked, mode="drop")
    link_proj = jnp.dot(link_sum.astype(jnp.bfloat16), w_link_in, preferred_element_type=jnp.float32)
    link_next = gated_update(link_proj, link_state.astype(jnp.float32), w_link_hid).astype(jnp.bfloat16)
    return link_next, carried.astype(jnp.bfloat16)


def reference(link_state, path_state, path_links, w_path_in, w_path_hid, w_link_in, w_link_hid, cotangent):
    link_next, path_final = lax.map(
        lambda sample_pair: one_sample(sample_pair, path_links, w_path_in, w_path_hid, w_link_in, w_link_hid),
        (link_state, path_state))
    read_grad = jnp.einsum("spr,sph->rh", cotangent.astype(jnp.float32), path_final.astype(jnp.float32))
    return link_next, path_final, read_grad
```

```python
import jax
import jax.numpy as jnp
from jax import lax
from jax.sharding import PartitionSpec as P


def gated_update(projected, carried, w_hidden):
    width = carried.shape[1]
    recur = jnp.dot(carried.astype(jnp.bfloat16), w_hidden, preferred_element_type=jnp.float32)
    reset = jax.nn.sigmoid(projected[:, :width] + recur[:, :width])
    update = jax.nn.sigmoid(projected[:, width : 2 * width] + recur[:, width : 2 * width])
    candidate = jnp.tanh(projected[:, 2 * width :] + reset * recur[:, 2 * width :])
    return (1.0 - update) * candidate + update * carried


def shards(
    link_state, path_state, path_links, w_path_in, w_path_hid, w_link_in, w_link_hid, cotangent
):
    bf16, f32 = jnp.bfloat16, jnp.float32
    own_links = link_state[0]
    link_dev, width = own_links.shape
    peer_count = lax.axis_size("path")
    path_count, hop_count = path_links.shape
    entries = path_count * hop_count
    capacity = entries // peer_count
    slots = peer_count * capacity
    flat_ids = path_links.reshape(-1)
    is_live = flat_ids >= 0
    owner_id = jnp.where(is_live, flat_ids // link_dev, peer_count)
    local_id = jnp.where(is_live, flat_ids % link_dev, 0)
    marks = (owner_id[:, None] == jnp.arange(peer_count)[None, :]).astype(bf16)
    order = jnp.arange(entries)
    earlier = (order[None, :] < order[:, None]).astype(bf16)
    before = jnp.dot(earlier, marks, preferred_element_type=f32)
    slot_id = jnp.sum(before * marks.astype(f32), axis=1).astype(jnp.int32)
    dest = jnp.where(is_live, owner_id * capacity + slot_id, -1)
    slot_ids = jnp.arange(slots)
    route = dest[None, :] == slot_ids[:, None]
    requests = jnp.sum(jnp.where(route, local_id[None, :] + 1, 0), axis=1) - 1
    received = lax.all_to_all(
        requests.reshape(peer_count, capacity), "path", split_axis=0, concat_axis=0, tiled=True
    ).reshape(-1)
    want = (received[:, None] == jnp.arange(link_dev)[None, :]).astype(bf16)
    served = jnp.dot(want, own_links, preferred_element_type=f32).astype(bf16)
    got = lax.all_to_all(
        served.reshape(peer_count, capacity, width), "path", split_axis=0, concat_axis=0, tiled=True
    ).reshape(slots, width)
    route_t = (dest[:, None] == slot_ids[None, :]).astype(bf16)
    fetched = jnp.dot(route_t, got, preferred_element_type=f32).astype(bf16)
    projected = jnp.dot(fetched, w_path_in, preferred_element_type=f32)
    projected = projected.reshape(path_count, hop_count, 3 * width)
    live_grid = is_live.reshape(path_count, hop_count)
    carried = path_state[0].astype(f32)
    messages = []
    for hop_index in range(hop_count):
        renewed = gated_update(projected[:, hop_index], carried, w_path_hid)
        carried = jnp.where(live_grid[:, hop_index, None], renewed, carried)
        messages.append(carried.astype(bf16))
    path_final = carried.astype(bf16)
    flat_messages = jnp.stack(messages, axis=1).reshape(-1, width)
    outgoing = jnp.dot(route.astype(bf16), flat_messages, preferred_element_type=f32).astype(bf16)
    incoming = lax.all_to_all(
        outgoing.reshape(peer_count, capacity, width), "path", split_axis=0, concat_axis=0, tiled=True
    ).reshape(slots, width)
    link_sum = lax.dot_general(
        want, incoming, (((0,), (0,)), ((), ())), preferred_element_type=f32
    )
    link_proj = jnp.dot(link_sum.astype(bf16), w_link_in, preferred_element_type=f32)
    link_next = gated_update(link_proj, own_links.astype(f32), w_link_hid).astype(bf16)
    grad_term = lax.dot_general(
        cotangent[0], path_final, (((0,), (0,)), ((), ())), preferred_element_type=f32
    )
    part = lax.psum_scatter(grad_term, "path", scatter_dimension=0, tiled=True)
    read_grad = lax.psum(part, "grp")
    return (link_next[None], path_final[None], read_grad)


def solution(mesh):
    return jax.shard_map(
        shards,
        mesh=mesh,
        in_specs=(
            P("grp", "path", None),
            P("grp", "path", None),
            P("path", None),
            P(),
            P(),
            P(),
            P(),
            P("grp", "path", None),
        ),
        out_specs=(P("grp", "path", None), P("grp", "path", None), P("path", None)),
        check_vma=False,
    )
```

```python
import jax
import jax.numpy as jnp
from jax import lax
from jax.experimental import pallas as pl
from jax.experimental.pallas import tpu as pltpu
from jax.sharding import PartitionSpec as P

MESH = pl.DeviceIdType.MESH


def _readout_kernel(n_grp, n_path, term_ref, out_ref, recv1, recv2, mid, send1, got1, send2, got2):
    g = lax.axis_index("grp")
    p = lax.axis_index("path")
    barrier = pltpu.get_barrier_semaphore()

    def greet_path(k, c):
        pl.semaphore_signal(barrier, inc=1, device_id=(g, lax.rem(p + k, n_path)), device_id_type=MESH)
        return c

    def greet_grp(k, c):
        pl.semaphore_signal(barrier, inc=1, device_id=(lax.rem(g + k, n_grp), p), device_id_type=MESH)
        return c

    lax.fori_loop(1, n_path, greet_path, 0)
    lax.fori_loop(1, n_grp, greet_grp, 0)
    pl.semaphore_wait(barrier, (n_path - 1) + (n_grp - 1))

    def path_copy(k, q):
        return pltpu.make_async_remote_copy(
            src_ref=term_ref.at[q], dst_ref=recv1.at[k - 1], send_sem=send1.at[k - 1],
            recv_sem=got1.at[k - 1], device_id=(g, q), device_id_type=MESH)

    def start1(k, c):
        path_copy(k, lax.rem(p + k, n_path)).start()
        return c

    def finish1(k, c):
        copy = path_copy(k, lax.rem(p + k, n_path))
        copy.wait_send()
        copy.wait_recv()
        return c

    lax.fori_loop(1, n_path, start1, 0)
    lax.fori_loop(1, n_path, finish1, 0)
    mid[...] = term_ref[p] + jnp.sum(recv1[...], axis=0)

    def grp_copy(k, h):
        return pltpu.make_async_remote_copy(
            src_ref=mid, dst_ref=recv2.at[k - 1], send_sem=send2.at[k - 1],
            recv_sem=got2.at[k - 1], device_id=(h, p), device_id_type=MESH)

    def start2(k, c):
        grp_copy(k, lax.rem(g + k, n_grp)).start()
        return c

    def finish2(k, c):
        copy = grp_copy(k, lax.rem(g + k, n_grp))
        copy.wait_send()
        copy.wait_recv()
        return c

    lax.fori_loop(1, n_grp, start2, 0)
    lax.fori_loop(1, n_grp, finish2, 0)
    out_ref[...] = mid[...] + jnp.sum(recv2[...], axis=0)


def readout_reduce(term, n_grp, n_path):
    _, rows, width = term.shape
    return pl.pallas_call(
        lambda *refs: _readout_kernel(n_grp, n_path, *refs),
        out_shape=jax.ShapeDtypeStruct((rows, width), jnp.float32),
        in_specs=[pl.BlockSpec(memory_space=pltpu.VMEM)],
        out_specs=pl.BlockSpec(memory_space=pltpu.VMEM),
        scratch_shapes=[
            pltpu.VMEM((n_path - 1, rows, width), jnp.float32),
            pltpu.VMEM((n_grp - 1, rows, width), jnp.float32),
            pltpu.VMEM((rows, width), jnp.float32),
            pltpu.SemaphoreType.DMA((n_path - 1,)),
            pltpu.SemaphoreType.DMA((n_path - 1,)),
            pltpu.SemaphoreType.DMA((n_grp - 1,)),
            pltpu.SemaphoreType.DMA((n_grp - 1,)),
        ],
        compiler_params=pltpu.CompilerParams(collective_id=0, has_side_effects=True),
    )(term)


def gated_update(projected, carried, w_hidden):
    width = carried.shape[1]
    recur = jnp.dot(carried.astype(jnp.bfloat16), w_hidden, preferred_element_type=jnp.float32)
    reset = jax.nn.sigmoid(projected[:, :width] + recur[:, :width])
    update = jax.nn.sigmoid(projected[:, width : 2 * width] + recur[:, width : 2 * width])
    candidate = jnp.tanh(projected[:, 2 * width :] + reset * recur[:, 2 * width :])
    return (1.0 - update) * candidate + update * carried


def shards(
    link_state, path_state, path_links, w_path_in, w_path_hid, w_link_in, w_link_hid, cotangent
):
    bf16, f32 = jnp.bfloat16, jnp.float32
    own_links = link_state[0]
    link_dev, width = own_links.shape
    peer_count = lax.axis_size("path")
    path_count, hop_count = path_links.shape
    entries = path_count * hop_count
    capacity = entries // peer_count
    slots = peer_count * capacity
    flat_ids = path_links.reshape(-1)
    is_live = flat_ids >= 0
    owner_id = jnp.where(is_live, flat_ids // link_dev, peer_count)
    local_id = jnp.where(is_live, flat_ids % link_dev, 0)
    marks = (owner_id[:, None] == jnp.arange(peer_count)[None, :]).astype(bf16)
    order = jnp.arange(entries)
    earlier = (order[None, :] < order[:, None]).astype(bf16)
    before = jnp.dot(earlier, marks, preferred_element_type=f32)
    slot_id = jnp.sum(before * marks.astype(f32), axis=1).astype(jnp.int32)
    dest = jnp.where(is_live, owner_id * capacity + slot_id, -1)
    slot_ids = jnp.arange(slots)
    route = dest[None, :] == slot_ids[:, None]
    requests = jnp.sum(jnp.where(route, local_id[None, :] + 1, 0), axis=1) - 1
    received = lax.all_to_all(
        requests.reshape(peer_count, capacity), "path", split_axis=0, concat_axis=0, tiled=True
    ).reshape(-1)
    want = (received[:, None] == jnp.arange(link_dev)[None, :]).astype(bf16)
    served = jnp.dot(want, own_links, preferred_element_type=f32).astype(bf16)
    got = lax.all_to_all(
        served.reshape(peer_count, capacity, width), "path", split_axis=0, concat_axis=0, tiled=True
    ).reshape(slots, width)
    route_t = (dest[:, None] == slot_ids[None, :]).astype(bf16)
    fetched = jnp.dot(route_t, got, preferred_element_type=f32).astype(bf16)
    projected = jnp.dot(fetched, w_path_in, preferred_element_type=f32)
    projected = projected.reshape(path_count, hop_count, 3 * width)
    live_grid = is_live.reshape(path_count, hop_count)
    carried = path_state[0].astype(f32)
    messages = []
    for hop_index in range(hop_count):
        renewed = gated_update(projected[:, hop_index], carried, w_path_hid)
        carried = jnp.where(live_grid[:, hop_index, None], renewed, carried)
        messages.append(carried.astype(bf16))
    path_final = carried.astype(bf16)
    flat_messages = jnp.stack(messages, axis=1).reshape(-1, width)
    outgoing = jnp.dot(route.astype(bf16), flat_messages, preferred_element_type=f32).astype(bf16)
    incoming = lax.all_to_all(
        outgoing.reshape(peer_count, capacity, width), "path", split_axis=0, concat_axis=0, tiled=True
    ).reshape(slots, width)
    link_sum = lax.dot_general(
        want, incoming, (((0,), (0,)), ((), ())), preferred_element_type=f32
    )
    link_proj = jnp.dot(link_sum.astype(bf16), w_link_in, preferred_element_type=f32)
    link_next = gated_update(link_proj, own_links.astype(f32), w_link_hid).astype(bf16)
    cot = cotangent[0].reshape(path_count, peer_count, -1)
    term = lax.dot_general(cot, path_final, (((0,), (0,)), ((), ())), preferred_element_type=f32)
    read_grad = readout_reduce(term, lax.axis_size("grp"), peer_count)
    return (link_next[None], path_final[None], read_grad)


def solution(mesh):
    return jax.shard_map(
        shards,
        mesh=mesh,
        in_specs=(
            P("grp", "path", None),
            P("grp", "path", None),
            P("path", None),
            P(),
            P(),
            P(),
            P(),
            P("grp", "path", None),
        ),
        out_specs=(P("grp", "path", None), P("grp", "path", None), P("path", None)),
        check_vma=False,
    )
```

```python
import jax
import jax.numpy as jnp
from jax import lax
from jax.experimental import pallas as pl
from jax.experimental.pallas import tpu as pltpu
from jax.sharding import PartitionSpec as P

MESH = pl.DeviceIdType.MESH


def gated_update(projected, carried, w_hidden):
    width = carried.shape[1]
    recur = jnp.dot(carried.astype(jnp.bfloat16), w_hidden, preferred_element_type=jnp.float32)
    reset = jax.nn.sigmoid(projected[:, :width] + recur[:, :width])
    update = jax.nn.sigmoid(projected[:, width : 2 * width] + recur[:, width : 2 * width])
    candidate = jnp.tanh(projected[:, 2 * width :] + reset * recur[:, 2 * width :])
    return (1.0 - update) * candidate + update * carried


def _greet(barrier, g, p, n_grp, n_path, with_grp):
    def greet_path(k, c):
        pl.semaphore_signal(barrier, inc=1, device_id=(g, lax.rem(p + k, n_path)), device_id_type=MESH)
        return c

    def greet_grp(k, c):
        pl.semaphore_signal(barrier, inc=1, device_id=(lax.rem(g + k, n_grp), p), device_id_type=MESH)
        return c

    lax.fori_loop(1, n_path, greet_path, 0)
    count = n_path - 1
    if with_grp:
        lax.fori_loop(1, n_grp, greet_grp, 0)
        count += n_grp - 1
    pl.semaphore_wait(barrier, count)


def _ring_copies(src, dst, send, recv, g, p, n_path, sign):
    def make(k):
        return pltpu.make_async_remote_copy(
            src_ref=src.at[k], dst_ref=dst.at[k], send_sem=send.at[k - 1], recv_sem=recv.at[k - 1],
            device_id=(g, lax.rem(p + sign * k + n_path, n_path)), device_id_type=MESH)

    def start(k, c):
        make(k).start()
        return c

    def finish(k, c):
        copy = make(k)
        copy.wait_send()
        copy.wait_recv()
        return c

    return start, finish


def _fetch_kernel(n_grp, n_path, req_ref, links_ref, got_ref, ids_ref,
                  reqin, served, gotbuf, rsend, rrecv, asend, arecv):
    g = lax.axis_index("grp")
    p = lax.axis_index("path")
    _greet(pltpu.get_barrier_semaphore(), g, p, n_grp, n_path, False)
    start_req, finish_req = _ring_copies(req_ref, reqin, rsend, rrecv, g, p, n_path, 1)
    lax.fori_loop(1, n_path, start_req, 0)
    reqin[0] = req_ref[0]
    lax.fori_loop(1, n_path, finish_req, 0)
    n_k, cap, lanes = reqin.shape
    link_dev = links_ref.shape[0]
    ids = reqin[...].reshape(n_k * cap, lanes)[:, 0:1]
    want = (ids == lax.broadcasted_iota(jnp.int32, (1, link_dev), 1)).astype(jnp.bfloat16)
    rows = jnp.dot(want, links_ref[...], preferred_element_type=jnp.float32).astype(jnp.bfloat16)
    served[...] = rows.reshape(n_k, cap, rows.shape[-1])
    start_ans, finish_ans = _ring_copies(served, gotbuf, asend, arecv, g, p, n_path, -1)
    lax.fori_loop(1, n_path, start_ans, 0)
    gotbuf[0] = served[0]
    ids_ref[...] = reqin[...]
    lax.fori_loop(1, n_path, finish_ans, 0)
    got_ref[...] = gotbuf[...]


def fetch_rows(req, own_links, n_grp, n_path):
    n_k, cap, lanes = req.shape
    width = own_links.shape[1]
    return pl.pallas_call(
        lambda *refs: _fetch_kernel(n_grp, n_path, *refs),
        out_shape=(jax.ShapeDtypeStruct((n_k, cap, width), jnp.bfloat16),
                   jax.ShapeDtypeStruct((n_k, cap, lanes), jnp.int32)),
        in_specs=[pl.BlockSpec(memory_space=pltpu.VMEM)] * 2,
        out_specs=(pl.BlockSpec(memory_space=pltpu.VMEM),) * 2,
        scratch_shapes=[
            pltpu.VMEM((n_k, cap, lanes), jnp.int32),
            pltpu.VMEM((n_k, cap, width), jnp.bfloat16),
            pltpu.VMEM((n_k, cap, width), jnp.bfloat16),
            pltpu.SemaphoreType.DMA((n_path - 1,)),
            pltpu.SemaphoreType.DMA((n_path - 1,)),
            pltpu.SemaphoreType.DMA((n_path - 1,)),
            pltpu.SemaphoreType.DMA((n_path - 1,)),
        ],
        compiler_params=pltpu.CompilerParams(collective_id=0, has_side_effects=True),
    )(req, own_links)


def _message_kernel(n_grp, n_path, out_ref, term_ref, inc_ref, grad_ref,
                    inbuf, recv1, recv2, mid, msend, mrecv, send1, got1, send2, got2):
    g = lax.axis_index("grp")
    p = lax.axis_index("path")
    _greet(pltpu.get_barrier_semaphore(), g, p, n_grp, n_path, True)
    start_msg, finish_msg = _ring_copies(out_ref, inbuf, msend, mrecv, g, p, n_path, 1)
    lax.fori_loop(1, n_path, start_msg, 0)

    def path_copy(k, q):
        return pltpu.make_async_remote_copy(
            src_ref=term_ref.at[q], dst_ref=recv1.at[k - 1], send_sem=send1.at[k - 1],
            recv_sem=got1.at[k - 1], device_id=(g, q), device_id_type=MESH)

    def start1(k, c):
        path_copy(k, lax.rem(p + k, n_path)).start()
        return c

    def finish1(k, c):
        copy = path_copy(k, lax.rem(p + k, n_path))
        copy.wait_send()
        copy.wait_recv()
        return c

    lax.fori_loop(1, n_path, start1, 0)
    inbuf[0] = out_ref[0]
    lax.fori_loop(1, n_path, finish1, 0)
    mid[...] = term_ref[p] + jnp.sum(recv1[...], axis=0)

    def grp_copy(k, h):
        return pltpu.make_async_remote_copy(
            src_ref=mid, dst_ref=recv2.at[k - 1], send_sem=send2.at[k - 1],
            recv_sem=got2.at[k - 1], device_id=(h, p), device_id_type=MESH)

    def start2(k, c):
        grp_copy(k, lax.rem(g + k, n_grp)).start()
        return c

    def finish2(k, c):
        copy = grp_copy(k, lax.rem(g + k, n_grp))
        copy.wait_send()
        copy.wait_recv()
        return c

    lax.fori_loop(1, n_grp, start2, 0)
    lax.fori_loop(1, n_path, finish_msg, 0)
    inc_ref[...] = inbuf[...]
    lax.fori_loop(1, n_grp, finish2, 0)
    grad_ref[...] = mid[...] + jnp.sum(recv2[...], axis=0)


def exchange_messages(outgoing, term, n_grp, n_path):
    n_k, cap, width = outgoing.shape
    _, rows, gwidth = term.shape
    return pl.pallas_call(
        lambda *refs: _message_kernel(n_grp, n_path, *refs),
        out_shape=(jax.ShapeDtypeStruct((n_k, cap, width), jnp.bfloat16),
                   jax.ShapeDtypeStruct((rows, gwidth), jnp.float32)),
        in_specs=[pl.BlockSpec(memory_space=pltpu.VMEM)] * 2,
        out_specs=(pl.BlockSpec(memory_space=pltpu.VMEM),) * 2,
        scratch_shapes=[
            pltpu.VMEM((n_k, cap, width), jnp.bfloat16),
            pltpu.VMEM((n_path - 1, rows, gwidth), jnp.float32),
            pltpu.VMEM((n_grp - 1, rows, gwidth), jnp.float32),
            pltpu.VMEM((rows, gwidth), jnp.float32),
            pltpu.SemaphoreType.DMA((n_path - 1,)),
            pltpu.SemaphoreType.DMA((n_path - 1,)),
            pltpu.SemaphoreType.DMA((n_path - 1,)),
            pltpu.SemaphoreType.DMA((n_path - 1,)),
            pltpu.SemaphoreType.DMA((n_grp - 1,)),
            pltpu.SemaphoreType.DMA((n_grp - 1,)),
        ],
        compiler_params=pltpu.CompilerParams(collective_id=1, has_side_effects=True),
    )(outgoing, term)


def shards(
    link_state, path_state, path_links, w_path_in, w_path_hid, w_link_in, w_link_hid, cotangent
):
    bf16, f32 = jnp.bfloat16, jnp.float32
    own_links = link_state[0]
    link_dev, width = own_links.shape
    n_grp = lax.axis_size("grp")
    peer_count = lax.axis_size("path")
    me = lax.axis_index("path")
    path_count, hop_count = path_links.shape
    entries = path_count * hop_count
    capacity = entries // peer_count
    slots = peer_count * capacity
    flat_ids = path_links.reshape(-1)
    is_live = flat_ids >= 0
    owner_id = jnp.where(is_live, flat_ids // link_dev, peer_count)
    local_id = jnp.where(is_live, flat_ids % link_dev, 0)
    marks = (owner_id[:, None] == jnp.arange(peer_count)[None, :]).astype(bf16)
    order = jnp.arange(entries)
    earlier = (order[None, :] < order[:, None]).astype(bf16)
    before = jnp.dot(earlier, marks, preferred_element_type=f32)
    slot_id = jnp.sum(before * marks.astype(f32), axis=1).astype(jnp.int32)
    offset = lax.rem(owner_id - me + peer_count, peer_count)
    dest = jnp.where(is_live, offset * capacity + slot_id, -1)
    slot_ids = jnp.arange(slots)
    route = dest[None, :] == slot_ids[:, None]
    requests = jnp.sum(jnp.where(route, local_id[None, :] + 1, 0), axis=1) - 1
    req = jnp.broadcast_to(requests.reshape(peer_count, capacity, 1), (peer_count, capacity, 128))
    got, req_ids = fetch_rows(req, own_links, n_grp, peer_count)
    route_t = (dest[:, None] == slot_ids[None, :]).astype(bf16)
    fetched = jnp.dot(route_t, got.reshape(slots, width), preferred_element_type=f32).astype(bf16)
    projected = jnp.dot(fetched, w_path_in, preferred_element_type=f32)
    projected = projected.reshape(path_count, hop_count, 3 * width)
    live_grid = is_live.reshape(path_count, hop_count)
    carried = path_state[0].astype(f32)
    messages = []
    for hop_index in range(hop_count):
        renewed = gated_update(projected[:, hop_index], carried, w_path_hid)
        carried = jnp.where(live_grid[:, hop_index, None], renewed, carried)
        messages.append(carried.astype(bf16))
    path_final = carried.astype(bf16)
    flat_messages = jnp.stack(messages, axis=1).reshape(-1, width)
    outgoing = jnp.dot(route.astype(bf16), flat_messages, preferred_element_type=f32).astype(bf16)
    cot = cotangent[0].reshape(path_count, peer_count, -1)
    term = lax.dot_general(cot, path_final, (((0,), (0,)), ((), ())), preferred_element_type=f32)
    incoming, read_grad = exchange_messages(
        outgoing.reshape(peer_count, capacity, width), term, n_grp, peer_count)
    received = req_ids[:, :, 0].reshape(-1)
    want = (received[:, None] == jnp.arange(link_dev)[None, :]).astype(bf16)
    link_sum = lax.dot_general(
        want, incoming.reshape(slots, width), (((0,), (0,)), ((), ())), preferred_element_type=f32
    )
    link_proj = jnp.dot(link_sum.astype(bf16), w_link_in, preferred_element_type=f32)
    link_next = gated_update(link_proj, own_links.astype(f32), w_link_hid).astype(bf16)
    return (link_next[None], path_final[None], read_grad)


def solution(mesh):
    return jax.shard_map(
        shards,
        mesh=mesh,
        in_specs=(
            P("grp", "path", None),
            P("grp", "path", None),
            P("path", None),
            P(),
            P(),
            P(),
            P(),
            P("grp", "path", None),
        ),
        out_specs=(P("grp", "path", None), P("grp", "path", None), P("path", None)),
        check_vma=False,
    )
```

```python
import jax
import jax.numpy as jnp
from jax import lax
from jax.experimental import pallas as pl
from jax.experimental.pallas import tpu as pltpu
from jax.sharding import PartitionSpec as P

MESH = pl.DeviceIdType.MESH


def gated_update(projected, carried, w_hidden):
    width = carried.shape[1]
    recur = jnp.dot(carried.astype(jnp.bfloat16), w_hidden, preferred_element_type=jnp.float32)
    reset = jax.nn.sigmoid(projected[:, :width] + recur[:, :width])
    update = jax.nn.sigmoid(projected[:, width : 2 * width] + recur[:, width : 2 * width])
    candidate = jnp.tanh(projected[:, 2 * width :] + reset * recur[:, 2 * width :])
    return (1.0 - update) * candidate + update * carried


def _greet(barrier, g, p, n_grp, n_path, with_grp):
    def greet_path(k, c):
        pl.semaphore_signal(barrier, inc=1, device_id=(g, lax.rem(p + k, n_path)), device_id_type=MESH)
        return c

    def greet_grp(k, c):
        pl.semaphore_signal(barrier, inc=1, device_id=(lax.rem(g + k, n_grp), p), device_id_type=MESH)
        return c

    lax.fori_loop(1, n_path, greet_path, 0)
    count = n_path - 1
    if with_grp:
        lax.fori_loop(1, n_grp, greet_grp, 0)
        count += n_grp - 1
    pl.semaphore_wait(barrier, count)


def _ring_copies(src, dst, send, recv, g, p, n_path, sign):
    def make(k):
        return pltpu.make_async_remote_copy(
            src_ref=src.at[k], dst_ref=dst.at[k], send_sem=send.at[k - 1], recv_sem=recv.at[k - 1],
            device_id=(g, lax.rem(p + sign * k + n_path, n_path)), device_id_type=MESH)

    def start(k, c):
        make(k).start()
        return c

    def finish(k, c):
        copy = make(k)
        copy.wait_send()
        copy.wait_recv()
        return c

    return start, finish


def _fetch_kernel(n_grp, n_path, req_ref, links_ref, got_ref, ids_ref,
                  reqin, want, served, gotbuf, rsend, rrecv, asend, arecv):
    g = lax.axis_index("grp")
    p = lax.axis_index("path")
    _greet(pltpu.get_barrier_semaphore(), g, p, n_grp, n_path, False)
    start_req, finish_req = _ring_copies(req_ref, reqin, rsend, rrecv, g, p, n_path, 1)
    lax.fori_loop(1, n_path, start_req, 0)
    reqin[0] = req_ref[0]
    lax.fori_loop(1, n_path, finish_req, 0)
    n_k, cap = served.shape[0], served.shape[1]
    link_dev = links_ref.shape[0]
    ids_t = jnp.transpose(reqin[:, 0, :])
    lanes = lax.broadcasted_iota(jnp.int32, (1, link_dev), 1)
    for k in range(n_k):
        want[k * cap : (k + 1) * cap, :] = (ids_t[0:cap, k : k + 1] == lanes).astype(jnp.bfloat16)
    rows = jnp.dot(want[...], links_ref[...], preferred_element_type=jnp.float32).astype(jnp.bfloat16)
    served[...] = rows.reshape(served.shape)
    start_ans, finish_ans = _ring_copies(served, gotbuf, asend, arecv, g, p, n_path, -1)
    lax.fori_loop(1, n_path, start_ans, 0)
    gotbuf[0] = served[0]
    ids_ref[...] = reqin[...]
    lax.fori_loop(1, n_path, finish_ans, 0)
    got_ref[...] = gotbuf[...]


def fetch_rows(req, own_links, cap, n_grp, n_path):
    n_k, rows, lanes = req.shape
    width = own_links.shape[1]
    return pl.pallas_call(
        lambda *refs: _fetch_kernel(n_grp, n_path, *refs),
        out_shape=(jax.ShapeDtypeStruct((n_k, cap, width), jnp.bfloat16),
                   jax.ShapeDtypeStruct((n_k, rows, lanes), jnp.int32)),
        in_specs=[pl.BlockSpec(memory_space=pltpu.VMEM)] * 2,
        out_specs=(pl.BlockSpec(memory_space=pltpu.VMEM),) * 2,
        scratch_shapes=[
            pltpu.VMEM((n_k, rows, lanes), jnp.int32),
            pltpu.VMEM((n_k * cap, own_links.shape[0]), jnp.bfloat16),
            pltpu.VMEM((n_k, cap, width), jnp.bfloat16),
            pltpu.VMEM((n_k, cap, width), jnp.bfloat16),
            pltpu.SemaphoreType.DMA((n_path - 1,)),
            pltpu.SemaphoreType.DMA((n_path - 1,)),
            pltpu.SemaphoreType.DMA((n_path - 1,)),
            pltpu.SemaphoreType.DMA((n_path - 1,)),
        ],
        compiler_params=pltpu.CompilerParams(collective_id=0, has_side_effects=True),
    )(req, own_links)


def _message_kernel(n_grp, n_path, out_ref, term_ref, inc_ref, grad_ref,
                    inbuf, recv1, recv2, mid, msend, mrecv, send1, got1, send2, got2):
    g = lax.axis_index("grp")
    p = lax.axis_index("path")
    _greet(pltpu.get_barrier_semaphore(), g, p, n_grp, n_path, True)
    start_msg, finish_msg = _ring_copies(out_ref, inbuf, msend, mrecv, g, p, n_path, 1)
    lax.fori_loop(1, n_path, start_msg, 0)

    def path_copy(k, q):
        return pltpu.make_async_remote_copy(
            src_ref=term_ref.at[q], dst_ref=recv1.at[k - 1], send_sem=send1.at[k - 1],
            recv_sem=got1.at[k - 1], device_id=(g, q), device_id_type=MESH)

    def start1(k, c):
        path_copy(k, lax.rem(p + k, n_path)).start()
        return c

    def finish1(k, c):
        copy = path_copy(k, lax.rem(p + k, n_path))
        copy.wait_send()
        copy.wait_recv()
        return c

    lax.fori_loop(1, n_path, start1, 0)
    inbuf[0] = out_ref[0]
    lax.fori_loop(1, n_path, finish1, 0)
    mid[...] = term_ref[p] + jnp.sum(recv1[...], axis=0)

    def grp_copy(k, h):
        return pltpu.make_async_remote_copy(
            src_ref=mid, dst_ref=recv2.at[k - 1], send_sem=send2.at[k - 1],
            recv_sem=got2.at[k - 1], device_id=(h, p), device_id_type=MESH)

    def start2(k, c):
        grp_copy(k, lax.rem(g + k, n_grp)).start()
        return c

    def finish2(k, c):
        copy = grp_copy(k, lax.rem(g + k, n_grp))
        copy.wait_send()
        copy.wait_recv()
        return c

    lax.fori_loop(1, n_grp, start2, 0)
    lax.fori_loop(1, n_path, finish_msg, 0)
    inc_ref[...] = inbuf[...]
    lax.fori_loop(1, n_grp, finish2, 0)
    grad_ref[...] = mid[...] + jnp.sum(recv2[...], axis=0)


def exchange_messages(outgoing, term, n_grp, n_path):
    n_k, cap, width = outgoing.shape
    _, rows, gwidth = term.shape
    return pl.pallas_call(
        lambda *refs: _message_kernel(n_grp, n_path, *refs),
        out_shape=(jax.ShapeDtypeStruct((n_k, cap, width), jnp.bfloat16),
                   jax.ShapeDtypeStruct((rows, gwidth), jnp.float32)),
        in_specs=[pl.BlockSpec(memory_space=pltpu.VMEM)] * 2,
        out_specs=(pl.BlockSpec(memory_space=pltpu.VMEM),) * 2,
        scratch_shapes=[
            pltpu.VMEM((n_k, cap, width), jnp.bfloat16),
            pltpu.VMEM((n_path - 1, rows, gwidth), jnp.float32),
            pltpu.VMEM((n_grp - 1, rows, gwidth), jnp.float32),
            pltpu.VMEM((rows, gwidth), jnp.float32),
            pltpu.SemaphoreType.DMA((n_path - 1,)),
            pltpu.SemaphoreType.DMA((n_path - 1,)),
            pltpu.SemaphoreType.DMA((n_path - 1,)),
            pltpu.SemaphoreType.DMA((n_path - 1,)),
            pltpu.SemaphoreType.DMA((n_grp - 1,)),
            pltpu.SemaphoreType.DMA((n_grp - 1,)),
        ],
        compiler_params=pltpu.CompilerParams(collective_id=1, has_side_effects=True),
    )(outgoing, term)


def shards(
    link_state, path_state, path_links, w_path_in, w_path_hid, w_link_in, w_link_hid, cotangent
):
    bf16, f32 = jnp.bfloat16, jnp.float32
    own_links = link_state[0]
    link_dev, width = own_links.shape
    n_grp = lax.axis_size("grp")
    peer_count = lax.axis_size("path")
    me = lax.axis_index("path")
    path_count, hop_count = path_links.shape
    entries = path_count * hop_count
    capacity = entries // peer_count
    slots = peer_count * capacity
    flat_ids = path_links.reshape(-1)
    is_live = flat_ids >= 0
    owner_id = jnp.where(is_live, flat_ids // link_dev, peer_count)
    local_id = jnp.where(is_live, flat_ids % link_dev, 0)
    marks = (owner_id[:, None] == jnp.arange(peer_count)[None, :]).astype(bf16)
    order = jnp.arange(entries)
    earlier = (order[None, :] < order[:, None]).astype(bf16)
    before = jnp.dot(earlier, marks, preferred_element_type=f32)
    slot_id = jnp.sum(before * marks.astype(f32), axis=1).astype(jnp.int32)
    offset = lax.rem(owner_id - me + peer_count, peer_count)
    dest = jnp.where(is_live, offset * capacity + slot_id, -1)
    slot_ids = jnp.arange(slots)
    route = dest[None, :] == slot_ids[:, None]
    requests = jnp.sum(jnp.where(route, local_id[None, :] + 1, 0), axis=1) - 1
    req = jnp.full((peer_count, 8, 128), -1, jnp.int32)
    req = lax.dynamic_update_slice(req, requests.reshape(peer_count, 1, capacity), (0, 0, 0))
    got, req_ids = fetch_rows(req, own_links, capacity, n_grp, peer_count)
    route_t = (dest[:, None] == slot_ids[None, :]).astype(bf16)
    fetched = jnp.dot(route_t, got.reshape(slots, width), preferred_element_type=f32).astype(bf16)
    projected = jnp.dot(fetched, w_path_in, preferred_element_type=f32)
    projected = projected.reshape(path_count, hop_count, 3 * width)
    live_grid = is_live.reshape(path_count, hop_count)
    carried = path_state[0].astype(f32)
    messages = []
    for hop_index in range(hop_count):
        renewed = gated_update(projected[:, hop_index], carried, w_path_hid)
        carried = jnp.where(live_grid[:, hop_index, None], renewed, carried)
        messages.append(carried.astype(bf16))
    path_final = carried.astype(bf16)
    flat_messages = jnp.stack(messages, axis=1).reshape(-1, width)
    outgoing = jnp.dot(route.astype(bf16), flat_messages, preferred_element_type=f32).astype(bf16)
    cot = cotangent[0].reshape(path_count, peer_count, -1)
    term = lax.dot_general(cot, path_final, (((0,), (0,)), ((), ())), preferred_element_type=f32)
    incoming, read_grad = exchange_messages(
        outgoing.reshape(peer_count, capacity, width), term, n_grp, peer_count)
    received = req_ids[:, 0, :capacity].reshape(-1)
    want = (received[:, None] == jnp.arange(link_dev)[None, :]).astype(bf16)
    link_sum = lax.dot_general(
        want, incoming.reshape(slots, width), (((0,), (0,)), ((), ())), preferred_element_type=f32
    )
    link_proj = jnp.dot(link_sum.astype(bf16), w_link_in, preferred_element_type=f32)
    link_next = gated_update(link_proj, own_links.astype(f32), w_link_hid).astype(bf16)
    return (link_next[None], path_final[None], read_grad)


def solution(mesh):
    return jax.shard_map(
        shards,
        mesh=mesh,
        in_specs=(
            P("grp", "path", None),
            P("grp", "path", None),
            P("path", None),
            P(),
            P(),
            P(),
            P(),
            P("grp", "path", None),
        ),
        out_specs=(P("grp", "path", None), P("grp", "path", None), P("path", None)),
        check_vma=False,
    )
```

```python
import jax
import jax.numpy as jnp
from jax import lax
from jax.experimental import pallas as pl
from jax.experimental.pallas import tpu as pltpu
from jax.sharding import PartitionSpec as P

MESH = pl.DeviceIdType.MESH


def gated_update(projected, carried, w_hidden):
    width = carried.shape[1]
    recur = jnp.dot(carried.astype(jnp.bfloat16), w_hidden, preferred_element_type=jnp.float32)
    reset = jax.nn.sigmoid(projected[:, :width] + recur[:, :width])
    update = jax.nn.sigmoid(projected[:, width : 2 * width] + recur[:, width : 2 * width])
    candidate = jnp.tanh(projected[:, 2 * width :] + reset * recur[:, 2 * width :])
    return (1.0 - update) * candidate + update * carried


def _greet(barrier, g, p, n_grp, n_path, with_grp):
    def greet_path(k, c):
        pl.semaphore_signal(barrier, inc=1, device_id=(g, lax.rem(p + k, n_path)), device_id_type=MESH)
        return c

    def greet_grp(k, c):
        pl.semaphore_signal(barrier, inc=1, device_id=(lax.rem(g + k, n_grp), p), device_id_type=MESH)
        return c

    lax.fori_loop(1, n_path, greet_path, 0)
    count = n_path - 1
    if with_grp:
        lax.fori_loop(1, n_grp, greet_grp, 0)
        count += n_grp - 1
    pl.semaphore_wait(barrier, count)


def _ring_copies(src, dst, send, recv, g, p, n_path, sign):
    def make(k):
        return pltpu.make_async_remote_copy(
            src_ref=src.at[k], dst_ref=dst.at[k], send_sem=send.at[k - 1], recv_sem=recv.at[k - 1],
            device_id=(g, lax.rem(p + sign * k + n_path, n_path)), device_id_type=MESH)

    def start(k, c):
        make(k).start()
        return c

    def finish(k, c):
        copy = make(k)
        copy.wait_send()
        copy.wait_recv()
        return c

    return start, finish


def _fetch_kernel(n_grp, n_path, req_ref, links_ref, got_ref, ids_ref,
                  reqin, want, served, gotbuf, rsend, rrecv, asend, arecv):
    g = lax.axis_index("grp")
    p = lax.axis_index("path")
    _greet(pltpu.get_barrier_semaphore(), g, p, n_grp, n_path, False)
    start_req, finish_req = _ring_copies(req_ref, reqin, rsend, rrecv, g, p, n_path, 1)
    lax.fori_loop(1, n_path, start_req, 0)
    reqin[0] = req_ref[0]
    lax.fori_loop(1, n_path, finish_req, 0)
    n_k, cap = served.shape[0], served.shape[1]
    link_dev = links_ref.shape[0]
    ids_t = jnp.transpose(reqin[:, 0, :])
    lanes = lax.broadcasted_iota(jnp.int32, (1, link_dev), 1)
    for k in range(n_k):
        want[k * cap : (k + 1) * cap, :] = (ids_t[0:cap, k : k + 1] == lanes).astype(jnp.bfloat16)
    rows = jnp.dot(want[...], links_ref[...], preferred_element_type=jnp.float32).astype(jnp.bfloat16)
    served[...] = rows.reshape(served.shape)
    start_ans, finish_ans = _ring_copies(served, gotbuf, asend, arecv, g, p, n_path, -1)
    lax.fori_loop(1, n_path, start_ans, 0)
    gotbuf[0] = served[0]
    ids_ref[...] = reqin[...]
    lax.fori_loop(1, n_path, finish_ans, 0)
    got_ref[...] = gotbuf[...]


def fetch_rows(req, own_links, cap, n_grp, n_path):
    n_k, rows, lanes = req.shape
    width = own_links.shape[1]
    return pl.pallas_call(
        lambda *refs: _fetch_kernel(n_grp, n_path, *refs),
        out_shape=(jax.ShapeDtypeStruct((n_k, cap, width), jnp.bfloat16),
                   jax.ShapeDtypeStruct((n_k, rows, lanes), jnp.int32)),
        in_specs=[pl.BlockSpec(memory_space=pltpu.VMEM)] * 2,
        out_specs=(pl.BlockSpec(memory_space=pltpu.VMEM),) * 2,
        scratch_shapes=[
            pltpu.VMEM((n_k, rows, lanes), jnp.int32),
            pltpu.VMEM((n_k * cap, own_links.shape[0]), jnp.bfloat16),
            pltpu.VMEM((n_k, cap, width), jnp.bfloat16),
            pltpu.VMEM((n_k, cap, width), jnp.bfloat16),
            pltpu.SemaphoreType.DMA((n_path - 1,)),
            pltpu.SemaphoreType.DMA((n_path - 1,)),
            pltpu.SemaphoreType.DMA((n_path - 1,)),
            pltpu.SemaphoreType.DMA((n_path - 1,)),
        ],
        compiler_params=pltpu.CompilerParams(collective_id=0, has_side_effects=True),
    )(req, own_links)


def _message_kernel(n_grp, n_path, out_ref, term_ref, sel_ref, w_in_ref, recur_ref, links_ref,
                    next_ref, grad_ref, inbuf, recv1, recv2, mid, msend, mrecv, send1, got1, send2, got2):
    g = lax.axis_index("grp")
    p = lax.axis_index("path")
    _greet(pltpu.get_barrier_semaphore(), g, p, n_grp, n_path, True)
    start_msg, finish_msg = _ring_copies(out_ref, inbuf, msend, mrecv, g, p, n_path, 1)
    lax.fori_loop(1, n_path, start_msg, 0)

    def path_copy(k, q):
        return pltpu.make_async_remote_copy(
            src_ref=term_ref.at[q], dst_ref=recv1.at[k - 1], send_sem=send1.at[k - 1],
            recv_sem=got1.at[k - 1], device_id=(g, q), device_id_type=MESH)

    def start1(k, c):
        path_copy(k, lax.rem(p + k, n_path)).start()
        return c

    def finish1(k, c):
        copy = path_copy(k, lax.rem(p + k, n_path))
        copy.wait_send()
        copy.wait_recv()
        return c

    lax.fori_loop(1, n_path, start1, 0)
    inbuf[0] = out_ref[0]
    lax.fori_loop(1, n_path, finish1, 0)
    mid[...] = term_ref[p] + jnp.sum(recv1[...], axis=0)

    def grp_copy(k, h):
        return pltpu.make_async_remote_copy(
            src_ref=mid, dst_ref=recv2.at[k - 1], send_sem=send2.at[k - 1],
            recv_sem=got2.at[k - 1], device_id=(h, p), device_id_type=MESH)

    def start2(k, c):
        grp_copy(k, lax.rem(g + k, n_grp)).start()
        return c

    def finish2(k, c):
        copy = grp_copy(k, lax.rem(g + k, n_grp))
        copy.wait_send()
        copy.wait_recv()
        return c

    lax.fori_loop(1, n_grp, start2, 0)
    lax.fori_loop(1, n_path, finish_msg, 0)
    n_k, cap, width = inbuf.shape
    incoming = inbuf[...].reshape(n_k * cap, width)
    link_sum = jnp.dot(sel_ref[...], incoming, preferred_element_type=jnp.float32)
    link_proj = jnp.dot(link_sum.astype(jnp.bfloat16), w_in_ref[...], preferred_element_type=jnp.float32)
    recur = recur_ref[...]
    own = links_ref[...].astype(jnp.float32)
    reset = jax.nn.sigmoid(link_proj[:, :width] + recur[:, :width])
    update = jax.nn.sigmoid(link_proj[:, width : 2 * width] + recur[:, width : 2 * width])
    candidate = jnp.tanh(link_proj[:, 2 * width :] + reset * recur[:, 2 * width :])
    next_ref[...] = ((1.0 - update) * candidate + update * own).astype(next_ref.dtype)
    lax.fori_loop(1, n_grp, finish2, 0)
    grad_ref[...] = mid[...] + jnp.sum(recv2[...], axis=0)


def exchange_messages(outgoing, term, sel, w_link_in, recur, own_links, n_grp, n_path):
    n_k, cap, width = outgoing.shape
    _, rows, gwidth = term.shape
    return pl.pallas_call(
        lambda *refs: _message_kernel(n_grp, n_path, *refs),
        out_shape=(jax.ShapeDtypeStruct(own_links.shape, jnp.bfloat16),
                   jax.ShapeDtypeStruct((rows, gwidth), jnp.float32)),
        in_specs=[pl.BlockSpec(memory_space=pltpu.VMEM)] * 6,
        out_specs=(pl.BlockSpec(memory_space=pltpu.VMEM),) * 2,
        scratch_shapes=[
            pltpu.VMEM((n_k, cap, width), jnp.bfloat16),
            pltpu.VMEM((n_path - 1, rows, gwidth), jnp.float32),
            pltpu.VMEM((n_grp - 1, rows, gwidth), jnp.float32),
            pltpu.VMEM((rows, gwidth), jnp.float32),
            pltpu.SemaphoreType.DMA((n_path - 1,)),
            pltpu.SemaphoreType.DMA((n_path - 1,)),
            pltpu.SemaphoreType.DMA((n_path - 1,)),
            pltpu.SemaphoreType.DMA((n_path - 1,)),
            pltpu.SemaphoreType.DMA((n_grp - 1,)),
            pltpu.SemaphoreType.DMA((n_grp - 1,)),
        ],
        compiler_params=pltpu.CompilerParams(collective_id=1, has_side_effects=True),
    )(outgoing, term, sel, w_link_in, recur, own_links)


def shards(
    link_state, path_state, path_links, w_path_in, w_path_hid, w_link_in, w_link_hid, cotangent
):
    bf16, f32 = jnp.bfloat16, jnp.float32
    own_links = link_state[0]
    link_dev, width = own_links.shape
    n_grp = lax.axis_size("grp")
    peer_count = lax.axis_size("path")
    me = lax.axis_index("path")
    path_count, hop_count = path_links.shape
    entries = path_count * hop_count
    capacity = entries // peer_count
    slots = peer_count * capacity
    flat_ids = path_links.reshape(-1)
    is_live = flat_ids >= 0
    owner_id = jnp.where(is_live, flat_ids // link_dev, peer_count)
    local_id = jnp.where(is_live, flat_ids % link_dev, 0)
    marks = (owner_id[:, None] == jnp.arange(peer_count)[None, :]).astype(bf16)
    order = jnp.arange(entries)
    earlier = (order[None, :] < order[:, None]).astype(bf16)
    before = jnp.dot(earlier, marks, preferred_element_type=f32)
    slot_id = jnp.sum(before * marks.astype(f32), axis=1).astype(jnp.int32)
    offset = lax.rem(owner_id - me + peer_count, peer_count)
    dest = jnp.where(is_live, offset * capacity + slot_id, -1)
    slot_ids = jnp.arange(slots)
    route = dest[None, :] == slot_ids[:, None]
    requests = jnp.sum(jnp.where(route, local_id[None, :] + 1, 0), axis=1) - 1
    req = jnp.full((peer_count, 8, 128), -1, jnp.int32)
    req = lax.dynamic_update_slice(req, requests.reshape(peer_count, 1, capacity), (0, 0, 0))
    link_recur = jnp.dot(own_links, w_link_hid, preferred_element_type=f32)
    got, req_ids = fetch_rows(req, own_links, capacity, n_grp, peer_count)
    route_t = (dest[:, None] == slot_ids[None, :]).astype(bf16)
    fetched = jnp.dot(route_t, got.reshape(slots, width), preferred_element_type=f32).astype(bf16)
    projected = jnp.dot(fetched, w_path_in, preferred_element_type=f32)
    projected = projected.reshape(path_count, hop_count, 3 * width)
    live_grid = is_live.reshape(path_count, hop_count)
    carried = path_state[0].astype(f32)
    messages = []
    for hop_index in range(hop_count):
        renewed = gated_update(projected[:, hop_index], carried, w_path_hid)
        carried = jnp.where(live_grid[:, hop_index, None], renewed, carried)
        messages.append(carried.astype(bf16))
    path_final = carried.astype(bf16)
    flat_messages = jnp.stack(messages, axis=1).reshape(-1, width)
    outgoing = jnp.dot(route.astype(bf16), flat_messages, preferred_element_type=f32).astype(bf16)
    cot = cotangent[0].reshape(path_count, peer_count, -1)
    term = lax.dot_general(cot, path_final, (((0,), (0,)), ((), ())), preferred_element_type=f32)
    received = req_ids[:, 0, :capacity].reshape(-1)
    sel = (jnp.arange(link_dev)[:, None] == received[None, :]).astype(bf16)
    link_next, read_grad = exchange_messages(
        outgoing.reshape(peer_count, capacity, width), term, sel, w_link_in, link_recur, own_links,
        n_grp, peer_count)
    return (link_next[None], path_final[None], read_grad)


def solution(mesh):
    return jax.shard_map(
        shards,
        mesh=mesh,
        in_specs=(
            P("grp", "path", None),
            P("grp", "path", None),
            P("path", None),
            P(),
            P(),
            P(),
            P(),
            P("grp", "path", None),
        ),
        out_specs=(P("grp", "path", None), P("grp", "path", None), P("path", None)),
        check_vma=False,
    )
```

```python
import jax
import jax.numpy as jnp
from jax import lax
from jax.experimental import pallas as pl
from jax.experimental.pallas import tpu as pltpu
from jax.sharding import PartitionSpec as P

MESH = pl.DeviceIdType.MESH


def gated_update(projected, carried, w_hidden):
    width = carried.shape[1]
    recur = jnp.dot(carried.astype(jnp.bfloat16), w_hidden, preferred_element_type=jnp.float32)
    reset = jax.nn.sigmoid(projected[:, :width] + recur[:, :width])
    update = jax.nn.sigmoid(projected[:, width : 2 * width] + recur[:, width : 2 * width])
    candidate = jnp.tanh(projected[:, 2 * width :] + reset * recur[:, 2 * width :])
    return (1.0 - update) * candidate + update * carried


def _greet(barrier, g, p, n_grp, n_path, with_grp):
    def greet_path(k, c):
        pl.semaphore_signal(barrier, inc=1, device_id=(g, lax.rem(p + k, n_path)), device_id_type=MESH)
        return c

    def greet_grp(k, c):
        pl.semaphore_signal(barrier, inc=1, device_id=(lax.rem(g + k, n_grp), p), device_id_type=MESH)
        return c

    lax.fori_loop(1, n_path, greet_path, 0)
    count = n_path - 1
    if with_grp:
        lax.fori_loop(1, n_grp, greet_grp, 0)
        count += n_grp - 1
    pl.semaphore_wait(barrier, count)


def _ring_copies(src, dst, send, recv, g, p, n_path, sign):
    def make(k):
        return pltpu.make_async_remote_copy(
            src_ref=src.at[k], dst_ref=dst.at[k], send_sem=send.at[k - 1], recv_sem=recv.at[k - 1],
            device_id=(g, lax.rem(p + sign * k + n_path, n_path)), device_id_type=MESH)

    def start(k, c):
        make(k).start()
        return c

    def finish(k, c):
        copy = make(k)
        copy.wait_send()
        copy.wait_recv()
        return c

    return start, finish


def _fetch_kernel(n_grp, n_path, req_ref, links_ref, got_ref, ids_ref,
                  reqin, want, served, gotbuf, rsend, rrecv, asend, arecv):
    g = lax.axis_index("grp")
    p = lax.axis_index("path")
    _greet(pltpu.get_barrier_semaphore(), g, p, n_grp, n_path, False)
    start_req, finish_req = _ring_copies(req_ref, reqin, rsend, rrecv, g, p, n_path, 1)
    lax.fori_loop(1, n_path, start_req, 0)
    reqin[0] = req_ref[0]
    lax.fori_loop(1, n_path, finish_req, 0)
    n_k, cap = served.shape[0], served.shape[1]
    link_dev = links_ref.shape[0]
    ids_t = jnp.transpose(reqin[:, 0, :])
    lanes = lax.broadcasted_iota(jnp.int32, (1, link_dev), 1)
    for k in range(n_k):
        want[k * cap : (k + 1) * cap, :] = (ids_t[0:cap, k : k + 1] == lanes).astype(jnp.bfloat16)
    rows = jnp.dot(want[...], links_ref[...], preferred_element_type=jnp.float32).astype(jnp.bfloat16)
    served[...] = rows.reshape(served.shape)
    start_ans, finish_ans = _ring_copies(served, gotbuf, asend, arecv, g, p, n_path, -1)
    lax.fori_loop(1, n_path, start_ans, 0)
    gotbuf[0] = served[0]
    ids_ref[...] = reqin[...]
    lax.fori_loop(1, n_path, finish_ans, 0)
    got_ref[...] = gotbuf[...]


def fetch_rows(req, own_links, cap, n_grp, n_path):
    n_k, rows, lanes = req.shape
    width = own_links.shape[1]
    return pl.pallas_call(
        lambda *refs: _fetch_kernel(n_grp, n_path, *refs),
        out_shape=(jax.ShapeDtypeStruct((n_k, cap, width), jnp.bfloat16),
                   jax.ShapeDtypeStruct((n_k, rows, lanes), jnp.int32)),
        in_specs=[pl.BlockSpec(memory_space=pltpu.VMEM)] * 2,
        out_specs=(pl.BlockSpec(memory_space=pltpu.VMEM),) * 2,
        scratch_shapes=[
            pltpu.VMEM((n_k, rows, lanes), jnp.int32),
            pltpu.VMEM((n_k * cap, own_links.shape[0]), jnp.bfloat16),
            pltpu.VMEM((n_k, cap, width), jnp.bfloat16),
            pltpu.VMEM((n_k, cap, width), jnp.bfloat16),
            pltpu.SemaphoreType.DMA((n_path - 1,)),
            pltpu.SemaphoreType.DMA((n_path - 1,)),
            pltpu.SemaphoreType.DMA((n_path - 1,)),
            pltpu.SemaphoreType.DMA((n_path - 1,)),
        ],
        compiler_params=pltpu.CompilerParams(collective_id=0, has_side_effects=True),
    )(req, own_links)


def _message_kernel(n_grp, n_path, out_ref, term_ref, inc_ref, grad_ref,
                    inbuf, recv1, recv2, mid, msend, mrecv, send1, got1, send2, got2):
    g = lax.axis_index("grp")
    p = lax.axis_index("path")
    _greet(pltpu.get_barrier_semaphore(), g, p, n_grp, n_path, True)
    start_msg, finish_msg = _ring_copies(out_ref, inbuf, msend, mrecv, g, p, n_path, 1)

    def path_copy(k, q):
        return pltpu.make_async_remote_copy(
            src_ref=term_ref.at[q], dst_ref=recv1.at[k - 1], send_sem=send1.at[k - 1],
            recv_sem=got1.at[k - 1], device_id=(g, q), device_id_type=MESH)

    def start1(k, c):
        path_copy(k, lax.rem(p + k, n_path)).start()
        return c

    def finish1(k, c):
        copy = path_copy(k, lax.rem(p + k, n_path))
        copy.wait_send()
        copy.wait_recv()
        return c

    lax.fori_loop(1, n_path, start1, 0)
    lax.fori_loop(1, n_path, start_msg, 0)
    inbuf[0] = out_ref[0]
    lax.fori_loop(1, n_path, finish1, 0)
    mid[...] = term_ref[p] + jnp.sum(recv1[...], axis=0)

    def grp_copy(k, h):
        return pltpu.make_async_remote_copy(
            src_ref=mid, dst_ref=recv2.at[k - 1], send_sem=send2.at[k - 1],
            recv_sem=got2.at[k - 1], device_id=(h, p), device_id_type=MESH)

    def start2(k, c):
        grp_copy(k, lax.rem(g + k, n_grp)).start()
        return c

    def finish2(k, c):
        copy = grp_copy(k, lax.rem(g + k, n_grp))
        copy.wait_send()
        copy.wait_recv()
        return c

    lax.fori_loop(1, n_grp, start2, 0)
    lax.fori_loop(1, n_path, finish_msg, 0)
    inc_ref[...] = inbuf[...]
    lax.fori_loop(1, n_grp, finish2, 0)
    grad_ref[...] = mid[...] + jnp.sum(recv2[...], axis=0)


def exchange_messages(outgoing, term, n_grp, n_path):
    n_k, cap, width = outgoing.shape
    _, rows, gwidth = term.shape
    return pl.pallas_call(
        lambda *refs: _message_kernel(n_grp, n_path, *refs),
        out_shape=(jax.ShapeDtypeStruct((n_k, cap, width), jnp.bfloat16),
                   jax.ShapeDtypeStruct((rows, gwidth), jnp.float32)),
        in_specs=[pl.BlockSpec(memory_space=pltpu.VMEM)] * 2,
        out_specs=(pl.BlockSpec(memory_space=pltpu.VMEM),) * 2,
        scratch_shapes=[
            pltpu.VMEM((n_k, cap, width), jnp.bfloat16),
            pltpu.VMEM((n_path - 1, rows, gwidth), jnp.float32),
            pltpu.VMEM((n_grp - 1, rows, gwidth), jnp.float32),
            pltpu.VMEM((rows, gwidth), jnp.float32),
            pltpu.SemaphoreType.DMA((n_path - 1,)),
            pltpu.SemaphoreType.DMA((n_path - 1,)),
            pltpu.SemaphoreType.DMA((n_path - 1,)),
            pltpu.SemaphoreType.DMA((n_path - 1,)),
            pltpu.SemaphoreType.DMA((n_grp - 1,)),
            pltpu.SemaphoreType.DMA((n_grp - 1,)),
        ],
        compiler_params=pltpu.CompilerParams(collective_id=1, has_side_effects=True),
    )(outgoing, term)


def shards(
    link_state, path_state, path_links, w_path_in, w_path_hid, w_link_in, w_link_hid, cotangent
):
    bf16, f32 = jnp.bfloat16, jnp.float32
    own_links = link_state[0]
    link_dev, width = own_links.shape
    n_grp = lax.axis_size("grp")
    peer_count = lax.axis_size("path")
    me = lax.axis_index("path")
    path_count, hop_count = path_links.shape
    entries = path_count * hop_count
    capacity = entries // peer_count
    slots = peer_count * capacity
    flat_ids = path_links.reshape(-1)
    is_live = flat_ids >= 0
    owner_id = jnp.where(is_live, flat_ids // link_dev, peer_count)
    local_id = jnp.where(is_live, flat_ids % link_dev, 0)
    marks = (owner_id[:, None] == jnp.arange(peer_count)[None, :]).astype(bf16)
    order = jnp.arange(entries)
    earlier = (order[None, :] < order[:, None]).astype(bf16)
    before = jnp.dot(earlier, marks, preferred_element_type=f32)
    slot_id = jnp.sum(before * marks.astype(f32), axis=1).astype(jnp.int32)
    offset = lax.rem(owner_id - me + peer_count, peer_count)
    dest = jnp.where(is_live, offset * capacity + slot_id, -1)
    slot_ids = jnp.arange(slots)
    route = dest[None, :] == slot_ids[:, None]
    requests = jnp.sum(jnp.where(route, local_id[None, :] + 1, 0), axis=1) - 1
    req = jnp.full((peer_count, 8, 128), -1, jnp.int32)
    req = lax.dynamic_update_slice(req, requests.reshape(peer_count, 1, capacity), (0, 0, 0))
    got, req_ids = fetch_rows(req, own_links, capacity, n_grp, peer_count)
    route_t = (dest[:, None] == slot_ids[None, :]).astype(bf16)
    fetched = jnp.dot(route_t, got.reshape(slots, width), preferred_element_type=f32).astype(bf16)
    projected = jnp.dot(fetched, w_path_in, preferred_element_type=f32)
    projected = projected.reshape(path_count, hop_count, 3 * width)
    live_grid = is_live.reshape(path_count, hop_count)
    carried = path_state[0].astype(f32)
    messages = []
    for hop_index in range(hop_count):
        renewed = gated_update(projected[:, hop_index], carried, w_path_hid)
        carried = jnp.where(live_grid[:, hop_index, None], renewed, carried)
        messages.append(carried.astype(bf16))
    path_final = carried.astype(bf16)
    flat_messages = jnp.stack(messages, axis=1).reshape(-1, width)
    outgoing = jnp.dot(route.astype(bf16), flat_messages, preferred_element_type=f32).astype(bf16)
    cot = cotangent[0].reshape(path_count, peer_count, -1)
    term = lax.dot_general(cot, path_final, (((0,), (0,)), ((), ())), preferred_element_type=f32)
    incoming, read_grad = exchange_messages(
        outgoing.reshape(peer_count, capacity, width), term, n_grp, peer_count)
    received = req_ids[:, 0, :capacity].reshape(-1)
    want = (received[:, None] == jnp.arange(link_dev)[None, :]).astype(bf16)
    link_sum = lax.dot_general(
        want, incoming.reshape(slots, width), (((0,), (0,)), ((), ())), preferred_element_type=f32
    )
    link_proj = jnp.dot(link_sum.astype(bf16), w_link_in, preferred_element_type=f32)
    link_next = gated_update(link_proj, own_links.astype(f32), w_link_hid).astype(bf16)
    return (link_next[None], path_final[None], read_grad)


def solution(mesh):
    return jax.shard_map(
        shards,
        mesh=mesh,
        in_specs=(
            P("grp", "path", None),
            P("grp", "path", None),
            P("path", None),
            P(),
            P(),
            P(),
            P(),
            P("grp", "path", None),
        ),
        out_specs=(P("grp", "path", None), P("grp", "path", None), P("path", None)),
        check_vma=False,
    )
```

```python
import jax
import jax.numpy as jnp
from jax import lax
from jax.experimental import pallas as pl
from jax.experimental.pallas import tpu as pltpu
from jax.sharding import PartitionSpec as P

MESH = pl.DeviceIdType.MESH


def gated_update(projected, carried, w_hidden):
    width = carried.shape[1]
    recur = jnp.dot(carried.astype(jnp.bfloat16), w_hidden, preferred_element_type=jnp.float32)
    reset = jax.nn.sigmoid(projected[:, :width] + recur[:, :width])
    update = jax.nn.sigmoid(projected[:, width : 2 * width] + recur[:, width : 2 * width])
    candidate = jnp.tanh(projected[:, 2 * width :] + reset * recur[:, 2 * width :])
    return (1.0 - update) * candidate + update * carried


def _greet(barrier, g, p, n_grp, n_path, with_grp):
    def greet_path(k, c):
        pl.semaphore_signal(barrier, inc=1, device_id=(g, lax.rem(p + k, n_path)), device_id_type=MESH)
        return c

    def greet_grp(k, c):
        pl.semaphore_signal(barrier, inc=1, device_id=(lax.rem(g + k, n_grp), p), device_id_type=MESH)
        return c

    lax.fori_loop(1, n_path, greet_path, 0)
    count = n_path - 1
    if with_grp:
        lax.fori_loop(1, n_grp, greet_grp, 0)
        count += n_grp - 1
    pl.semaphore_wait(barrier, count)


def _ring_copies(src, dst, send, recv, g, p, n_path, sign):
    def make(k):
        return pltpu.make_async_remote_copy(
            src_ref=src.at[k], dst_ref=dst.at[k], send_sem=send.at[k - 1], recv_sem=recv.at[k - 1],
            device_id=(g, lax.rem(p + sign * k + n_path, n_path)), device_id_type=MESH)

    def start(k, c):
        make(k).start()
        return c

    def finish(k, c):
        copy = make(k)
        copy.wait_send()
        copy.wait_recv()
        return c

    return start, finish


def _fetch_kernel(n_grp, n_path, req_ref, links_ref, got_ref, ids_ref,
                  reqin, want, served, gotbuf, rsend, rrecv, asend, arecv):
    g = lax.axis_index("grp")
    p = lax.axis_index("path")
    _greet(pltpu.get_barrier_semaphore(), g, p, n_grp, n_path, False)
    start_req, finish_req = _ring_copies(req_ref, reqin, rsend, rrecv, g, p, n_path, 1)
    lax.fori_loop(1, n_path, start_req, 0)
    reqin[0] = req_ref[0]
    lax.fori_loop(1, n_path, finish_req, 0)
    n_k, cap = served.shape[0], served.shape[1]
    link_dev = links_ref.shape[0]
    ids_t = jnp.transpose(reqin[:, 0, :])
    lanes = lax.broadcasted_iota(jnp.int32, (1, link_dev), 1)
    for k in range(n_k):
        want[k * cap : (k + 1) * cap, :] = (ids_t[0:cap, k : k + 1] == lanes).astype(jnp.bfloat16)
    rows = jnp.dot(want[...], links_ref[...], preferred_element_type=jnp.float32).astype(jnp.bfloat16)
    served[...] = rows.reshape(served.shape)
    start_ans, finish_ans = _ring_copies(served, gotbuf, asend, arecv, g, p, n_path, -1)
    lax.fori_loop(1, n_path, start_ans, 0)
    gotbuf[0] = served[0]
    ids_ref[...] = reqin[...]
    lax.fori_loop(1, n_path, finish_ans, 0)
    got_ref[...] = gotbuf[...]


def fetch_rows(req, own_links, cap, n_grp, n_path):
    n_k, rows, lanes = req.shape
    width = own_links.shape[1]
    return pl.pallas_call(
        lambda *refs: _fetch_kernel(n_grp, n_path, *refs),
        out_shape=(jax.ShapeDtypeStruct((n_k, cap, width), jnp.bfloat16),
                   jax.ShapeDtypeStruct((n_k, rows, lanes), jnp.int32)),
        in_specs=[pl.BlockSpec(memory_space=pltpu.VMEM)] * 2,
        out_specs=(pl.BlockSpec(memory_space=pltpu.VMEM),) * 2,
        scratch_shapes=[
            pltpu.VMEM((n_k, rows, lanes), jnp.int32),
            pltpu.VMEM((n_k * cap, own_links.shape[0]), jnp.bfloat16),
            pltpu.VMEM((n_k, cap, width), jnp.bfloat16),
            pltpu.VMEM((n_k, cap, width), jnp.bfloat16),
            pltpu.SemaphoreType.DMA((n_path - 1,)),
            pltpu.SemaphoreType.DMA((n_path - 1,)),
            pltpu.SemaphoreType.DMA((n_path - 1,)),
            pltpu.SemaphoreType.DMA((n_path - 1,)),
        ],
        compiler_params=pltpu.CompilerParams(collective_id=0, has_side_effects=True),
    )(req, own_links)


def _message_kernel(n_grp, n_path, out_ref, term_ref, inc_ref, grad_ref,
                    inbuf, recv1, recv2, mid, msend, mrecv, send1, got1, send2, got2):
    g = lax.axis_index("grp")
    p = lax.axis_index("path")
    _greet(pltpu.get_barrier_semaphore(), g, p, n_grp, n_path, True)
    start_msg, finish_msg = _ring_copies(out_ref, inbuf, msend, mrecv, g, p, n_path, 1)

    def path_copy(k, q):
        return pltpu.make_async_remote_copy(
            src_ref=term_ref.at[q], dst_ref=recv1.at[k - 1], send_sem=send1.at[k - 1],
            recv_sem=got1.at[k - 1], device_id=(g, q), device_id_type=MESH)

    def start1(k, c):
        path_copy(k, lax.rem(p + k, n_path)).start()
        return c

    def finish1(k, c):
        copy = path_copy(k, lax.rem(p + k, n_path))
        copy.wait_send()
        copy.wait_recv()
        return c

    lax.fori_loop(1, n_path, start1, 0)
    lax.fori_loop(1, n_path, start_msg, 0)
    inbuf[0] = out_ref[0]
    lax.fori_loop(1, n_path, finish1, 0)
    mid[...] = term_ref[p] + jnp.sum(recv1[...], axis=0)

    def grp_copy(k, h):
        return pltpu.make_async_remote_copy(
            src_ref=mid, dst_ref=recv2.at[k - 1], send_sem=send2.at[k - 1],
            recv_sem=got2.at[k - 1], device_id=(h, p), device_id_type=MESH)

    def start2(k, c):
        grp_copy(k, lax.rem(g + k, n_grp)).start()
        return c

    def finish2(k, c):
        copy = grp_copy(k, lax.rem(g + k, n_grp))
        copy.wait_send()
        copy.wait_recv()
        return c

    lax.fori_loop(1, n_grp, start2, 0)
    lax.fori_loop(1, n_path, finish_msg, 0)
    inc_ref[...] = inbuf[...]
    lax.fori_loop(1, n_grp, finish2, 0)
    grad_ref[...] = mid[...] + jnp.sum(recv2[...], axis=0)


def exchange_messages(outgoing, term, n_grp, n_path):
    n_k, cap, width = outgoing.shape
    _, rows, gwidth = term.shape
    return pl.pallas_call(
        lambda *refs: _message_kernel(n_grp, n_path, *refs),
        out_shape=(jax.ShapeDtypeStruct((n_k, cap, width), jnp.bfloat16),
                   jax.ShapeDtypeStruct((rows, gwidth), jnp.float32)),
        in_specs=[pl.BlockSpec(memory_space=pltpu.VMEM)] * 2,
        out_specs=(pl.BlockSpec(memory_space=pltpu.VMEM),) * 2,
        scratch_shapes=[
            pltpu.VMEM((n_k, cap, width), jnp.bfloat16),
            pltpu.VMEM((n_path - 1, rows, gwidth), jnp.float32),
            pltpu.VMEM((n_grp - 1, rows, gwidth), jnp.float32),
            pltpu.VMEM((rows, gwidth), jnp.float32),
            pltpu.SemaphoreType.DMA((n_path - 1,)),
            pltpu.SemaphoreType.DMA((n_path - 1,)),
            pltpu.SemaphoreType.DMA((n_path - 1,)),
            pltpu.SemaphoreType.DMA((n_path - 1,)),
            pltpu.SemaphoreType.DMA((n_grp - 1,)),
            pltpu.SemaphoreType.DMA((n_grp - 1,)),
        ],
        compiler_params=pltpu.CompilerParams(collective_id=1, has_side_effects=True),
    )(outgoing, term)


def _hop_kernel(hops, route_t_ref, got_ref, w_in_ref, w_hid_ref, state_ref, live_ref, route_ref, cot_t_ref,
                final_ref, out_ref, term_ref, proj, msgs):
    bf16, f32 = jnp.bfloat16, jnp.float32
    fetched = jnp.dot(route_t_ref[...], got_ref[...], preferred_element_type=f32).astype(bf16)
    proj[...] = jnp.dot(fetched, w_in_ref[...], preferred_element_type=f32)
    carried = state_ref[...].astype(f32)
    n, width = carried.shape
    for h in range(hops):
        p_h = proj[h * n : (h + 1) * n, :]
        renewed = gated_update(p_h, carried, w_hid_ref[...])
        carried = jnp.where(live_ref[:, h : h + 1] > 0, renewed, carried)
        msgs[h * n : (h + 1) * n, :] = carried.astype(bf16)
    final = carried.astype(bf16)
    final_ref[...] = final
    out_ref[...] = jnp.dot(route_ref[...], msgs[...], preferred_element_type=f32).astype(bf16)
    term_ref[...] = jnp.dot(cot_t_ref[...], final, preferred_element_type=f32)


def run_hops(route_t, got, w_path_in, w_path_hid, state, live, route, cot_t):
    entries, slots = route_t.shape
    n, width = state.shape
    hops = entries // n
    return pl.pallas_call(
        lambda *refs: _hop_kernel(hops, *refs),
        out_shape=(jax.ShapeDtypeStruct((n, width), jnp.bfloat16),
                   jax.ShapeDtypeStruct((slots, width), jnp.bfloat16),
                   jax.ShapeDtypeStruct((cot_t.shape[0], width), jnp.float32)),
        in_specs=[pl.BlockSpec(memory_space=pltpu.VMEM)] * 8,
        out_specs=(pl.BlockSpec(memory_space=pltpu.VMEM),) * 3,
        scratch_shapes=[
            pltpu.VMEM((entries, w_path_in.shape[1]), jnp.float32),
            pltpu.VMEM((entries, width), jnp.bfloat16),
        ],
    )(route_t, got, w_path_in, w_path_hid, state, live, route, cot_t)


def shards(
    link_state, path_state, path_links, w_path_in, w_path_hid, w_link_in, w_link_hid, cotangent
):
    bf16, f32 = jnp.bfloat16, jnp.float32
    own_links = link_state[0]
    link_dev, width = own_links.shape
    n_grp = lax.axis_size("grp")
    peer_count = lax.axis_size("path")
    me = lax.axis_index("path")
    path_count, hop_count = path_links.shape
    entries = path_count * hop_count
    capacity = entries // peer_count
    slots = peer_count * capacity
    flat_ids = path_links.reshape(-1)
    is_live = flat_ids >= 0
    owner_id = jnp.where(is_live, flat_ids // link_dev, peer_count)
    local_id = jnp.where(is_live, flat_ids % link_dev, 0)
    marks = (owner_id[:, None] == jnp.arange(peer_count)[None, :]).astype(bf16)
    order = jnp.arange(entries)
    earlier = (order[None, :] < order[:, None]).astype(bf16)
    before = jnp.dot(earlier, marks, preferred_element_type=f32)
    slot_id = jnp.sum(before * marks.astype(f32), axis=1).astype(jnp.int32)
    offset = lax.rem(owner_id - me + peer_count, peer_count)
    dest = jnp.where(is_live, offset * capacity + slot_id, -1)
    dest = dest.reshape(path_count, hop_count).T.reshape(-1)
    local_id = local_id.reshape(path_count, hop_count).T.reshape(-1)
    slot_ids = jnp.arange(slots)
    route = dest[None, :] == slot_ids[:, None]
    requests = jnp.sum(jnp.where(route, local_id[None, :] + 1, 0), axis=1) - 1
    req = jnp.full((peer_count, 8, 128), -1, jnp.int32)
    req = lax.dynamic_update_slice(req, requests.reshape(peer_count, 1, capacity), (0, 0, 0))
    route_t = (dest[:, None] == slot_ids[None, :]).astype(bf16)
    live_grid = is_live.reshape(path_count, hop_count).astype(jnp.int32)
    cot_t = cotangent[0].T
    got, req_ids = fetch_rows(req, own_links, capacity, n_grp, peer_count)
    path_final, outgoing, term = run_hops(
        route_t, got.reshape(slots, width), w_path_in, w_path_hid, path_state[0], live_grid,
        route.astype(bf16), cot_t)
    term = term.reshape(peer_count, -1, width)
    incoming, read_grad = exchange_messages(
        outgoing.reshape(peer_count, capacity, width), term, n_grp, peer_count)
    received = req_ids[:, 0, :capacity].reshape(-1)
    want = (received[:, None] == jnp.arange(link_dev)[None, :]).astype(bf16)
    link_sum = lax.dot_general(
        want, incoming.reshape(slots, width), (((0,), (0,)), ((), ())), preferred_element_type=f32
    )
    link_proj = jnp.dot(link_sum.astype(bf16), w_link_in, preferred_element_type=f32)
    link_next = gated_update(link_proj, own_links.astype(f32), w_link_hid).astype(bf16)
    return (link_next[None], path_final[None], read_grad)


def solution(mesh):
    return jax.shard_map(
        shards,
        mesh=mesh,
        in_specs=(
            P("grp", "path", None),
            P("grp", "path", None),
            P("path", None),
            P(),
            P(),
            P(),
            P(),
            P("grp", "path", None),
        ),
        out_specs=(P("grp", "path", None), P("grp", "path", None), P("path", None)),
        check_vma=False,
    )
```

```python
import jax
import jax.numpy as jnp
from jax import lax
from jax.experimental import pallas as pl
from jax.experimental.pallas import tpu as pltpu
from jax.sharding import PartitionSpec as P

MESH = pl.DeviceIdType.MESH


def gated_update(projected, carried, w_hidden):
    width = carried.shape[1]
    recur = jnp.dot(carried.astype(jnp.bfloat16), w_hidden, preferred_element_type=jnp.float32)
    reset = jax.nn.sigmoid(projected[:, :width] + recur[:, :width])
    update = jax.nn.sigmoid(projected[:, width : 2 * width] + recur[:, width : 2 * width])
    candidate = jnp.tanh(projected[:, 2 * width :] + reset * recur[:, 2 * width :])
    return (1.0 - update) * candidate + update * carried


def _greet(barrier, g, p, n_grp, n_path, with_grp):
    def greet_path(k, c):
        pl.semaphore_signal(barrier, inc=1, device_id=(g, lax.rem(p + k, n_path)), device_id_type=MESH)
        return c

    def greet_grp(k, c):
        pl.semaphore_signal(barrier, inc=1, device_id=(lax.rem(g + k, n_grp), p), device_id_type=MESH)
        return c

    lax.fori_loop(1, n_path, greet_path, 0)
    count = n_path - 1
    if with_grp:
        lax.fori_loop(1, n_grp, greet_grp, 0)
        count += n_grp - 1
    pl.semaphore_wait(barrier, count)


def _ring_copies(src, dst, send, recv, g, p, n_path, sign):
    def make(k):
        return pltpu.make_async_remote_copy(
            src_ref=src.at[k], dst_ref=dst.at[k], send_sem=send.at[k - 1], recv_sem=recv.at[k - 1],
            device_id=(g, lax.rem(p + sign * k + n_path, n_path)), device_id_type=MESH)

    def start(k, c):
        make(k).start()
        return c

    def finish(k, c):
        copy = make(k)
        copy.wait_send()
        copy.wait_recv()
        return c

    return start, finish


def _fetch_kernel(n_grp, n_path, req_ref, links_ref, got_ref, ids_ref,
                  reqin, want, served, gotbuf, rsend, rrecv, asend, arecv):
    g = lax.axis_index("grp")
    p = lax.axis_index("path")
    _greet(pltpu.get_barrier_semaphore(), g, p, n_grp, n_path, False)
    start_req, finish_req = _ring_copies(req_ref, reqin, rsend, rrecv, g, p, n_path, 1)
    lax.fori_loop(1, n_path, start_req, 0)
    reqin[0] = req_ref[0]
    lax.fori_loop(1, n_path, finish_req, 0)
    n_k, cap = served.shape[0], served.shape[1]
    link_dev = links_ref.shape[0]
    ids_t = jnp.transpose(reqin[:, 0, :])
    lanes = lax.broadcasted_iota(jnp.int32, (1, link_dev), 1)
    for k in range(n_k):
        want[k * cap : (k + 1) * cap, :] = (ids_t[0:cap, k : k + 1] == lanes).astype(jnp.bfloat16)
    rows = jnp.dot(want[...], links_ref[...], preferred_element_type=jnp.float32).astype(jnp.bfloat16)
    served[...] = rows.reshape(served.shape)
    start_ans, finish_ans = _ring_copies(served, gotbuf, asend, arecv, g, p, n_path, -1)
    lax.fori_loop(1, n_path, start_ans, 0)
    gotbuf[0] = served[0]
    ids_ref[...] = reqin[...]
    lax.fori_loop(1, n_path, finish_ans, 0)
    got_ref[...] = gotbuf[...]


def fetch_rows(req, own_links, cap, n_grp, n_path):
    n_k, rows, lanes = req.shape
    width = own_links.shape[1]
    return pl.pallas_call(
        lambda *refs: _fetch_kernel(n_grp, n_path, *refs),
        out_shape=(jax.ShapeDtypeStruct((n_k, cap, width), jnp.bfloat16),
                   jax.ShapeDtypeStruct((n_k, rows, lanes), jnp.int32)),
        in_specs=[pl.BlockSpec(memory_space=pltpu.VMEM)] * 2,
        out_specs=(pl.BlockSpec(memory_space=pltpu.VMEM),) * 2,
        scratch_shapes=[
            pltpu.VMEM((n_k, rows, lanes), jnp.int32),
            pltpu.VMEM((n_k * cap, own_links.shape[0]), jnp.bfloat16),
            pltpu.VMEM((n_k, cap, width), jnp.bfloat16),
            pltpu.VMEM((n_k, cap, width), jnp.bfloat16),
            pltpu.SemaphoreType.DMA((n_path - 1,)),
            pltpu.SemaphoreType.DMA((n_path - 1,)),
            pltpu.SemaphoreType.DMA((n_path - 1,)),
            pltpu.SemaphoreType.DMA((n_path - 1,)),
        ],
        compiler_params=pltpu.CompilerParams(collective_id=0, has_side_effects=True),
    )(req, own_links)


def _message_kernel(n_grp, n_path, out_ref, term_ref, inc_ref, grad_ref,
                    inbuf, recv1, recv2, mid, msend, mrecv, send1, got1, send2, got2):
    g = lax.axis_index("grp")
    p = lax.axis_index("path")
    _greet(pltpu.get_barrier_semaphore(), g, p, n_grp, n_path, True)
    start_msg, finish_msg = _ring_copies(out_ref, inbuf, msend, mrecv, g, p, n_path, 1)

    def path_copy(k, q):
        return pltpu.make_async_remote_copy(
            src_ref=term_ref.at[q], dst_ref=recv1.at[k - 1], send_sem=send1.at[k - 1],
            recv_sem=got1.at[k - 1], device_id=(g, q), device_id_type=MESH)

    def start1(k, c):
        path_copy(k, lax.rem(p + k, n_path)).start()
        return c

    def finish1(k, c):
        copy = path_copy(k, lax.rem(p + k, n_path))
        copy.wait_send()
        copy.wait_recv()
        return c

    lax.fori_loop(1, n_path, start1, 0)
    lax.fori_loop(1, n_path, start_msg, 0)
    inbuf[0] = out_ref[0]
    lax.fori_loop(1, n_path, finish1, 0)
    mid[...] = term_ref[p] + jnp.sum(recv1[...], axis=0)

    def grp_copy(k, h):
        return pltpu.make_async_remote_copy(
            src_ref=mid, dst_ref=recv2.at[k - 1], send_sem=send2.at[k - 1],
            recv_sem=got2.at[k - 1], device_id=(h, p), device_id_type=MESH)

    def start2(k, c):
        grp_copy(k, lax.rem(g + k, n_grp)).start()
        return c

    def finish2(k, c):
        copy = grp_copy(k, lax.rem(g + k, n_grp))
        copy.wait_send()
        copy.wait_recv()
        return c

    lax.fori_loop(1, n_grp, start2, 0)
    lax.fori_loop(1, n_path, finish_msg, 0)
    inc_ref[...] = inbuf[...]
    lax.fori_loop(1, n_grp, finish2, 0)
    grad_ref[...] = mid[...] + jnp.sum(recv2[...], axis=0)


def exchange_messages(outgoing, term, n_grp, n_path):
    n_k, cap, width = outgoing.shape
    _, rows, gwidth = term.shape
    return pl.pallas_call(
        lambda *refs: _message_kernel(n_grp, n_path, *refs),
        out_shape=(jax.ShapeDtypeStruct((n_k, cap, width), jnp.bfloat16),
                   jax.ShapeDtypeStruct((rows, gwidth), jnp.float32)),
        in_specs=[pl.BlockSpec(memory_space=pltpu.VMEM)] * 2,
        out_specs=(pl.BlockSpec(memory_space=pltpu.VMEM),) * 2,
        scratch_shapes=[
            pltpu.VMEM((n_k, cap, width), jnp.bfloat16),
            pltpu.VMEM((n_path - 1, rows, gwidth), jnp.float32),
            pltpu.VMEM((n_grp - 1, rows, gwidth), jnp.float32),
            pltpu.VMEM((rows, gwidth), jnp.float32),
            pltpu.SemaphoreType.DMA((n_path - 1,)),
            pltpu.SemaphoreType.DMA((n_path - 1,)),
            pltpu.SemaphoreType.DMA((n_path - 1,)),
            pltpu.SemaphoreType.DMA((n_path - 1,)),
            pltpu.SemaphoreType.DMA((n_grp - 1,)),
            pltpu.SemaphoreType.DMA((n_grp - 1,)),
        ],
        compiler_params=pltpu.CompilerParams(collective_id=1, has_side_effects=True),
    )(outgoing, term)


def _hop_kernel(hops, dcol_ref, got_ref, w_in_ref, w_hid_ref, state_ref, live_ref, drow_ref, cot_t_ref,
                final_ref, out_ref, term_ref, proj, msgs):
    bf16, f32 = jnp.bfloat16, jnp.float32
    entries, slots = dcol_ref.shape[0], got_ref.shape[0]
    route_t = (dcol_ref[:, 0:1] == lax.broadcasted_iota(jnp.int32, (1, slots), 1)).astype(bf16)
    fetched = jnp.dot(route_t, got_ref[...], preferred_element_type=f32).astype(bf16)
    proj[...] = jnp.dot(fetched, w_in_ref[...], preferred_element_type=f32)
    carried = state_ref[...].astype(f32)
    n, width = carried.shape
    for h in range(hops):
        p_h = proj[h * n : (h + 1) * n, :]
        renewed = gated_update(p_h, carried, w_hid_ref[...])
        carried = jnp.where(live_ref[:, h : h + 1] > 0, renewed, carried)
        msgs[h * n : (h + 1) * n, :] = carried.astype(bf16)
    final = carried.astype(bf16)
    final_ref[...] = final
    route = (lax.broadcasted_iota(jnp.int32, (slots, 1), 0) == drow_ref[...]).astype(bf16)
    out_ref[...] = jnp.dot(route, msgs[...], preferred_element_type=f32).astype(bf16)
    term = jnp.dot(cot_t_ref[...], final, preferred_element_type=f32)
    share = term_ref.shape[1]
    for q in range(term_ref.shape[0]):
        term_ref[q] = term[q * share : (q + 1) * share, :]


def run_hops(dcol, got, w_path_in, w_path_hid, state, live, drow, cot_t, n_path):
    entries = dcol.shape[0]
    slots = got.shape[0]
    n, width = state.shape
    hops = entries // n
    return pl.pallas_call(
        lambda *refs: _hop_kernel(hops, *refs),
        out_shape=(jax.ShapeDtypeStruct((n, width), jnp.bfloat16),
                   jax.ShapeDtypeStruct((slots, width), jnp.bfloat16),
                   jax.ShapeDtypeStruct((n_path, cot_t.shape[0] // n_path, width), jnp.float32)),
        in_specs=[pl.BlockSpec(memory_space=pltpu.VMEM)] * 8,
        out_specs=(pl.BlockSpec(memory_space=pltpu.VMEM),) * 3,
        scratch_shapes=[
            pltpu.VMEM((entries, w_path_in.shape[1]), jnp.float32),
            pltpu.VMEM((entries, width), jnp.bfloat16),
        ],
    )(dcol, got, w_path_in, w_path_hid, state, live, drow, cot_t)


def shards(
    link_state, path_state, path_links, w_path_in, w_path_hid, w_link_in, w_link_hid, cotangent
):
    bf16, f32 = jnp.bfloat16, jnp.float32
    own_links = link_state[0]
    link_dev, width = own_links.shape
    n_grp = lax.axis_size("grp")
    peer_count = lax.axis_size("path")
    me = lax.axis_index("path")
    path_count, hop_count = path_links.shape
    entries = path_count * hop_count
    capacity = entries // peer_count
    slots = peer_count * capacity
    flat_ids = path_links.reshape(-1)
    is_live = flat_ids >= 0
    owner_id = jnp.where(is_live, flat_ids // link_dev, peer_count)
    local_id = jnp.where(is_live, flat_ids % link_dev, 0)
    marks = (owner_id[:, None] == jnp.arange(peer_count)[None, :]).astype(bf16)
    order = jnp.arange(entries)
    earlier = (order[None, :] < order[:, None]).astype(bf16)
    before = jnp.dot(earlier, marks, preferred_element_type=f32)
    slot_id = jnp.sum(before * marks.astype(f32), axis=1).astype(jnp.int32)
    offset = lax.rem(owner_id - me + peer_count, peer_count)
    dest = jnp.where(is_live, offset * capacity + slot_id, -1)
    dest = dest.reshape(path_count, hop_count).T.reshape(-1)
    local_id = local_id.reshape(path_count, hop_count).T.reshape(-1)
    slot_ids = jnp.arange(slots)
    route = dest[None, :] == slot_ids[:, None]
    requests = jnp.sum(jnp.where(route, local_id[None, :] + 1, 0), axis=1) - 1
    req = jnp.full((peer_count, 8, 128), -1, jnp.int32)
    req = lax.dynamic_update_slice(req, requests.reshape(peer_count, 1, capacity), (0, 0, 0))
    live_grid = is_live.reshape(path_count, hop_count).astype(jnp.int32)
    cot_t = cotangent[0].T
    got, req_ids = fetch_rows(req, own_links, capacity, n_grp, peer_count)
    dcol = jnp.broadcast_to(dest[:, None], (entries, 128))
    path_final, outgoing, term = run_hops(
        dcol, got.reshape(slots, width), w_path_in, w_path_hid, path_state[0], live_grid,
        dest[None, :], cot_t, peer_count)
    incoming, read_grad = exchange_messages(
        outgoing.reshape(peer_count, capacity, width), term, n_grp, peer_count)
    received = req_ids[:, 0, :capacity].reshape(-1)
    want = (received[:, None] == jnp.arange(link_dev)[None, :]).astype(bf16)
    link_sum = lax.dot_general(
        want, incoming.reshape(slots, width), (((0,), (0,)), ((), ())), preferred_element_type=f32
    )
    link_proj = jnp.dot(link_sum.astype(bf16), w_link_in, preferred_element_type=f32)
    link_next = gated_update(link_proj, own_links.astype(f32), w_link_hid).astype(bf16)
    return (link_next[None], path_final[None], read_grad)


def solution(mesh):
    return jax.shard_map(
        shards,
        mesh=mesh,
        in_specs=(
            P("grp", "path", None),
            P("grp", "path", None),
            P("path", None),
            P(),
            P(),
            P(),
            P(),
            P("grp", "path", None),
        ),
        out_specs=(P("grp", "path", None), P("grp", "path", None), P("path", None)),
        check_vma=False,
    )
```

```python
import jax
import jax.numpy as jnp
from jax import lax
from jax.experimental import pallas as pl
from jax.experimental.pallas import tpu as pltpu
from jax.sharding import PartitionSpec as P

MESH = pl.DeviceIdType.MESH


def gated_update(projected, carried, w_hidden):
    width = carried.shape[1]
    recur = jnp.dot(carried.astype(jnp.bfloat16), w_hidden, preferred_element_type=jnp.float32)
    reset = jax.nn.sigmoid(projected[:, :width] + recur[:, :width])
    update = jax.nn.sigmoid(projected[:, width : 2 * width] + recur[:, width : 2 * width])
    candidate = jnp.tanh(projected[:, 2 * width :] + reset * recur[:, 2 * width :])
    return (1.0 - update) * candidate + update * carried


def _greet(barrier, g, p, n_grp, n_path, with_grp):
    def greet_path(k, c):
        pl.semaphore_signal(barrier, inc=1, device_id=(g, lax.rem(p + k, n_path)), device_id_type=MESH)
        return c

    def greet_grp(k, c):
        pl.semaphore_signal(barrier, inc=1, device_id=(lax.rem(g + k, n_grp), p), device_id_type=MESH)
        return c

    lax.fori_loop(1, n_path, greet_path, 0)
    count = n_path - 1
    if with_grp:
        lax.fori_loop(1, n_grp, greet_grp, 0)
        count += n_grp - 1
    pl.semaphore_wait(barrier, count)


def _ring_copies(src, dst, send, recv, g, p, n_path, sign):
    def make(k):
        return pltpu.make_async_remote_copy(
            src_ref=src.at[k], dst_ref=dst.at[k], send_sem=send.at[k - 1], recv_sem=recv.at[k - 1],
            device_id=(g, lax.rem(p + sign * k + n_path, n_path)), device_id_type=MESH)

    def start(k, c):
        make(k).start()
        return c

    def finish(k, c):
        copy = make(k)
        copy.wait_send()
        copy.wait_recv()
        return c

    return start, finish


def _fetch_kernel(n_grp, n_path, req_ref, links_ref, got_ref, ids_ref,
                  reqin, want, served, gotbuf, rsend, rrecv, asend, arecv):
    g = lax.axis_index("grp")
    p = lax.axis_index("path")
    _greet(pltpu.get_barrier_semaphore(), g, p, n_grp, n_path, False)
    start_req, finish_req = _ring_copies(req_ref, reqin, rsend, rrecv, g, p, n_path, 1)
    lax.fori_loop(1, n_path, start_req, 0)
    reqin[0] = req_ref[0]
    lax.fori_loop(1, n_path, finish_req, 0)
    n_k, cap = served.shape[0], served.shape[1]
    link_dev = links_ref.shape[0]
    ids_t = jnp.transpose(reqin[:, 0, :])
    lanes = lax.broadcasted_iota(jnp.int32, (1, link_dev), 1)
    for k in range(n_k):
        want[k * cap : (k + 1) * cap, :] = (ids_t[0:cap, k : k + 1] == lanes).astype(jnp.bfloat16)
    rows = jnp.dot(want[...], links_ref[...], preferred_element_type=jnp.float32).astype(jnp.bfloat16)
    served[...] = rows.reshape(served.shape)
    start_ans, finish_ans = _ring_copies(served, gotbuf, asend, arecv, g, p, n_path, -1)
    lax.fori_loop(1, n_path, start_ans, 0)
    gotbuf[0] = served[0]
    ids_ref[...] = reqin[...]
    lax.fori_loop(1, n_path, finish_ans, 0)
    got_ref[...] = gotbuf[...]


def fetch_rows(req, own_links, cap, n_grp, n_path):
    n_k, rows, lanes = req.shape
    width = own_links.shape[1]
    return pl.pallas_call(
        lambda *refs: _fetch_kernel(n_grp, n_path, *refs),
        out_shape=(jax.ShapeDtypeStruct((n_k, cap, width), jnp.bfloat16),
                   jax.ShapeDtypeStruct((n_k, rows, lanes), jnp.int32)),
        in_specs=[pl.BlockSpec(memory_space=pltpu.VMEM)] * 2,
        out_specs=(pl.BlockSpec(memory_space=pltpu.VMEM),) * 2,
        scratch_shapes=[
            pltpu.VMEM((n_k, rows, lanes), jnp.int32),
            pltpu.VMEM((n_k * cap, own_links.shape[0]), jnp.bfloat16),
            pltpu.VMEM((n_k, cap, width), jnp.bfloat16),
            pltpu.VMEM((n_k, cap, width), jnp.bfloat16),
            pltpu.SemaphoreType.DMA((n_path - 1,)),
            pltpu.SemaphoreType.DMA((n_path - 1,)),
            pltpu.SemaphoreType.DMA((n_path - 1,)),
            pltpu.SemaphoreType.DMA((n_path - 1,)),
        ],
        compiler_params=pltpu.CompilerParams(collective_id=0, has_side_effects=True),
    )(req, own_links)


def _message_kernel(n_grp, n_path, out_ref, term_ref, inc_ref, grad_ref,
                    inbuf, recv1, recv2, mid, msend, mrecv, send1, got1, send2, got2):
    g = lax.axis_index("grp")
    p = lax.axis_index("path")
    _greet(pltpu.get_barrier_semaphore(), g, p, n_grp, n_path, True)
    start_msg, finish_msg = _ring_copies(out_ref, inbuf, msend, mrecv, g, p, n_path, 1)

    def path_copy(k, q):
        return pltpu.make_async_remote_copy(
            src_ref=term_ref.at[q], dst_ref=recv1.at[k - 1], send_sem=send1.at[k - 1],
            recv_sem=got1.at[k - 1], device_id=(g, q), device_id_type=MESH)

    def start1(k, c):
        path_copy(k, lax.rem(p + k, n_path)).start()
        return c

    def finish1(k, c):
        copy = path_copy(k, lax.rem(p + k, n_path))
        copy.wait_send()
        copy.wait_recv()
        return c

    lax.fori_loop(1, n_path, start1, 0)
    lax.fori_loop(1, n_path, start_msg, 0)
    inbuf[0] = out_ref[0]
    lax.fori_loop(1, n_path, finish1, 0)
    mid[...] = term_ref[p] + jnp.sum(recv1[...], axis=0)

    def grp_copy(k, h):
        return pltpu.make_async_remote_copy(
            src_ref=mid, dst_ref=recv2.at[k - 1], send_sem=send2.at[k - 1],
            recv_sem=got2.at[k - 1], device_id=(h, p), device_id_type=MESH)

    def start2(k, c):
        grp_copy(k, lax.rem(g + k, n_grp)).start()
        return c

    def finish2(k, c):
        copy = grp_copy(k, lax.rem(g + k, n_grp))
        copy.wait_send()
        copy.wait_recv()
        return c

    lax.fori_loop(1, n_grp, start2, 0)
    lax.fori_loop(1, n_path, finish_msg, 0)
    inc_ref[...] = inbuf[...]
    lax.fori_loop(1, n_grp, finish2, 0)
    grad_ref[...] = mid[...] + jnp.sum(recv2[...], axis=0)


def exchange_messages(outgoing, term, n_grp, n_path):
    n_k, cap, width = outgoing.shape
    _, rows, gwidth = term.shape
    return pl.pallas_call(
        lambda *refs: _message_kernel(n_grp, n_path, *refs),
        out_shape=(jax.ShapeDtypeStruct((n_k, cap, width), jnp.bfloat16),
                   jax.ShapeDtypeStruct((rows, gwidth), jnp.float32)),
        in_specs=[pl.BlockSpec(memory_space=pltpu.VMEM)] * 2,
        out_specs=(pl.BlockSpec(memory_space=pltpu.VMEM),) * 2,
        scratch_shapes=[
            pltpu.VMEM((n_k, cap, width), jnp.bfloat16),
            pltpu.VMEM((n_path - 1, rows, gwidth), jnp.float32),
            pltpu.VMEM((n_grp - 1, rows, gwidth), jnp.float32),
            pltpu.VMEM((rows, gwidth), jnp.float32),
            pltpu.SemaphoreType.DMA((n_path - 1,)),
            pltpu.SemaphoreType.DMA((n_path - 1,)),
            pltpu.SemaphoreType.DMA((n_path - 1,)),
            pltpu.SemaphoreType.DMA((n_path - 1,)),
            pltpu.SemaphoreType.DMA((n_grp - 1,)),
            pltpu.SemaphoreType.DMA((n_grp - 1,)),
        ],
        compiler_params=pltpu.CompilerParams(collective_id=1, has_side_effects=True),
    )(outgoing, term)


def _hop_kernel(hops, dcol_ref, got_ref, w_in_ref, w_hid_ref, state_ref, live_ref, drow_ref, cot_t_ref,
                final_ref, out_ref, term_ref, proj, msgs):
    bf16, f32 = jnp.bfloat16, jnp.float32
    entries, slots = dcol_ref.shape[1], got_ref.shape[0]
    dcol = jnp.transpose(dcol_ref[...])[:, 0:1]
    route_t = (dcol == lax.broadcasted_iota(jnp.int32, (1, slots), 1)).astype(bf16)
    fetched = jnp.dot(route_t, got_ref[...], preferred_element_type=f32).astype(bf16)
    proj[...] = jnp.dot(fetched, w_in_ref[...], preferred_element_type=f32)
    carried = state_ref[...].astype(f32)
    n, width = carried.shape
    for h in range(hops):
        p_h = proj[h * n : (h + 1) * n, :]
        renewed = gated_update(p_h, carried, w_hid_ref[...])
        carried = jnp.where(live_ref[:, h : h + 1] > 0, renewed, carried)
        msgs[h * n : (h + 1) * n, :] = carried.astype(bf16)
    final = carried.astype(bf16)
    final_ref[...] = final
    route = (lax.broadcasted_iota(jnp.int32, (slots, 1), 0) == drow_ref[...]).astype(bf16)
    out_ref[...] = jnp.dot(route, msgs[...], preferred_element_type=f32).astype(bf16)
    cot_t = jnp.transpose(cot_t_ref[...].astype(f32)).astype(bf16)
    term = jnp.dot(cot_t, final, preferred_element_type=f32)
    share = term_ref.shape[1]
    for q in range(term_ref.shape[0]):
        term_ref[q] = term[q * share : (q + 1) * share, :]


def run_hops(dcol, got, w_path_in, w_path_hid, state, live, drow, cot_t, n_path):
    entries = dcol.shape[1]
    slots = got.shape[0]
    n, width = state.shape
    hops = entries // n
    return pl.pallas_call(
        lambda *refs: _hop_kernel(hops, *refs),
        out_shape=(jax.ShapeDtypeStruct((n, width), jnp.bfloat16),
                   jax.ShapeDtypeStruct((slots, width), jnp.bfloat16),
                   jax.ShapeDtypeStruct((n_path, cot_t.shape[1] // n_path, width), jnp.float32)),
        in_specs=[pl.BlockSpec(memory_space=pltpu.VMEM)] * 8,
        out_specs=(pl.BlockSpec(memory_space=pltpu.VMEM),) * 3,
        scratch_shapes=[
            pltpu.VMEM((entries, w_path_in.shape[1]), jnp.float32),
            pltpu.VMEM((entries, width), jnp.bfloat16),
        ],
    )(dcol, got, w_path_in, w_path_hid, state, live, drow, cot_t)


def shards(
    link_state, path_state, path_links, w_path_in, w_path_hid, w_link_in, w_link_hid, cotangent
):
    bf16, f32 = jnp.bfloat16, jnp.float32
    own_links = link_state[0]
    link_dev, width = own_links.shape
    n_grp = lax.axis_size("grp")
    peer_count = lax.axis_size("path")
    me = lax.axis_index("path")
    path_count, hop_count = path_links.shape
    entries = path_count * hop_count
    capacity = entries // peer_count
    slots = peer_count * capacity
    flat_ids = path_links.reshape(-1)
    is_live = flat_ids >= 0
    owner_id = jnp.where(is_live, flat_ids // link_dev, peer_count)
    local_id = jnp.where(is_live, flat_ids % link_dev, 0)
    marks = (owner_id[:, None] == jnp.arange(peer_count)[None, :]).astype(bf16)
    order = jnp.arange(entries)
    earlier = (order[None, :] < order[:, None]).astype(bf16)
    before = jnp.dot(earlier, marks, preferred_element_type=f32)
    slot_id = jnp.sum(before * marks.astype(f32), axis=1).astype(jnp.int32)
    offset = lax.rem(owner_id - me + peer_count, peer_count)
    dest = jnp.where(is_live, offset * capacity + slot_id, -1)
    dest = dest.reshape(path_count, hop_count).T.reshape(-1)
    local_id = local_id.reshape(path_count, hop_count).T.reshape(-1)
    slot_ids = jnp.arange(slots)
    route = dest[None, :] == slot_ids[:, None]
    requests = jnp.sum(jnp.where(route, local_id[None, :] + 1, 0), axis=1) - 1
    req = jnp.full((peer_count, 8, 128), -1, jnp.int32)
    req = lax.dynamic_update_slice(req, requests.reshape(peer_count, 1, capacity), (0, 0, 0))
    live_grid = is_live.reshape(path_count, hop_count).astype(jnp.int32)
    got, req_ids = fetch_rows(req, own_links, capacity, n_grp, peer_count)
    drow = jnp.broadcast_to(dest[None, :], (8, entries))
    path_final, outgoing, term = run_hops(
        drow, got.reshape(slots, width), w_path_in, w_path_hid, path_state[0], live_grid,
        drow[0:1], cotangent[0], peer_count)
    incoming, read_grad = exchange_messages(
        outgoing.reshape(peer_count, capacity, width), term, n_grp, peer_count)
    received = req_ids[:, 0, :capacity].reshape(-1)
    want = (received[:, None] == jnp.arange(link_dev)[None, :]).astype(bf16)
    link_sum = lax.dot_general(
        want, incoming.reshape(slots, width), (((0,), (0,)), ((), ())), preferred_element_type=f32
    )
    link_proj = jnp.dot(link_sum.astype(bf16), w_link_in, preferred_element_type=f32)
    link_next = gated_update(link_proj, own_links.astype(f32), w_link_hid).astype(bf16)
    return (link_next[None], path_final[None], read_grad)


def solution(mesh):
    return jax.shard_map(
        shards,
        mesh=mesh,
        in_specs=(
            P("grp", "path", None),
            P("grp", "path", None),
            P("path", None),
            P(),
            P(),
            P(),
            P(),
            P("grp", "path", None),
        ),
        out_specs=(P("grp", "path", None), P("grp", "path", None), P("path", None)),
        check_vma=False,
    )
```

```python
import jax
import jax.numpy as jnp
from jax import lax
from jax.experimental import pallas as pl
from jax.experimental.pallas import tpu as pltpu
from jax.sharding import PartitionSpec as P

MESH = pl.DeviceIdType.MESH


def gated_update(projected, carried, w_hidden):
    width = carried.shape[1]
    recur = jnp.dot(carried.astype(jnp.bfloat16), w_hidden, preferred_element_type=jnp.float32)
    reset = jax.nn.sigmoid(projected[:, :width] + recur[:, :width])
    update = jax.nn.sigmoid(projected[:, width : 2 * width] + recur[:, width : 2 * width])
    candidate = jnp.tanh(projected[:, 2 * width :] + reset * recur[:, 2 * width :])
    return (1.0 - update) * candidate + update * carried


def _greet(barrier, g, p, n_grp, n_path, with_grp):
    def greet_path(k, c):
        pl.semaphore_signal(barrier, inc=1, device_id=(g, lax.rem(p + k, n_path)), device_id_type=MESH)
        return c

    def greet_grp(k, c):
        pl.semaphore_signal(barrier, inc=1, device_id=(lax.rem(g + k, n_grp), p), device_id_type=MESH)
        return c

    lax.fori_loop(1, n_path, greet_path, 0)
    count = n_path - 1
    if with_grp:
        lax.fori_loop(1, n_grp, greet_grp, 0)
        count += n_grp - 1
    pl.semaphore_wait(barrier, count)


def _ring_copies(src, dst, send, recv, g, p, n_path, sign):
    def make(k):
        return pltpu.make_async_remote_copy(
            src_ref=src.at[k], dst_ref=dst.at[k], send_sem=send.at[k - 1], recv_sem=recv.at[k - 1],
            device_id=(g, lax.rem(p + sign * k + n_path, n_path)), device_id_type=MESH)

    def start(k, c):
        make(k).start()
        return c

    def finish(k, c):
        copy = make(k)
        copy.wait_send()
        copy.wait_recv()
        return c

    return start, finish


def _fetch_kernel(n_grp, n_path, req_ref, links_ref, got_ref, ids_ref,
                  reqin, want, served, gotbuf, rsend, rrecv, asend, arecv, greet=True):
    g = lax.axis_index("grp")
    p = lax.axis_index("path")
    if greet:
        _greet(pltpu.get_barrier_semaphore(), g, p, n_grp, n_path, False)
    start_req, finish_req = _ring_copies(req_ref, reqin, rsend, rrecv, g, p, n_path, 1)
    lax.fori_loop(1, n_path, start_req, 0)
    reqin[0] = req_ref[0]
    lax.fori_loop(1, n_path, finish_req, 0)
    n_k, cap = served.shape[0], served.shape[1]
    link_dev = links_ref.shape[0]
    ids_t = jnp.transpose(reqin[:, 0, :])
    lanes = lax.broadcasted_iota(jnp.int32, (1, link_dev), 1)
    for k in range(n_k):
        want[k * cap : (k + 1) * cap, :] = (ids_t[0:cap, k : k + 1] == lanes).astype(jnp.bfloat16)
    rows = jnp.dot(want[...], links_ref[...], preferred_element_type=jnp.float32).astype(jnp.bfloat16)
    served[...] = rows.reshape(served.shape)
    start_ans, finish_ans = _ring_copies(served, gotbuf, asend, arecv, g, p, n_path, -1)
    lax.fori_loop(1, n_path, start_ans, 0)
    gotbuf[0] = served[0]
    ids_ref[...] = reqin[...]
    lax.fori_loop(1, n_path, finish_ans, 0)
    got_ref[...] = gotbuf[...]


def fetch_rows(req, own_links, cap, n_grp, n_path):
    n_k, rows, lanes = req.shape
    width = own_links.shape[1]
    return pl.pallas_call(
        lambda *refs: _fetch_kernel(n_grp, n_path, *refs),
        out_shape=(jax.ShapeDtypeStruct((n_k, cap, width), jnp.bfloat16),
                   jax.ShapeDtypeStruct((n_k, rows, lanes), jnp.int32)),
        in_specs=[pl.BlockSpec(memory_space=pltpu.VMEM)] * 2,
        out_specs=(pl.BlockSpec(memory_space=pltpu.VMEM),) * 2,
        scratch_shapes=[
            pltpu.VMEM((n_k, rows, lanes), jnp.int32),
            pltpu.VMEM((n_k * cap, own_links.shape[0]), jnp.bfloat16),
            pltpu.VMEM((n_k, cap, width), jnp.bfloat16),
            pltpu.VMEM((n_k, cap, width), jnp.bfloat16),
            pltpu.SemaphoreType.DMA((n_path - 1,)),
            pltpu.SemaphoreType.DMA((n_path - 1,)),
            pltpu.SemaphoreType.DMA((n_path - 1,)),
            pltpu.SemaphoreType.DMA((n_path - 1,)),
        ],
        compiler_params=pltpu.CompilerParams(collective_id=0, has_side_effects=True),
    )(req, own_links)


def _message_kernel(n_grp, n_path, out_ref, term_ref, inc_ref, grad_ref,
                    inbuf, recv1, recv2, mid, msend, mrecv, send1, got1, send2, got2, greet=True):
    g = lax.axis_index("grp")
    p = lax.axis_index("path")
    if greet:
        _greet(pltpu.get_barrier_semaphore(), g, p, n_grp, n_path, True)
    start_msg, finish_msg = _ring_copies(out_ref, inbuf, msend, mrecv, g, p, n_path, 1)

    def path_copy(k, q):
        return pltpu.make_async_remote_copy(
            src_ref=term_ref.at[q], dst_ref=recv1.at[k - 1], send_sem=send1.at[k - 1],
            recv_sem=got1.at[k - 1], device_id=(g, q), device_id_type=MESH)

    def start1(k, c):
        path_copy(k, lax.rem(p + k, n_path)).start()
        return c

    def finish1(k, c):
        copy = path_copy(k, lax.rem(p + k, n_path))
        copy.wait_send()
        copy.wait_recv()
        return c

    lax.fori_loop(1, n_path, start1, 0)
    lax.fori_loop(1, n_path, start_msg, 0)
    inbuf[0] = out_ref[0]
    lax.fori_loop(1, n_path, finish1, 0)
    mid[...] = term_ref[p] + jnp.sum(recv1[...], axis=0)

    def grp_copy(k, h):
        return pltpu.make_async_remote_copy(
            src_ref=mid, dst_ref=recv2.at[k - 1], send_sem=send2.at[k - 1],
            recv_sem=got2.at[k - 1], device_id=(h, p), device_id_type=MESH)

    def start2(k, c):
        grp_copy(k, lax.rem(g + k, n_grp)).start()
        return c

    def finish2(k, c):
        copy = grp_copy(k, lax.rem(g + k, n_grp))
        copy.wait_send()
        copy.wait_recv()
        return c

    lax.fori_loop(1, n_grp, start2, 0)
    lax.fori_loop(1, n_path, finish_msg, 0)
    inc_ref[...] = inbuf[...]
    lax.fori_loop(1, n_grp, finish2, 0)
    grad_ref[...] = mid[...] + jnp.sum(recv2[...], axis=0)


def exchange_messages(outgoing, term, n_grp, n_path):
    n_k, cap, width = outgoing.shape
    _, rows, gwidth = term.shape
    return pl.pallas_call(
        lambda *refs: _message_kernel(n_grp, n_path, *refs),
        out_shape=(jax.ShapeDtypeStruct((n_k, cap, width), jnp.bfloat16),
                   jax.ShapeDtypeStruct((rows, gwidth), jnp.float32)),
        in_specs=[pl.BlockSpec(memory_space=pltpu.VMEM)] * 2,
        out_specs=(pl.BlockSpec(memory_space=pltpu.VMEM),) * 2,
        scratch_shapes=[
            pltpu.VMEM((n_k, cap, width), jnp.bfloat16),
            pltpu.VMEM((n_path - 1, rows, gwidth), jnp.float32),
            pltpu.VMEM((n_grp - 1, rows, gwidth), jnp.float32),
            pltpu.VMEM((rows, gwidth), jnp.float32),
            pltpu.SemaphoreType.DMA((n_path - 1,)),
            pltpu.SemaphoreType.DMA((n_path - 1,)),
            pltpu.SemaphoreType.DMA((n_path - 1,)),
            pltpu.SemaphoreType.DMA((n_path - 1,)),
            pltpu.SemaphoreType.DMA((n_grp - 1,)),
            pltpu.SemaphoreType.DMA((n_grp - 1,)),
        ],
        compiler_params=pltpu.CompilerParams(collective_id=1, has_side_effects=True),
    )(outgoing, term)


def _hop_kernel(hops, dcol_ref, got_ref, w_in_ref, w_hid_ref, state_ref, live_ref, drow_ref, cot_t_ref,
                final_ref, out_ref, term_ref, proj, msgs):
    bf16, f32 = jnp.bfloat16, jnp.float32
    width = got_ref.shape[-1]
    got = got_ref[...].reshape(-1, width)
    entries, slots = dcol_ref.shape[1], got.shape[0]
    dcol = jnp.transpose(dcol_ref[...])[:, 0:1]
    route_t = (dcol == lax.broadcasted_iota(jnp.int32, (1, slots), 1)).astype(bf16)
    fetched = jnp.dot(route_t, got, preferred_element_type=f32).astype(bf16)
    proj[...] = jnp.dot(fetched, w_in_ref[...], preferred_element_type=f32)
    carried = state_ref[...].astype(f32)
    n, width = carried.shape
    for h in range(hops):
        p_h = proj[h * n : (h + 1) * n, :]
        renewed = gated_update(p_h, carried, w_hid_ref[...])
        carried = jnp.where(live_ref[:, h : h + 1] > 0, renewed, carried)
        msgs[h * n : (h + 1) * n, :] = carried.astype(bf16)
    final = carried.astype(bf16)
    final_ref[...] = final
    route = (lax.broadcasted_iota(jnp.int32, (slots, 1), 0) == drow_ref[...]).astype(bf16)
    out_ref[...] = jnp.dot(route, msgs[...], preferred_element_type=f32).astype(bf16).reshape(out_ref.shape)
    cot_t = jnp.transpose(cot_t_ref[...].astype(f32)).astype(bf16)
    term = jnp.dot(cot_t, final, preferred_element_type=f32)
    share = term_ref.shape[1]
    for q in range(term_ref.shape[0]):
        term_ref[q] = term[q * share : (q + 1) * share, :]


def run_hops(dcol, got, w_path_in, w_path_hid, state, live, drow, cot_t, n_path):
    entries = dcol.shape[1]
    slots = got.shape[0]
    n, width = state.shape
    hops = entries // n
    return pl.pallas_call(
        lambda *refs: _hop_kernel(hops, *refs),
        out_shape=(jax.ShapeDtypeStruct((n, width), jnp.bfloat16),
                   jax.ShapeDtypeStruct((slots, width), jnp.bfloat16),
                   jax.ShapeDtypeStruct((n_path, cot_t.shape[1] // n_path, width), jnp.float32)),
        in_specs=[pl.BlockSpec(memory_space=pltpu.VMEM)] * 8,
        out_specs=(pl.BlockSpec(memory_space=pltpu.VMEM),) * 3,
        scratch_shapes=[
            pltpu.VMEM((entries, w_path_in.shape[1]), jnp.float32),
            pltpu.VMEM((entries, width), jnp.bfloat16),
        ],
    )(dcol, got, w_path_in, w_path_hid, state, live, drow, cot_t)


def _all_kernel(n_grp, n_path, req_ref, links_ref, dcol_ref, w_in_ref, w_hid_ref, state_ref, live_ref,
                drow_ref, cot_ref, ids_ref, final_ref, inc_ref, grad_ref,
                reqin, want, served, gotbuf, gotv, rsend, rrecv, asend, arecv,
                proj, msgs, outbuf, termbuf,
                inbuf, recv1, recv2, mid, msend, mrecv, send1, got1, send2, got2):
    g = lax.axis_index("grp")
    p = lax.axis_index("path")
    _greet(pltpu.get_barrier_semaphore(), g, p, n_grp, n_path, True)
    _fetch_kernel(n_grp, n_path, req_ref, links_ref, gotv, ids_ref,
                  reqin, want, served, gotbuf, rsend, rrecv, asend, arecv, greet=False)
    hops = dcol_ref.shape[1] // state_ref.shape[0]
    _hop_kernel(hops, dcol_ref, gotv, w_in_ref, w_hid_ref, state_ref, live_ref, drow_ref, cot_ref,
                final_ref, outbuf, termbuf, proj, msgs)
    _message_kernel(n_grp, n_path, outbuf, termbuf, inc_ref, grad_ref,
                    inbuf, recv1, recv2, mid, msend, mrecv, send1, got1, send2, got2, greet=False)


def run_all(req, own_links, drow8, w_path_in, w_path_hid, state, live, drow1, cot, cap, n_grp, n_path):
    n_k, rows, lanes = req.shape
    link_dev, width = own_links.shape
    entries = drow8.shape[1]
    n = state.shape[0]
    share = cot.shape[1] // n_path
    vmem = pltpu.VMEM
    dma = pltpu.SemaphoreType.DMA
    return pl.pallas_call(
        lambda *refs: _all_kernel(n_grp, n_path, *refs),
        out_shape=(jax.ShapeDtypeStruct((n_k, rows, lanes), jnp.int32),
                   jax.ShapeDtypeStruct((n, width), jnp.bfloat16),
                   jax.ShapeDtypeStruct((n_k, cap, width), jnp.bfloat16),
                   jax.ShapeDtypeStruct((share, width), jnp.float32)),
        in_specs=[pl.BlockSpec(memory_space=vmem)] * 9,
        out_specs=(pl.BlockSpec(memory_space=vmem),) * 4,
        scratch_shapes=[
            vmem((n_k, rows, lanes), jnp.int32),
            vmem((n_k * cap, link_dev), jnp.bfloat16),
            vmem((n_k, cap, width), jnp.bfloat16),
            vmem((n_k, cap, width), jnp.bfloat16),
            vmem((n_k, cap, width), jnp.bfloat16),
            dma((n_path - 1,)), dma((n_path - 1,)), dma((n_path - 1,)), dma((n_path - 1,)),
            vmem((entries, w_path_in.shape[1]), jnp.float32),
            vmem((entries, width), jnp.bfloat16),
            vmem((n_k, cap, width), jnp.bfloat16),
            vmem((n_path, share, width), jnp.float32),
            vmem((n_k, cap, width), jnp.bfloat16),
            vmem((n_path - 1, share, width), jnp.float32),
            vmem((n_grp - 1, share, width), jnp.float32),
            vmem((share, width), jnp.float32),
            dma((n_path - 1,)), dma((n_path - 1,)), dma((n_path - 1,)), dma((n_path - 1,)),
            dma((n_grp - 1,)), dma((n_grp - 1,)),
        ],
        compiler_params=pltpu.CompilerParams(collective_id=0, has_side_effects=True),
    )(req, own_links, drow8, w_path_in, w_path_hid, state, live, drow1, cot)


def shards(
    link_state, path_state, path_links, w_path_in, w_path_hid, w_link_in, w_link_hid, cotangent
):
    bf16, f32 = jnp.bfloat16, jnp.float32
    own_links = link_state[0]
    link_dev, width = own_links.shape
    n_grp = lax.axis_size("grp")
    peer_count = lax.axis_size("path")
    me = lax.axis_index("path")
    path_count, hop_count = path_links.shape
    entries = path_count * hop_count
    capacity = entries // peer_count
    slots = peer_count * capacity
    flat_ids = path_links.reshape(-1)
    is_live = flat_ids >= 0
    owner_id = jnp.where(is_live, flat_ids // link_dev, peer_count)
    local_id = jnp.where(is_live, flat_ids % link_dev, 0)
    marks = (owner_id[:, None] == jnp.arange(peer_count)[None, :]).astype(bf16)
    order = jnp.arange(entries)
    earlier = (order[None, :] < order[:, None]).astype(bf16)
    before = jnp.dot(earlier, marks, preferred_element_type=f32)
    slot_id = jnp.sum(before * marks.astype(f32), axis=1).astype(jnp.int32)
    offset = lax.rem(owner_id - me + peer_count, peer_count)
    dest = jnp.where(is_live, offset * capacity + slot_id, -1)
    dest = dest.reshape(path_count, hop_count).T.reshape(-1)
    local_id = local_id.reshape(path_count, hop_count).T.reshape(-1)
    slot_ids = jnp.arange(slots)
    route = dest[None, :] == slot_ids[:, None]
    requests = jnp.sum(jnp.where(route, local_id[None, :] + 1, 0), axis=1) - 1
    req = jnp.full((peer_count, 8, 128), -1, jnp.int32)
    req = lax.dynamic_update_slice(req, requests.reshape(peer_count, 1, capacity), (0, 0, 0))
    live_grid = is_live.reshape(path_count, hop_count).astype(jnp.int32)
    drow = jnp.broadcast_to(dest[None, :], (8, entries))
    req_ids, path_final, incoming, read_grad = run_all(
        req, own_links, drow, w_path_in, w_path_hid, path_state[0], live_grid, drow[0:1],
        cotangent[0], capacity, n_grp, peer_count)
    received = req_ids[:, 0, :capacity].reshape(-1)
    want = (received[:, None] == jnp.arange(link_dev)[None, :]).astype(bf16)
    link_sum = lax.dot_general(
        want, incoming.reshape(slots, width), (((0,), (0,)), ((), ())), preferred_element_type=f32
    )
    link_proj = jnp.dot(link_sum.astype(bf16), w_link_in, preferred_element_type=f32)
    link_next = gated_update(link_proj, own_links.astype(f32), w_link_hid).astype(bf16)
    return (link_next[None], path_final[None], read_grad)


def solution(mesh):
    return jax.shard_map(
        shards,
        mesh=mesh,
        in_specs=(
            P("grp", "path", None),
            P("grp", "path", None),
            P("path", None),
            P(),
            P(),
            P(),
            P(),
            P("grp", "path", None),
        ),
        out_specs=(P("grp", "path", None), P("grp", "path", None), P("path", None)),
        check_vma=False,
    )
```

```python
import jax
import jax.numpy as jnp
from jax import lax
from jax.experimental import pallas as pl
from jax.experimental.pallas import tpu as pltpu
from jax.sharding import PartitionSpec as P

MESH = pl.DeviceIdType.MESH


def gated_update(projected, carried, w_hidden):
    width = carried.shape[1]
    recur = jnp.dot(carried.astype(jnp.bfloat16), w_hidden, preferred_element_type=jnp.float32)
    reset = jax.nn.sigmoid(projected[:, :width] + recur[:, :width])
    update = jax.nn.sigmoid(projected[:, width : 2 * width] + recur[:, width : 2 * width])
    candidate = jnp.tanh(projected[:, 2 * width :] + reset * recur[:, 2 * width :])
    return (1.0 - update) * candidate + update * carried


def _greet(barrier, g, p, n_grp, n_path, with_grp):
    def greet_path(k, c):
        pl.semaphore_signal(barrier, inc=1, device_id=(g, lax.rem(p + k, n_path)), device_id_type=MESH)
        return c

    def greet_grp(k, c):
        pl.semaphore_signal(barrier, inc=1, device_id=(lax.rem(g + k, n_grp), p), device_id_type=MESH)
        return c

    lax.fori_loop(1, n_path, greet_path, 0)
    count = n_path - 1
    if with_grp:
        lax.fori_loop(1, n_grp, greet_grp, 0)
        count += n_grp - 1
    pl.semaphore_wait(barrier, count)


def _ring_copies(src, dst, send, recv, g, p, n_path, sign):
    def make(k):
        return pltpu.make_async_remote_copy(
            src_ref=src.at[k], dst_ref=dst.at[k], send_sem=send.at[k - 1], recv_sem=recv.at[k - 1],
            device_id=(g, lax.rem(p + sign * k + n_path, n_path)), device_id_type=MESH)

    def start(k, c):
        make(k).start()
        return c

    def finish(k, c):
        copy = make(k)
        copy.wait_send()
        copy.wait_recv()
        return c

    return start, finish


def _fetch_kernel(n_grp, n_path, req_ref, links_ref, got_ref, ids_ref,
                  reqin, want, served, gotbuf, rsend, rrecv, asend, arecv, greet=True, during=None):
    g = lax.axis_index("grp")
    p = lax.axis_index("path")
    if greet:
        _greet(pltpu.get_barrier_semaphore(), g, p, n_grp, n_path, False)
    start_req, finish_req = _ring_copies(req_ref, reqin, rsend, rrecv, g, p, n_path, 1)
    lax.fori_loop(1, n_path, start_req, 0)
    reqin[0] = req_ref[0]
    lax.fori_loop(1, n_path, finish_req, 0)
    n_k, cap = served.shape[0], served.shape[1]
    link_dev = links_ref.shape[0]
    ids_t = jnp.transpose(reqin[:, 0, :])
    lanes = lax.broadcasted_iota(jnp.int32, (1, link_dev), 1)
    for k in range(n_k):
        want[k * cap : (k + 1) * cap, :] = (ids_t[0:cap, k : k + 1] == lanes).astype(jnp.bfloat16)
    rows = jnp.dot(want[...], links_ref[...], preferred_element_type=jnp.float32).astype(jnp.bfloat16)
    served[...] = rows.reshape(served.shape)
    start_ans, finish_ans = _ring_copies(served, gotbuf, asend, arecv, g, p, n_path, -1)
    lax.fori_loop(1, n_path, start_ans, 0)
    gotbuf[0] = served[0]
    if ids_ref is not None:
        ids_ref[...] = reqin[...]
    if during is not None:
        during()
    lax.fori_loop(1, n_path, finish_ans, 0)
    got_ref[...] = gotbuf[...]


def fetch_rows(req, own_links, cap, n_grp, n_path):
    n_k, rows, lanes = req.shape
    width = own_links.shape[1]
    return pl.pallas_call(
        lambda *refs: _fetch_kernel(n_grp, n_path, *refs),
        out_shape=(jax.ShapeDtypeStruct((n_k, cap, width), jnp.bfloat16),
                   jax.ShapeDtypeStruct((n_k, rows, lanes), jnp.int32)),
        in_specs=[pl.BlockSpec(memory_space=pltpu.VMEM)] * 2,
        out_specs=(pl.BlockSpec(memory_space=pltpu.VMEM),) * 2,
        scratch_shapes=[
            pltpu.VMEM((n_k, rows, lanes), jnp.int32),
            pltpu.VMEM((n_k * cap, own_links.shape[0]), jnp.bfloat16),
            pltpu.VMEM((n_k, cap, width), jnp.bfloat16),
            pltpu.VMEM((n_k, cap, width), jnp.bfloat16),
            pltpu.SemaphoreType.DMA((n_path - 1,)),
            pltpu.SemaphoreType.DMA((n_path - 1,)),
            pltpu.SemaphoreType.DMA((n_path - 1,)),
            pltpu.SemaphoreType.DMA((n_path - 1,)),
        ],
        compiler_params=pltpu.CompilerParams(collective_id=0, has_side_effects=True),
    )(req, own_links)


def _message_kernel(n_grp, n_path, out_ref, term_ref, inc_ref, grad_ref,
                    inbuf, recv1, recv2, mid, msend, mrecv, send1, got1, send2, got2, greet=True,
                    after_msgs=None):
    g = lax.axis_index("grp")
    p = lax.axis_index("path")
    if greet:
        _greet(pltpu.get_barrier_semaphore(), g, p, n_grp, n_path, True)
    start_msg, finish_msg = _ring_copies(out_ref, inbuf, msend, mrecv, g, p, n_path, 1)

    def path_copy(k, q):
        return pltpu.make_async_remote_copy(
            src_ref=term_ref.at[q], dst_ref=recv1.at[k - 1], send_sem=send1.at[k - 1],
            recv_sem=got1.at[k - 1], device_id=(g, q), device_id_type=MESH)

    def start1(k, c):
        path_copy(k, lax.rem(p + k, n_path)).start()
        return c

    def finish1(k, c):
        copy = path_copy(k, lax.rem(p + k, n_path))
        copy.wait_send()
        copy.wait_recv()
        return c

    lax.fori_loop(1, n_path, start1, 0)
    lax.fori_loop(1, n_path, start_msg, 0)
    inbuf[0] = out_ref[0]
    lax.fori_loop(1, n_path, finish1, 0)
    mid[...] = term_ref[p] + jnp.sum(recv1[...], axis=0)

    def grp_copy(k, h):
        return pltpu.make_async_remote_copy(
            src_ref=mid, dst_ref=recv2.at[k - 1], send_sem=send2.at[k - 1],
            recv_sem=got2.at[k - 1], device_id=(h, p), device_id_type=MESH)

    def start2(k, c):
        grp_copy(k, lax.rem(g + k, n_grp)).start()
        return c

    def finish2(k, c):
        copy = grp_copy(k, lax.rem(g + k, n_grp))
        copy.wait_send()
        copy.wait_recv()
        return c

    lax.fori_loop(1, n_grp, start2, 0)
    lax.fori_loop(1, n_path, finish_msg, 0)
    if inc_ref is not None:
        inc_ref[...] = inbuf[...]
    if after_msgs is not None:
        after_msgs()
    lax.fori_loop(1, n_grp, finish2, 0)
    grad_ref[...] = mid[...] + jnp.sum(recv2[...], axis=0)


def exchange_messages(outgoing, term, n_grp, n_path):
    n_k, cap, width = outgoing.shape
    _, rows, gwidth = term.shape
    return pl.pallas_call(
        lambda *refs: _message_kernel(n_grp, n_path, *refs),
        out_shape=(jax.ShapeDtypeStruct((n_k, cap, width), jnp.bfloat16),
                   jax.ShapeDtypeStruct((rows, gwidth), jnp.float32)),
        in_specs=[pl.BlockSpec(memory_space=pltpu.VMEM)] * 2,
        out_specs=(pl.BlockSpec(memory_space=pltpu.VMEM),) * 2,
        scratch_shapes=[
            pltpu.VMEM((n_k, cap, width), jnp.bfloat16),
            pltpu.VMEM((n_path - 1, rows, gwidth), jnp.float32),
            pltpu.VMEM((n_grp - 1, rows, gwidth), jnp.float32),
            pltpu.VMEM((rows, gwidth), jnp.float32),
            pltpu.SemaphoreType.DMA((n_path - 1,)),
            pltpu.SemaphoreType.DMA((n_path - 1,)),
            pltpu.SemaphoreType.DMA((n_path - 1,)),
            pltpu.SemaphoreType.DMA((n_path - 1,)),
            pltpu.SemaphoreType.DMA((n_grp - 1,)),
            pltpu.SemaphoreType.DMA((n_grp - 1,)),
        ],
        compiler_params=pltpu.CompilerParams(collective_id=1, has_side_effects=True),
    )(outgoing, term)


def _hop_kernel(hops, dcol_ref, got_ref, w_in_ref, w_hid_ref, state_ref, live_ref, drow_ref, cot_t_ref,
                final_ref, out_ref, term_ref, proj, msgs):
    bf16, f32 = jnp.bfloat16, jnp.float32
    width = got_ref.shape[-1]
    got = got_ref[...].reshape(-1, width)
    entries, slots = dcol_ref.shape[1], got.shape[0]
    dcol = jnp.transpose(dcol_ref[...])[:, 0:1]
    route_t = (dcol == lax.broadcasted_iota(jnp.int32, (1, slots), 1)).astype(bf16)
    fetched = jnp.dot(route_t, got, preferred_element_type=f32).astype(bf16)
    proj[...] = jnp.dot(fetched, w_in_ref[...], preferred_element_type=f32)
    carried = state_ref[...].astype(f32)
    n, width = carried.shape
    for h in range(hops):
        p_h = proj[h * n : (h + 1) * n, :]
        renewed = gated_update(p_h, carried, w_hid_ref[...])
        carried = jnp.where(live_ref[:, h : h + 1] > 0, renewed, carried)
        msgs[h * n : (h + 1) * n, :] = carried.astype(bf16)
    final = carried.astype(bf16)
    final_ref[...] = final
    route = (lax.broadcasted_iota(jnp.int32, (slots, 1), 0) == drow_ref[...]).astype(bf16)
    out_ref[...] = jnp.dot(route, msgs[...], preferred_element_type=f32).astype(bf16).reshape(out_ref.shape)
    cot_t = jnp.transpose(cot_t_ref[...].astype(f32)).astype(bf16)
    term = jnp.dot(cot_t, final, preferred_element_type=f32)
    share = term_ref.shape[1]
    for q in range(term_ref.shape[0]):
        term_ref[q] = term[q * share : (q + 1) * share, :]


def run_hops(dcol, got, w_path_in, w_path_hid, state, live, drow, cot_t, n_path):
    entries = dcol.shape[1]
    slots = got.shape[0]
    n, width = state.shape
    hops = entries // n
    return pl.pallas_call(
        lambda *refs: _hop_kernel(hops, *refs),
        out_shape=(jax.ShapeDtypeStruct((n, width), jnp.bfloat16),
                   jax.ShapeDtypeStruct((slots, width), jnp.bfloat16),
                   jax.ShapeDtypeStruct((n_path, cot_t.shape[1] // n_path, width), jnp.float32)),
        in_specs=[pl.BlockSpec(memory_space=pltpu.VMEM)] * 8,
        out_specs=(pl.BlockSpec(memory_space=pltpu.VMEM),) * 3,
        scratch_shapes=[
            pltpu.VMEM((entries, w_path_in.shape[1]), jnp.float32),
            pltpu.VMEM((entries, width), jnp.bfloat16),
        ],
    )(dcol, got, w_path_in, w_path_hid, state, live, drow, cot_t)


def _all_kernel(n_grp, n_path, req_ref, links_ref, dcol_ref, w_in_ref, w_hid_ref, state_ref, live_ref,
                drow_ref, cot_ref, w_lin_ref, w_lhid_ref, final_ref, next_ref, grad_ref,
                reqin, want, served, gotbuf, gotv, rsend, rrecv, asend, arecv,
                proj, msgs, outbuf, termbuf, recur_buf,
                inbuf, recv1, recv2, mid, msend, mrecv, send1, got1, send2, got2):
    f32 = jnp.float32
    g = lax.axis_index("grp")
    p = lax.axis_index("path")
    _greet(pltpu.get_barrier_semaphore(), g, p, n_grp, n_path, True)

    def link_recur():
        recur_buf[...] = jnp.dot(links_ref[...], w_lhid_ref[...], preferred_element_type=f32)

    def link_update():
        width = links_ref.shape[1]
        incoming = inbuf[...].reshape(-1, width)
        link_sum = lax.dot_general(want[...], incoming, (((0,), (0,)), ((), ())), preferred_element_type=f32)
        link_proj = jnp.dot(link_sum.astype(jnp.bfloat16), w_lin_ref[...], preferred_element_type=f32)
        recur = recur_buf[...]
        own = links_ref[...].astype(f32)
        reset = jax.nn.sigmoid(link_proj[:, :width] + recur[:, :width])
        update = jax.nn.sigmoid(link_proj[:, width : 2 * width] + recur[:, width : 2 * width])
        candidate = jnp.tanh(link_proj[:, 2 * width :] + reset * recur[:, 2 * width :])
        next_ref[...] = ((1.0 - update) * candidate + update * own).astype(next_ref.dtype)

    _fetch_kernel(n_grp, n_path, req_ref, links_ref, gotv, None,
                  reqin, want, served, gotbuf, rsend, rrecv, asend, arecv, greet=False, during=link_recur)
    hops = dcol_ref.shape[1] // state_ref.shape[0]
    _hop_kernel(hops, dcol_ref, gotv, w_in_ref, w_hid_ref, state_ref, live_ref, drow_ref, cot_ref,
                final_ref, outbuf, termbuf, proj, msgs)
    _message_kernel(n_grp, n_path, outbuf, termbuf, None, grad_ref,
                    inbuf, recv1, recv2, mid, msend, mrecv, send1, got1, send2, got2, greet=False,
                    after_msgs=link_update)


def run_all(req, own_links, drow8, w_path_in, w_path_hid, state, live, drow1, cot, w_link_in, w_link_hid,
            cap, n_grp, n_path):
    n_k, rows, lanes = req.shape
    link_dev, width = own_links.shape
    entries = drow8.shape[1]
    n = state.shape[0]
    share = cot.shape[1] // n_path
    vmem = pltpu.VMEM
    dma = pltpu.SemaphoreType.DMA
    return pl.pallas_call(
        lambda *refs: _all_kernel(n_grp, n_path, *refs),
        out_shape=(jax.ShapeDtypeStruct((n, width), jnp.bfloat16),
                   jax.ShapeDtypeStruct((link_dev, width), jnp.bfloat16),
                   jax.ShapeDtypeStruct((share, width), jnp.float32)),
        in_specs=[pl.BlockSpec(memory_space=vmem)] * 11,
        out_specs=(pl.BlockSpec(memory_space=vmem),) * 3,
        scratch_shapes=[
            vmem((n_k, rows, lanes), jnp.int32),
            vmem((n_k * cap, link_dev), jnp.bfloat16),
            vmem((n_k, cap, width), jnp.bfloat16),
            vmem((n_k, cap, width), jnp.bfloat16),
            vmem((n_k, cap, width), jnp.bfloat16),
            dma((n_path - 1,)), dma((n_path - 1,)), dma((n_path - 1,)), dma((n_path - 1,)),
            vmem((entries, w_path_in.shape[1]), jnp.float32),
            vmem((entries, width), jnp.bfloat16),
            vmem((n_k, cap, width), jnp.bfloat16),
            vmem((n_path, share, width), jnp.float32),
            vmem((link_dev, w_link_hid.shape[1]), jnp.float32),
            vmem((n_k, cap, width), jnp.bfloat16),
            vmem((n_path - 1, share, width), jnp.float32),
            vmem((n_grp - 1, share, width), jnp.float32),
            vmem((share, width), jnp.float32),
            dma((n_path - 1,)), dma((n_path - 1,)), dma((n_path - 1,)), dma((n_path - 1,)),
            dma((n_grp - 1,)), dma((n_grp - 1,)),
        ],
        compiler_params=pltpu.CompilerParams(collective_id=0, has_side_effects=True),
    )(req, own_links, drow8, w_path_in, w_path_hid, state, live, drow1, cot, w_link_in, w_link_hid)


def shards(
    link_state, path_state, path_links, w_path_in, w_path_hid, w_link_in, w_link_hid, cotangent
):
    bf16, f32 = jnp.bfloat16, jnp.float32
    own_links = link_state[0]
    link_dev, width = own_links.shape
    n_grp = lax.axis_size("grp")
    peer_count = lax.axis_size("path")
    me = lax.axis_index("path")
    path_count, hop_count = path_links.shape
    entries = path_count * hop_count
    capacity = entries // peer_count
    slots = peer_count * capacity
    flat_ids = path_links.reshape(-1)
    is_live = flat_ids >= 0
    owner_id = jnp.where(is_live, flat_ids // link_dev, peer_count)
    local_id = jnp.where(is_live, flat_ids % link_dev, 0)
    marks = (owner_id[:, None] == jnp.arange(peer_count)[None, :]).astype(bf16)
    order = jnp.arange(entries)
    earlier = (order[None, :] < order[:, None]).astype(bf16)
    before = jnp.dot(earlier, marks, preferred_element_type=f32)
    slot_id = jnp.sum(before * marks.astype(f32), axis=1).astype(jnp.int32)
    offset = lax.rem(owner_id - me + peer_count, peer_count)
    dest = jnp.where(is_live, offset * capacity + slot_id, -1)
    dest = dest.reshape(path_count, hop_count).T.reshape(-1)
    local_id = local_id.reshape(path_count, hop_count).T.reshape(-1)
    slot_ids = jnp.arange(slots)
    route = dest[None, :] == slot_ids[:, None]
    requests = jnp.sum(jnp.where(route, local_id[None, :] + 1, 0), axis=1) - 1
    req = jnp.full((peer_count, 8, 128), -1, jnp.int32)
    req = lax.dynamic_update_slice(req, requests.reshape(peer_count, 1, capacity), (0, 0, 0))
    live_grid = is_live.reshape(path_count, hop_count).astype(jnp.int32)
    drow = jnp.broadcast_to(dest[None, :], (8, entries))
    path_final, link_next, read_grad = run_all(
        req, own_links, drow, w_path_in, w_path_hid, path_state[0], live_grid, drow[0:1],
        cotangent[0], w_link_in, w_link_hid, capacity, n_grp, peer_count)
    return (link_next[None], path_final[None], read_grad)


def solution(mesh):
    return jax.shard_map(
        shards,
        mesh=mesh,
        in_specs=(
            P("grp", "path", None),
            P("grp", "path", None),
            P("path", None),
            P(),
            P(),
            P(),
            P(),
            P("grp", "path", None),
        ),
        out_specs=(P("grp", "path", None), P("grp", "path", None), P("path", None)),
        check_vma=False,
    )
```

```python
import jax
import jax.numpy as jnp
from jax import lax
from jax.experimental import pallas as pl
from jax.experimental.pallas import tpu as pltpu
from jax.sharding import PartitionSpec as P

MESH = pl.DeviceIdType.MESH


def gated_update(projected, carried, w_hidden):
    width = carried.shape[1]
    recur = jnp.dot(carried.astype(jnp.bfloat16), w_hidden, preferred_element_type=jnp.float32)
    reset = jax.nn.sigmoid(projected[:, :width] + recur[:, :width])
    update = jax.nn.sigmoid(projected[:, width : 2 * width] + recur[:, width : 2 * width])
    candidate = jnp.tanh(projected[:, 2 * width :] + reset * recur[:, 2 * width :])
    return (1.0 - update) * candidate + update * carried


def _greet(barrier, g, p, n_grp, n_path, with_grp):
    def greet_path(k, c):
        pl.semaphore_signal(barrier, inc=1, device_id=(g, lax.rem(p + k, n_path)), device_id_type=MESH)
        return c

    def greet_grp(k, c):
        pl.semaphore_signal(barrier, inc=1, device_id=(lax.rem(g + k, n_grp), p), device_id_type=MESH)
        return c

    lax.fori_loop(1, n_path, greet_path, 0)
    count = n_path - 1
    if with_grp:
        lax.fori_loop(1, n_grp, greet_grp, 0)
        count += n_grp - 1
    pl.semaphore_wait(barrier, count)


def _ring_copies(src, dst, send, recv, g, p, n_path, sign):
    def make(k):
        return pltpu.make_async_remote_copy(
            src_ref=src.at[k], dst_ref=dst.at[k], send_sem=send.at[k - 1], recv_sem=recv.at[k - 1],
            device_id=(g, lax.rem(p + sign * k + n_path, n_path)), device_id_type=MESH)

    def start(k, c):
        make(k).start()
        return c

    def finish(k, c):
        copy = make(k)
        copy.wait_send()
        copy.wait_recv()
        return c

    return start, finish


def _fetch_kernel(n_grp, n_path, req_ref, links_ref, got_ref, ids_ref,
                  reqin, want, served, gotbuf, rsend, rrecv, asend, arecv, greet=True, during=None):
    g = lax.axis_index("grp")
    p = lax.axis_index("path")
    if greet:
        _greet(pltpu.get_barrier_semaphore(), g, p, n_grp, n_path, False)
    start_req, finish_req = _ring_copies(req_ref, reqin, rsend, rrecv, g, p, n_path, 1)
    lax.fori_loop(1, n_path, start_req, 0)
    reqin[0] = req_ref[0]
    lax.fori_loop(1, n_path, finish_req, 0)
    n_k, cap = served.shape[0], served.shape[1]
    link_dev = links_ref.shape[0]
    ids_t = jnp.transpose(reqin[:, 0, :])
    lanes = lax.broadcasted_iota(jnp.int32, (1, link_dev), 1)
    for k in range(n_k):
        want[k * cap : (k + 1) * cap, :] = (ids_t[0:cap, k : k + 1] == lanes).astype(jnp.bfloat16)
    rows = jnp.dot(want[...], links_ref[...], preferred_element_type=jnp.float32).astype(jnp.bfloat16)
    served[...] = rows.reshape(served.shape)
    start_ans, finish_ans = _ring_copies(served, gotbuf, asend, arecv, g, p, n_path, -1)
    lax.fori_loop(1, n_path, start_ans, 0)
    gotbuf[0] = served[0]
    if ids_ref is not None:
        ids_ref[...] = reqin[...]
    if during is not None:
        during()
    lax.fori_loop(1, n_path, finish_ans, 0)
    got_ref[...] = gotbuf[...]


def fetch_rows(req, own_links, cap, n_grp, n_path):
    n_k, rows, lanes = req.shape
    width = own_links.shape[1]
    return pl.pallas_call(
        lambda *refs: _fetch_kernel(n_grp, n_path, *refs),
        out_shape=(jax.ShapeDtypeStruct((n_k, cap, width), jnp.bfloat16),
                   jax.ShapeDtypeStruct((n_k, rows, lanes), jnp.int32)),
        in_specs=[pl.BlockSpec(memory_space=pltpu.VMEM)] * 2,
        out_specs=(pl.BlockSpec(memory_space=pltpu.VMEM),) * 2,
        scratch_shapes=[
            pltpu.VMEM((n_k, rows, lanes), jnp.int32),
            pltpu.VMEM((n_k * cap, own_links.shape[0]), jnp.bfloat16),
            pltpu.VMEM((n_k, cap, width), jnp.bfloat16),
            pltpu.VMEM((n_k, cap, width), jnp.bfloat16),
            pltpu.SemaphoreType.DMA((n_path - 1,)),
            pltpu.SemaphoreType.DMA((n_path - 1,)),
            pltpu.SemaphoreType.DMA((n_path - 1,)),
            pltpu.SemaphoreType.DMA((n_path - 1,)),
        ],
        compiler_params=pltpu.CompilerParams(collective_id=0, has_side_effects=True),
    )(req, own_links)


def _message_kernel(n_grp, n_path, out_ref, term_ref, inc_ref, grad_ref,
                    inbuf, recv1, recv2, mid, msend, mrecv, send1, got1, send2, got2, greet=True,
                    after_msgs=None):
    g = lax.axis_index("grp")
    p = lax.axis_index("path")
    if greet:
        _greet(pltpu.get_barrier_semaphore(), g, p, n_grp, n_path, True)
    start_msg, finish_msg = _ring_copies(out_ref, inbuf, msend, mrecv, g, p, n_path, 1)

    def path_copy(k, q):
        return pltpu.make_async_remote_copy(
            src_ref=term_ref.at[q], dst_ref=recv1.at[k - 1], send_sem=send1.at[k - 1],
            recv_sem=got1.at[k - 1], device_id=(g, q), device_id_type=MESH)

    def start1(k, c):
        path_copy(k, lax.rem(p + k, n_path)).start()
        return c

    def finish1(k, c):
        copy = path_copy(k, lax.rem(p + k, n_path))
        copy.wait_send()
        copy.wait_recv()
        return c

    lax.fori_loop(1, n_path, start1, 0)
    lax.fori_loop(1, n_path, start_msg, 0)
    inbuf[0] = out_ref[0]
    lax.fori_loop(1, n_path, finish1, 0)
    mid[...] = term_ref[p] + jnp.sum(recv1[...], axis=0)

    def grp_copy(k, h):
        return pltpu.make_async_remote_copy(
            src_ref=mid, dst_ref=recv2.at[k - 1], send_sem=send2.at[k - 1],
            recv_sem=got2.at[k - 1], device_id=(h, p), device_id_type=MESH)

    def start2(k, c):
        grp_copy(k, lax.rem(g + k, n_grp)).start()
        return c

    def finish2(k, c):
        copy = grp_copy(k, lax.rem(g + k, n_grp))
        copy.wait_send()
        copy.wait_recv()
        return c

    lax.fori_loop(1, n_grp, start2, 0)
    lax.fori_loop(1, n_path, finish_msg, 0)
    if inc_ref is not None:
        inc_ref[...] = inbuf[...]
    if after_msgs is not None:
        after_msgs()
    lax.fori_loop(1, n_grp, finish2, 0)
    grad_ref[...] = mid[...] + jnp.sum(recv2[...], axis=0)


def exchange_messages(outgoing, term, n_grp, n_path):
    n_k, cap, width = outgoing.shape
    _, rows, gwidth = term.shape
    return pl.pallas_call(
        lambda *refs: _message_kernel(n_grp, n_path, *refs),
        out_shape=(jax.ShapeDtypeStruct((n_k, cap, width), jnp.bfloat16),
                   jax.ShapeDtypeStruct((rows, gwidth), jnp.float32)),
        in_specs=[pl.BlockSpec(memory_space=pltpu.VMEM)] * 2,
        out_specs=(pl.BlockSpec(memory_space=pltpu.VMEM),) * 2,
        scratch_shapes=[
            pltpu.VMEM((n_k, cap, width), jnp.bfloat16),
            pltpu.VMEM((n_path - 1, rows, gwidth), jnp.float32),
            pltpu.VMEM((n_grp - 1, rows, gwidth), jnp.float32),
            pltpu.VMEM((rows, gwidth), jnp.float32),
            pltpu.SemaphoreType.DMA((n_path - 1,)),
            pltpu.SemaphoreType.DMA((n_path - 1,)),
            pltpu.SemaphoreType.DMA((n_path - 1,)),
            pltpu.SemaphoreType.DMA((n_path - 1,)),
            pltpu.SemaphoreType.DMA((n_grp - 1,)),
            pltpu.SemaphoreType.DMA((n_grp - 1,)),
        ],
        compiler_params=pltpu.CompilerParams(collective_id=1, has_side_effects=True),
    )(outgoing, term)


def _route_mats(drow, slots):
    dcol = jnp.transpose(jnp.broadcast_to(drow, (8, drow.shape[1])))[:, 0:1]
    route_t = (dcol == lax.broadcasted_iota(jnp.int32, (1, slots), 1)).astype(jnp.bfloat16)
    route = (lax.broadcasted_iota(jnp.int32, (slots, 1), 0) == drow).astype(jnp.bfloat16)
    return route_t, route


def _hop_kernel(hops, route_t_ref, got_ref, w_in_ref, w_hid_ref, state_ref, live_ref, route_ref, cot_t_ref,
                final_ref, out_ref, term_ref, proj, msgs):
    bf16, f32 = jnp.bfloat16, jnp.float32
    width = got_ref.shape[-1]
    got = got_ref[...].reshape(-1, width)
    fetched = jnp.dot(route_t_ref[...], got, preferred_element_type=f32).astype(bf16)
    proj[...] = jnp.dot(fetched, w_in_ref[...], preferred_element_type=f32)
    carried = state_ref[...].astype(f32)
    n, width = carried.shape
    for h in range(hops):
        p_h = proj[h * n : (h + 1) * n, :]
        renewed = gated_update(p_h, carried, w_hid_ref[...])
        carried = jnp.where(live_ref[:, h : h + 1] >= 0, renewed, carried)
        msgs[h * n : (h + 1) * n, :] = carried.astype(bf16)
    final = carried.astype(bf16)
    final_ref[...] = final
    out_ref[...] = jnp.dot(route_ref[...], msgs[...], preferred_element_type=f32).astype(bf16).reshape(out_ref.shape)
    cot_t = jnp.transpose(cot_t_ref[...].astype(f32)).astype(bf16)
    term = jnp.dot(cot_t, final, preferred_element_type=f32)
    share = term_ref.shape[1]
    for q in range(term_ref.shape[0]):
        term_ref[q] = term[q * share : (q + 1) * share, :]


def run_hops(dcol, got, w_path_in, w_path_hid, state, live, drow, cot_t, n_path):
    entries = dcol.shape[1]
    slots = got.shape[0]
    n, width = state.shape
    hops = entries // n
    return pl.pallas_call(
        lambda *refs: _hop_kernel(hops, *refs),
        out_shape=(jax.ShapeDtypeStruct((n, width), jnp.bfloat16),
                   jax.ShapeDtypeStruct((slots, width), jnp.bfloat16),
                   jax.ShapeDtypeStruct((n_path, cot_t.shape[1] // n_path, width), jnp.float32)),
        in_specs=[pl.BlockSpec(memory_space=pltpu.VMEM)] * 8,
        out_specs=(pl.BlockSpec(memory_space=pltpu.VMEM),) * 3,
        scratch_shapes=[
            pltpu.VMEM((entries, w_path_in.shape[1]), jnp.float32),
            pltpu.VMEM((entries, width), jnp.bfloat16),
        ],
    )(dcol, got, w_path_in, w_path_hid, state, live, drow, cot_t)


def _all_kernel(n_grp, n_path, req_ref, links_ref, w_in_ref, w_hid_ref, state_ref, live_ref,
                drow_ref, cot_ref, w_lin_ref, w_lhid_ref, final_ref, next_ref, grad_ref,
                reqin, want, served, gotbuf, gotv, rsend, rrecv, asend, arecv,
                proj, msgs, outbuf, termbuf, recur_buf, route_t_buf, route_buf,
                inbuf, recv1, recv2, mid, msend, mrecv, send1, got1, send2, got2):
    f32 = jnp.float32
    g = lax.axis_index("grp")
    p = lax.axis_index("path")
    _greet(pltpu.get_barrier_semaphore(), g, p, n_grp, n_path, True)

    def link_recur():
        recur_buf[...] = jnp.dot(links_ref[...], w_lhid_ref[...], preferred_element_type=f32)
        route_t, route = _route_mats(drow_ref[...], route_buf.shape[0])
        route_t_buf[...] = route_t
        route_buf[...] = route

    def link_update():
        width = links_ref.shape[1]
        incoming = inbuf[...].reshape(-1, width)
        link_sum = lax.dot_general(want[...], incoming, (((0,), (0,)), ((), ())), preferred_element_type=f32)
        link_proj = jnp.dot(link_sum.astype(jnp.bfloat16), w_lin_ref[...], preferred_element_type=f32)
        recur = recur_buf[...]
        own = links_ref[...].astype(f32)
        reset = jax.nn.sigmoid(link_proj[:, :width] + recur[:, :width])
        update = jax.nn.sigmoid(link_proj[:, width : 2 * width] + recur[:, width : 2 * width])
        candidate = jnp.tanh(link_proj[:, 2 * width :] + reset * recur[:, 2 * width :])
        next_ref[...] = ((1.0 - update) * candidate + update * own).astype(next_ref.dtype)

    _fetch_kernel(n_grp, n_path, req_ref, links_ref, gotv, None,
                  reqin, want, served, gotbuf, rsend, rrecv, asend, arecv, greet=False, during=link_recur)
    hops = drow_ref.shape[1] // state_ref.shape[0]
    _hop_kernel(hops, route_t_buf, gotv, w_in_ref, w_hid_ref, state_ref, live_ref, route_buf, cot_ref,
                final_ref, outbuf, termbuf, proj, msgs)
    _message_kernel(n_grp, n_path, outbuf, termbuf, None, grad_ref,
                    inbuf, recv1, recv2, mid, msend, mrecv, send1, got1, send2, got2, greet=False,
                    after_msgs=link_update)


def run_all(req, own_links, w_path_in, w_path_hid, state, live, drow1, cot, w_link_in, w_link_hid,
            cap, n_grp, n_path):
    n_k, rows, lanes = req.shape
    link_dev, width = own_links.shape
    entries = drow1.shape[1]
    n = state.shape[0]
    share = cot.shape[1] // n_path
    vmem = pltpu.VMEM
    dma = pltpu.SemaphoreType.DMA
    return pl.pallas_call(
        lambda *refs: _all_kernel(n_grp, n_path, *refs),
        out_shape=(jax.ShapeDtypeStruct((n, width), jnp.bfloat16),
                   jax.ShapeDtypeStruct((link_dev, width), jnp.bfloat16),
                   jax.ShapeDtypeStruct((share, width), jnp.float32)),
        in_specs=[pl.BlockSpec(memory_space=vmem)] * 10,
        out_specs=(pl.BlockSpec(memory_space=vmem),) * 3,
        scratch_shapes=[
            vmem((n_k, rows, lanes), jnp.int32),
            vmem((n_k * cap, link_dev), jnp.bfloat16),
            vmem((n_k, cap, width), jnp.bfloat16),
            vmem((n_k, cap, width), jnp.bfloat16),
            vmem((n_k, cap, width), jnp.bfloat16),
            dma((n_path - 1,)), dma((n_path - 1,)), dma((n_path - 1,)), dma((n_path - 1,)),
            vmem((entries, w_path_in.shape[1]), jnp.float32),
            vmem((entries, width), jnp.bfloat16),
            vmem((n_k, cap, width), jnp.bfloat16),
            vmem((n_path, share, width), jnp.float32),
            vmem((link_dev, w_link_hid.shape[1]), jnp.float32),
            vmem((entries, n_k * cap), jnp.bfloat16),
            vmem((n_k * cap, entries), jnp.bfloat16),
            vmem((n_k, cap, width), jnp.bfloat16),
            vmem((n_path - 1, share, width), jnp.float32),
            vmem((n_grp - 1, share, width), jnp.float32),
            vmem((share, width), jnp.float32),
            dma((n_path - 1,)), dma((n_path - 1,)), dma((n_path - 1,)), dma((n_path - 1,)),
            dma((n_grp - 1,)), dma((n_grp - 1,)),
        ],
        compiler_params=pltpu.CompilerParams(collective_id=0, has_side_effects=True),
    )(req, own_links, w_path_in, w_path_hid, state, live, drow1, cot, w_link_in, w_link_hid)


def shards(
    link_state, path_state, path_links, w_path_in, w_path_hid, w_link_in, w_link_hid, cotangent
):
    bf16, f32 = jnp.bfloat16, jnp.float32
    own_links = link_state[0]
    link_dev, width = own_links.shape
    n_grp = lax.axis_size("grp")
    peer_count = lax.axis_size("path")
    me = lax.axis_index("path")
    path_count, hop_count = path_links.shape
    entries = path_count * hop_count
    capacity = entries // peer_count
    slots = peer_count * capacity
    flat_ids = path_links.reshape(-1)
    is_live = flat_ids >= 0
    owner_id = jnp.where(is_live, flat_ids // link_dev, peer_count)
    local_id = jnp.where(is_live, flat_ids % link_dev, 0)
    marks = (owner_id[:, None] == jnp.arange(peer_count)[None, :]).astype(bf16)
    order = jnp.arange(entries)
    earlier = (order[None, :] < order[:, None]).astype(bf16)
    before = jnp.dot(earlier, marks, preferred_element_type=f32)
    slot_id = jnp.sum(before * marks.astype(f32), axis=1).astype(jnp.int32)
    offset = lax.rem(owner_id - me + peer_count, peer_count)
    dest = jnp.where(is_live, offset * capacity + slot_id, -1)
    dest = dest.reshape(path_count, hop_count).T.reshape(-1)
    local_id = local_id.reshape(path_count, hop_count).T.reshape(-1)
    slot_ids = jnp.arange(slots)
    route = dest[None, :] == slot_ids[:, None]
    requests = jnp.sum(jnp.where(route, local_id[None, :] + 1, 0), axis=1) - 1
    req = jnp.full((peer_count, 8, 128), -1, jnp.int32)
    req = lax.dynamic_update_slice(req, requests.reshape(peer_count, 1, capacity), (0, 0, 0))
    path_final, link_next, read_grad = run_all(
        req, own_links, w_path_in, w_path_hid, path_state[0], path_links, dest[None, :],
        cotangent[0], w_link_in, w_link_hid, capacity, n_grp, peer_count)
    return (link_next[None], path_final[None], read_grad)


def solution(mesh):
    return jax.shard_map(
        shards,
        mesh=mesh,
        in_specs=(
            P("grp", "path", None),
            P("grp", "path", None),
            P("path", None),
            P(),
            P(),
            P(),
            P(),
            P("grp", "path", None),
        ),
        out_specs=(P("grp", "path", None), P("grp", "path", None), P("path", None)),
        check_vma=False,
    )
```

```python
import jax
import jax.numpy as jnp
from jax import lax
from jax.experimental import pallas as pl
from jax.experimental.pallas import tpu as pltpu
from jax.sharding import PartitionSpec as P

MESH = pl.DeviceIdType.MESH


def gated_update(projected, carried, w_hidden):
    width = carried.shape[1]
    recur = jnp.dot(carried.astype(jnp.bfloat16), w_hidden, preferred_element_type=jnp.float32)
    reset = jax.nn.sigmoid(projected[:, :width] + recur[:, :width])
    update = jax.nn.sigmoid(projected[:, width : 2 * width] + recur[:, width : 2 * width])
    candidate = jnp.tanh(projected[:, 2 * width :] + reset * recur[:, 2 * width :])
    return (1.0 - update) * candidate + update * carried


def _greet(barrier, g, p, n_grp, n_path, with_grp):
    def greet_path(k, c):
        pl.semaphore_signal(barrier, inc=1, device_id=(g, lax.rem(p + k, n_path)), device_id_type=MESH)
        return c

    def greet_grp(k, c):
        pl.semaphore_signal(barrier, inc=1, device_id=(lax.rem(g + k, n_grp), p), device_id_type=MESH)
        return c

    lax.fori_loop(1, n_path, greet_path, 0)
    count = n_path - 1
    if with_grp:
        lax.fori_loop(1, n_grp, greet_grp, 0)
        count += n_grp - 1
    pl.semaphore_wait(barrier, count)


def _ring_copies(src, dst, send, recv, g, p, n_path, sign):
    def make(k):
        return pltpu.make_async_remote_copy(
            src_ref=src.at[k], dst_ref=dst.at[k], send_sem=send.at[k - 1], recv_sem=recv.at[k - 1],
            device_id=(g, lax.rem(p + sign * k + n_path, n_path)), device_id_type=MESH)

    def start(k, c):
        make(k).start()
        return c

    def finish(k, c):
        copy = make(k)
        copy.wait_send()
        copy.wait_recv()
        return c

    return start, finish


def _fetch_kernel(n_grp, n_path, req_ref, links_ref, got_ref, ids_ref,
                  reqin, want, served, gotbuf, rsend, rrecv, asend, arecv, greet=True, during=None):
    g = lax.axis_index("grp")
    p = lax.axis_index("path")
    if greet:
        _greet(pltpu.get_barrier_semaphore(), g, p, n_grp, n_path, False)
    start_req, finish_req = _ring_copies(req_ref, reqin, rsend, rrecv, g, p, n_path, 1)
    lax.fori_loop(1, n_path, start_req, 0)
    reqin[0] = req_ref[0]
    lax.fori_loop(1, n_path, finish_req, 0)
    n_k, cap = served.shape[0], served.shape[1]
    link_dev = links_ref.shape[0]
    ids_t = jnp.transpose(reqin[:, 0, :])
    lanes = lax.broadcasted_iota(jnp.int32, (1, link_dev), 1)
    for k in range(n_k):
        want[k * cap : (k + 1) * cap, :] = (ids_t[0:cap, k : k + 1] == lanes).astype(jnp.bfloat16)
    rows = jnp.dot(want[...], links_ref[...], preferred_element_type=jnp.float32).astype(jnp.bfloat16)
    served[...] = rows.reshape(served.shape)
    start_ans, finish_ans = _ring_copies(served, gotbuf, asend, arecv, g, p, n_path, -1)
    lax.fori_loop(1, n_path, start_ans, 0)
    gotbuf[0] = served[0]
    if ids_ref is not None:
        ids_ref[...] = reqin[...]
    if during is not None:
        during()
    lax.fori_loop(1, n_path, finish_ans, 0)
    got_ref[...] = gotbuf[...]


def fetch_rows(req, own_links, cap, n_grp, n_path):
    n_k, rows, lanes = req.shape
    width = own_links.shape[1]
    return pl.pallas_call(
        lambda *refs: _fetch_kernel(n_grp, n_path, *refs),
        out_shape=(jax.ShapeDtypeStruct((n_k, cap, width), jnp.bfloat16),
                   jax.ShapeDtypeStruct((n_k, rows, lanes), jnp.int32)),
        in_specs=[pl.BlockSpec(memory_space=pltpu.VMEM)] * 2,
        out_specs=(pl.BlockSpec(memory_space=pltpu.VMEM),) * 2,
        scratch_shapes=[
            pltpu.VMEM((n_k, rows, lanes), jnp.int32),
            pltpu.VMEM((n_k * cap, own_links.shape[0]), jnp.bfloat16),
            pltpu.VMEM((n_k, cap, width), jnp.bfloat16),
            pltpu.VMEM((n_k, cap, width), jnp.bfloat16),
            pltpu.SemaphoreType.DMA((n_path - 1,)),
            pltpu.SemaphoreType.DMA((n_path - 1,)),
            pltpu.SemaphoreType.DMA((n_path - 1,)),
            pltpu.SemaphoreType.DMA((n_path - 1,)),
        ],
        compiler_params=pltpu.CompilerParams(collective_id=0, has_side_effects=True),
    )(req, own_links)


def _message_kernel(n_grp, n_path, out_ref, term_ref, inc_ref, grad_ref,
                    inbuf, recv1, recv2, mid, msend, mrecv, send1, got1, send2, got2, greet=True,
                    after_msgs=None):
    g = lax.axis_index("grp")
    p = lax.axis_index("path")
    if greet:
        _greet(pltpu.get_barrier_semaphore(), g, p, n_grp, n_path, True)
    start_msg, finish_msg = _ring_copies(out_ref, inbuf, msend, mrecv, g, p, n_path, 1)

    def path_copy(k, q):
        return pltpu.make_async_remote_copy(
            src_ref=term_ref.at[q], dst_ref=recv1.at[k - 1], send_sem=send1.at[k - 1],
            recv_sem=got1.at[k - 1], device_id=(g, q), device_id_type=MESH)

    def start1(k, c):
        path_copy(k, lax.rem(p + k, n_path)).start()
        return c

    def finish1(k, c):
        copy = path_copy(k, lax.rem(p + k, n_path))
        copy.wait_send()
        copy.wait_recv()
        return c

    lax.fori_loop(1, n_path, start1, 0)
    lax.fori_loop(1, n_path, start_msg, 0)
    inbuf[0] = out_ref[0]
    lax.fori_loop(1, n_path, finish1, 0)
    mid[...] = term_ref[p] + jnp.sum(recv1[...], axis=0)

    def grp_copy(k, h):
        return pltpu.make_async_remote_copy(
            src_ref=mid, dst_ref=recv2.at[k - 1], send_sem=send2.at[k - 1],
            recv_sem=got2.at[k - 1], device_id=(h, p), device_id_type=MESH)

    def start2(k, c):
        grp_copy(k, lax.rem(g + k, n_grp)).start()
        return c

    def finish2(k, c):
        copy = grp_copy(k, lax.rem(g + k, n_grp))
        copy.wait_send()
        copy.wait_recv()
        return c

    lax.fori_loop(1, n_grp, start2, 0)
    lax.fori_loop(1, n_path, finish_msg, 0)
    if inc_ref is not None:
        inc_ref[...] = inbuf[...]
    if after_msgs is not None:
        after_msgs()
    lax.fori_loop(1, n_grp, finish2, 0)
    grad_ref[...] = mid[...] + jnp.sum(recv2[...], axis=0)


def exchange_messages(outgoing, term, n_grp, n_path):
    n_k, cap, width = outgoing.shape
    _, rows, gwidth = term.shape
    return pl.pallas_call(
        lambda *refs: _message_kernel(n_grp, n_path, *refs),
        out_shape=(jax.ShapeDtypeStruct((n_k, cap, width), jnp.bfloat16),
                   jax.ShapeDtypeStruct((rows, gwidth), jnp.float32)),
        in_specs=[pl.BlockSpec(memory_space=pltpu.VMEM)] * 2,
        out_specs=(pl.BlockSpec(memory_space=pltpu.VMEM),) * 2,
        scratch_shapes=[
            pltpu.VMEM((n_k, cap, width), jnp.bfloat16),
            pltpu.VMEM((n_path - 1, rows, gwidth), jnp.float32),
            pltpu.VMEM((n_grp - 1, rows, gwidth), jnp.float32),
            pltpu.VMEM((rows, gwidth), jnp.float32),
            pltpu.SemaphoreType.DMA((n_path - 1,)),
            pltpu.SemaphoreType.DMA((n_path - 1,)),
            pltpu.SemaphoreType.DMA((n_path - 1,)),
            pltpu.SemaphoreType.DMA((n_path - 1,)),
            pltpu.SemaphoreType.DMA((n_grp - 1,)),
            pltpu.SemaphoreType.DMA((n_grp - 1,)),
        ],
        compiler_params=pltpu.CompilerParams(collective_id=1, has_side_effects=True),
    )(outgoing, term)


def _route_mats(drow, slots):
    dcols = jnp.transpose(jnp.broadcast_to(drow, (8, drow.shape[1])))
    route_t = (dcols[:, 0:1] == lax.broadcasted_iota(jnp.int32, (1, slots), 1)).astype(jnp.bfloat16)
    route = (lax.broadcasted_iota(jnp.int32, (slots, 1), 0) == drow).astype(jnp.bfloat16)
    return route_t, route, dcols


def _hop_kernel(hops, route_t_ref, got_ref, w_in_ref, w_hid_ref, state_ref, live_ref, route_ref, cot_t_ref,
                final_ref, out_ref, term_ref, proj, msgs):
    bf16, f32 = jnp.bfloat16, jnp.float32
    width = got_ref.shape[-1]
    got = got_ref[...].reshape(-1, width)
    fetched = jnp.dot(route_t_ref[...], got, preferred_element_type=f32).astype(bf16)
    proj[...] = jnp.dot(fetched, w_in_ref[...], preferred_element_type=f32)
    carried = state_ref[...].astype(f32)
    n, width = carried.shape
    for h in range(hops):
        p_h = proj[h * n : (h + 1) * n, :]
        renewed = gated_update(p_h, carried, w_hid_ref[...])
        carried = jnp.where(live_ref[h * n : (h + 1) * n, 0:1] >= 0, renewed, carried)
        msgs[h * n : (h + 1) * n, :] = carried.astype(bf16)
    final = carried.astype(bf16)
    final_ref[...] = final
    out_ref[...] = jnp.dot(route_ref[...], msgs[...], preferred_element_type=f32).astype(bf16).reshape(out_ref.shape)
    cot_t = jnp.transpose(cot_t_ref[...].astype(f32)).astype(bf16)
    term = jnp.dot(cot_t, final, preferred_element_type=f32)
    share = term_ref.shape[1]
    for q in range(term_ref.shape[0]):
        term_ref[q] = term[q * share : (q + 1) * share, :]


def run_hops(dcol, got, w_path_in, w_path_hid, state, live, drow, cot_t, n_path):
    entries = dcol.shape[1]
    slots = got.shape[0]
    n, width = state.shape
    hops = entries // n
    return pl.pallas_call(
        lambda *refs: _hop_kernel(hops, *refs),
        out_shape=(jax.ShapeDtypeStruct((n, width), jnp.bfloat16),
                   jax.ShapeDtypeStruct((slots, width), jnp.bfloat16),
                   jax.ShapeDtypeStruct((n_path, cot_t.shape[1] // n_path, width), jnp.float32)),
        in_specs=[pl.BlockSpec(memory_space=pltpu.VMEM)] * 8,
        out_specs=(pl.BlockSpec(memory_space=pltpu.VMEM),) * 3,
        scratch_shapes=[
            pltpu.VMEM((entries, w_path_in.shape[1]), jnp.float32),
            pltpu.VMEM((entries, width), jnp.bfloat16),
        ],
    )(dcol, got, w_path_in, w_path_hid, state, live, drow, cot_t)


def _all_kernel(n_grp, n_path, req_ref, links_ref, w_in_ref, w_hid_ref, state_ref,
                drow_ref, cot_ref, w_lin_ref, w_lhid_ref, final_ref, next_ref, grad_ref,
                reqin, want, served, gotbuf, gotv, rsend, rrecv, asend, arecv,
                proj, msgs, outbuf, termbuf, recur_buf, route_t_buf, route_buf, live_buf, next_buf, next_sem,
                inbuf, recv1, recv2, mid, msend, mrecv, send1, got1, send2, got2):
    f32 = jnp.float32
    g = lax.axis_index("grp")
    p = lax.axis_index("path")
    _greet(pltpu.get_barrier_semaphore(), g, p, n_grp, n_path, True)

    def link_recur():
        recur_buf[...] = jnp.dot(links_ref[...], w_lhid_ref[...], preferred_element_type=f32)
        route_t, route, dcols = _route_mats(drow_ref[...], route_buf.shape[0])
        route_t_buf[...] = route_t
        route_buf[...] = route
        live_buf[...] = dcols

    def link_update():
        width = links_ref.shape[1]
        incoming = inbuf[...].reshape(-1, width)
        link_sum = lax.dot_general(want[...], incoming, (((0,), (0,)), ((), ())), preferred_element_type=f32)
        link_proj = jnp.dot(link_sum.astype(jnp.bfloat16), w_lin_ref[...], preferred_element_type=f32)
        recur = recur_buf[...]
        own = links_ref[...].astype(f32)
        reset = jax.nn.sigmoid(link_proj[:, :width] + recur[:, :width])
        update = jax.nn.sigmoid(link_proj[:, width : 2 * width] + recur[:, width : 2 * width])
        candidate = jnp.tanh(link_proj[:, 2 * width :] + reset * recur[:, 2 * width :])
        next_buf[...] = ((1.0 - update) * candidate + update * own).astype(next_buf.dtype)
        pltpu.make_async_copy(next_buf, next_ref, next_sem).start()

    _fetch_kernel(n_grp, n_path, req_ref, links_ref, gotv, None,
                  reqin, want, served, gotbuf, rsend, rrecv, asend, arecv, greet=False, during=link_recur)
    hops = drow_ref.shape[1] // state_ref.shape[0]
    _hop_kernel(hops, route_t_buf, gotv, w_in_ref, w_hid_ref, state_ref, live_buf, route_buf, cot_ref,
                final_ref, outbuf, termbuf, proj, msgs)
    _message_kernel(n_grp, n_path, outbuf, termbuf, None, grad_ref,
                    inbuf, recv1, recv2, mid, msend, mrecv, send1, got1, send2, got2, greet=False,
                    after_msgs=link_update)
    pltpu.make_async_copy(next_buf, next_ref, next_sem).wait()


def run_all(req, own_links, w_path_in, w_path_hid, state, drow1, cot, w_link_in, w_link_hid,
            cap, n_grp, n_path):
    n_k, rows, lanes = req.shape
    link_dev, width = own_links.shape
    entries = drow1.shape[1]
    n = state.shape[0]
    share = cot.shape[1] // n_path
    vmem = pltpu.VMEM
    dma = pltpu.SemaphoreType.DMA
    return pl.pallas_call(
        lambda *refs: _all_kernel(n_grp, n_path, *refs),
        out_shape=(jax.ShapeDtypeStruct((n, width), jnp.bfloat16),
                   jax.ShapeDtypeStruct((link_dev, width), jnp.bfloat16),
                   jax.ShapeDtypeStruct((share, width), jnp.float32)),
        in_specs=[pl.BlockSpec(memory_space=vmem)] * 9,
        out_specs=(pl.BlockSpec(memory_space=vmem), pl.BlockSpec(memory_space=pl.ANY),
                   pl.BlockSpec(memory_space=vmem)),
        scratch_shapes=[
            vmem((n_k, rows, lanes), jnp.int32),
            vmem((n_k * cap, link_dev), jnp.bfloat16),
            vmem((n_k, cap, width), jnp.bfloat16),
            vmem((n_k, cap, width), jnp.bfloat16),
            vmem((n_k, cap, width), jnp.bfloat16),
            dma((n_path - 1,)), dma((n_path - 1,)), dma((n_path - 1,)), dma((n_path - 1,)),
            vmem((entries, w_path_in.shape[1]), jnp.float32),
            vmem((entries, width), jnp.bfloat16),
            vmem((n_k, cap, width), jnp.bfloat16),
            vmem((n_path, share, width), jnp.float32),
            vmem((link_dev, w_link_hid.shape[1]), jnp.float32),
            vmem((entries, n_k * cap), jnp.bfloat16),
            vmem((n_k * cap, entries), jnp.bfloat16),
            vmem((entries, 8), jnp.int32),
            vmem((link_dev, width), jnp.bfloat16),
            dma(()),
            vmem((n_k, cap, width), jnp.bfloat16),
            vmem((n_path - 1, share, width), jnp.float32),
            vmem((n_grp - 1, share, width), jnp.float32),
            vmem((share, width), jnp.float32),
            dma((n_path - 1,)), dma((n_path - 1,)), dma((n_path - 1,)), dma((n_path - 1,)),
            dma((n_grp - 1,)), dma((n_grp - 1,)),
        ],
        compiler_params=pltpu.CompilerParams(collective_id=0, has_side_effects=True),
    )(req, own_links, w_path_in, w_path_hid, state, drow1, cot, w_link_in, w_link_hid)


def shards(
    link_state, path_state, path_links, w_path_in, w_path_hid, w_link_in, w_link_hid, cotangent
):
    bf16, f32 = jnp.bfloat16, jnp.float32
    own_links = link_state[0]
    link_dev, width = own_links.shape
    n_grp = lax.axis_size("grp")
    peer_count = lax.axis_size("path")
    me = lax.axis_index("path")
    path_count, hop_count = path_links.shape
    entries = path_count * hop_count
    capacity = entries // peer_count
    slots = peer_count * capacity
    flat_ids = path_links.reshape(-1)
    is_live = flat_ids >= 0
    owner_id = jnp.where(is_live, flat_ids // link_dev, peer_count)
    local_id = jnp.where(is_live, flat_ids % link_dev, 0)
    marks = (owner_id[:, None] == jnp.arange(peer_count)[None, :]).astype(bf16)
    order = jnp.arange(entries)
    earlier = (order[None, :] < order[:, None]).astype(bf16)
    before = jnp.dot(earlier, marks, preferred_element_type=f32)
    slot_id = jnp.sum(before * marks.astype(f32), axis=1).astype(jnp.int32)
    offset = lax.rem(owner_id - me + peer_count, peer_count)
    dest = jnp.where(is_live, offset * capacity + slot_id, -1)
    dest = dest.reshape(path_count, hop_count).T.reshape(-1)
    local_id = local_id.reshape(path_count, hop_count).T.reshape(-1)
    slot_ids = jnp.arange(slots)
    route = dest[None, :] == slot_ids[:, None]
    requests = jnp.sum(jnp.where(route, local_id[None, :] + 1, 0), axis=1) - 1
    req = jnp.full((peer_count, 8, 128), -1, jnp.int32)
    req = lax.dynamic_update_slice(req, requests.reshape(peer_count, 1, capacity), (0, 0, 0))
    path_final, link_next, read_grad = run_all(
        req, own_links, w_path_in, w_path_hid, path_state[0], dest[None, :],
        cotangent[0], w_link_in, w_link_hid, capacity, n_grp, peer_count)
    return (link_next[None], path_final[None], read_grad)


def solution(mesh):
    return jax.shard_map(
        shards,
        mesh=mesh,
        in_specs=(
            P("grp", "path", None),
            P("grp", "path", None),
            P("path", None),
            P(),
            P(),
            P(),
            P(),
            P("grp", "path", None),
        ),
        out_specs=(P("grp", "path", None), P("grp", "path", None), P("path", None)),
        check_vma=False,
    )
```

```python
import jax
import jax.numpy as jnp
from jax import lax
from jax.experimental import pallas as pl
from jax.experimental.pallas import tpu as pltpu
from jax.sharding import PartitionSpec as P

MESH = pl.DeviceIdType.MESH


def gated_update(projected, carried, w_hidden):
    width = carried.shape[1]
    recur = jnp.dot(carried.astype(jnp.bfloat16), w_hidden, preferred_element_type=jnp.float32)
    reset = jax.nn.sigmoid(projected[:, :width] + recur[:, :width])
    update = jax.nn.sigmoid(projected[:, width : 2 * width] + recur[:, width : 2 * width])
    candidate = jnp.tanh(projected[:, 2 * width :] + reset * recur[:, 2 * width :])
    return (1.0 - update) * candidate + update * carried


def _greet(barrier, g, p, n_grp, n_path, with_grp):
    def greet_path(k, c):
        pl.semaphore_signal(barrier, inc=1, device_id=(g, lax.rem(p + k, n_path)), device_id_type=MESH)
        return c

    def greet_grp(k, c):
        pl.semaphore_signal(barrier, inc=1, device_id=(lax.rem(g + k, n_grp), p), device_id_type=MESH)
        return c

    lax.fori_loop(1, n_path, greet_path, 0)
    count = n_path - 1
    if with_grp:
        lax.fori_loop(1, n_grp, greet_grp, 0)
        count += n_grp - 1
    pl.semaphore_wait(barrier, count)


def _ring_copies(src, dst, send, recv, g, p, n_path, sign):
    def make(k):
        return pltpu.make_async_remote_copy(
            src_ref=src.at[k], dst_ref=dst.at[k], send_sem=send.at[k - 1], recv_sem=recv.at[k - 1],
            device_id=(g, lax.rem(p + sign * k + n_path, n_path)), device_id_type=MESH)

    def start(k, c):
        make(k).start()
        return c

    def finish(k, c):
        copy = make(k)
        copy.wait_send()
        copy.wait_recv()
        return c

    return start, finish


def _fetch_kernel(n_grp, n_path, req_ref, links_ref, got_ref, ids_ref,
                  reqin, want, served, gotbuf, rsend, rrecv, asend, arecv, greet=True, during=None):
    g = lax.axis_index("grp")
    p = lax.axis_index("path")
    if greet:
        _greet(pltpu.get_barrier_semaphore(), g, p, n_grp, n_path, False)
    start_req, finish_req = _ring_copies(req_ref, reqin, rsend, rrecv, g, p, n_path, 1)
    lax.fori_loop(1, n_path, start_req, 0)
    reqin[0] = req_ref[0]
    n_k, cap = served.shape[0], served.shape[1]
    link_dev = links_ref.shape[0]
    lanes = lax.broadcasted_iota(jnp.int32, (1, link_dev), 1)
    start_ans, finish_ans = _ring_copies(served, gotbuf, asend, arecv, g, p, n_path, -1)
    half = n_k // 2
    for lo, hi in ((0, half), (half, n_k)):
        lax.fori_loop(max(lo, 1), hi, finish_req, 0)
        ids_t = jnp.transpose(reqin[lo:hi, 0, :])
        for k in range(lo, hi):
            want[k * cap : (k + 1) * cap, :] = (ids_t[0:cap, k - lo : k - lo + 1] == lanes).astype(jnp.bfloat16)
        rows = jnp.dot(want[lo * cap : hi * cap, :], links_ref[...], preferred_element_type=jnp.float32)
        served[lo:hi] = rows.astype(jnp.bfloat16).reshape(hi - lo, cap, rows.shape[-1])
        lax.fori_loop(max(lo, 1), hi, start_ans, 0)
    gotbuf[0] = served[0]
    if ids_ref is not None:
        ids_ref[...] = reqin[...]
    if during is not None:
        during()
    lax.fori_loop(1, n_path, finish_ans, 0)
    if got_ref is not None:
        got_ref[...] = gotbuf[...]


def fetch_rows(req, own_links, cap, n_grp, n_path):
    n_k, rows, lanes = req.shape
    width = own_links.shape[1]
    return pl.pallas_call(
        lambda *refs: _fetch_kernel(n_grp, n_path, *refs),
        out_shape=(jax.ShapeDtypeStruct((n_k, cap, width), jnp.bfloat16),
                   jax.ShapeDtypeStruct((n_k, rows, lanes), jnp.int32)),
        in_specs=[pl.BlockSpec(memory_space=pltpu.VMEM)] * 2,
        out_specs=(pl.BlockSpec(memory_space=pltpu.VMEM),) * 2,
        scratch_shapes=[
            pltpu.VMEM((n_k, rows, lanes), jnp.int32),
            pltpu.VMEM((n_k * cap, own_links.shape[0]), jnp.bfloat16),
            pltpu.VMEM((n_k, cap, width), jnp.bfloat16),
            pltpu.VMEM((n_k, cap, width), jnp.bfloat16),
            pltpu.SemaphoreType.DMA((n_path - 1,)),
            pltpu.SemaphoreType.DMA((n_path - 1,)),
            pltpu.SemaphoreType.DMA((n_path - 1,)),
            pltpu.SemaphoreType.DMA((n_path - 1,)),
        ],
        compiler_params=pltpu.CompilerParams(collective_id=0, has_side_effects=True),
    )(req, own_links)


def _message_kernel(n_grp, n_path, out_ref, term_ref, inc_ref, grad_ref,
                    inbuf, recv1, recv2, mid, msend, mrecv, send1, got1, send2, got2, greet=True,
                    after_msgs=None):
    g = lax.axis_index("grp")
    p = lax.axis_index("path")
    if greet:
        _greet(pltpu.get_barrier_semaphore(), g, p, n_grp, n_path, True)
    start_msg, finish_msg = _ring_copies(out_ref, inbuf, msend, mrecv, g, p, n_path, 1)

    def path_copy(k, q):
        return pltpu.make_async_remote_copy(
            src_ref=term_ref.at[q], dst_ref=recv1.at[k - 1], send_sem=send1.at[k - 1],
            recv_sem=got1.at[k - 1], device_id=(g, q), device_id_type=MESH)

    def start1(k, c):
        path_copy(k, lax.rem(p + k, n_path)).start()
        return c

    def finish1(k, c):
        copy = path_copy(k, lax.rem(p + k, n_path))
        copy.wait_send()
        copy.wait_recv()
        return c

    lax.fori_loop(1, n_path, start1, 0)
    lax.fori_loop(1, n_path, start_msg, 0)
    inbuf[0] = out_ref[0]
    lax.fori_loop(1, n_path, finish1, 0)
    mid[...] = term_ref[p] + jnp.sum(recv1[...], axis=0)

    def grp_copy(k, h):
        return pltpu.make_async_remote_copy(
            src_ref=mid, dst_ref=recv2.at[k - 1], send_sem=send2.at[k - 1],
            recv_sem=got2.at[k - 1], device_id=(h, p), device_id_type=MESH)

    def start2(k, c):
        grp_copy(k, lax.rem(g + k, n_grp)).start()
        return c

    def finish2(k, c):
        copy = grp_copy(k, lax.rem(g + k, n_grp))
        copy.wait_send()
        copy.wait_recv()
        return c

    lax.fori_loop(1, n_grp, start2, 0)
    lax.fori_loop(1, n_path, finish_msg, 0)
    if inc_ref is not None:
        inc_ref[...] = inbuf[...]
    if after_msgs is not None:
        after_msgs()
    lax.fori_loop(1, n_grp, finish2, 0)
    grad_ref[...] = mid[...] + jnp.sum(recv2[...], axis=0)


def exchange_messages(outgoing, term, n_grp, n_path):
    n_k, cap, width = outgoing.shape
    _, rows, gwidth = term.shape
    return pl.pallas_call(
        lambda *refs: _message_kernel(n_grp, n_path, *refs),
        out_shape=(jax.ShapeDtypeStruct((n_k, cap, width), jnp.bfloat16),
                   jax.ShapeDtypeStruct((rows, gwidth), jnp.float32)),
        in_specs=[pl.BlockSpec(memory_space=pltpu.VMEM)] * 2,
        out_specs=(pl.BlockSpec(memory_space=pltpu.VMEM),) * 2,
        scratch_shapes=[
            pltpu.VMEM((n_k, cap, width), jnp.bfloat16),
            pltpu.VMEM((n_path - 1, rows, gwidth), jnp.float32),
            pltpu.VMEM((n_grp - 1, rows, gwidth), jnp.float32),
            pltpu.VMEM((rows, gwidth), jnp.float32),
            pltpu.SemaphoreType.DMA((n_path - 1,)),
            pltpu.SemaphoreType.DMA((n_path - 1,)),
            pltpu.SemaphoreType.DMA((n_path - 1,)),
            pltpu.SemaphoreType.DMA((n_path - 1,)),
            pltpu.SemaphoreType.DMA((n_grp - 1,)),
            pltpu.SemaphoreType.DMA((n_grp - 1,)),
        ],
        compiler_params=pltpu.CompilerParams(collective_id=1, has_side_effects=True),
    )(outgoing, term)


def _route_mats(drow, slots):
    dcol = jnp.transpose(jnp.broadcast_to(drow, (8, drow.shape[1])))[:, 0:1]
    route_t = (dcol == lax.broadcasted_iota(jnp.int32, (1, slots), 1)).astype(jnp.bfloat16)
    route = (lax.broadcasted_iota(jnp.int32, (slots, 1), 0) == drow).astype(jnp.bfloat16)
    return route_t, route


def _hop_kernel(hops, route_t_ref, got_ref, w_in_ref, w_hid_ref, state_ref, live_ref, route_ref, cot_t_ref,
                final_ref, out_ref, term_ref, proj, msgs):
    bf16, f32 = jnp.bfloat16, jnp.float32
    width = got_ref.shape[-1]
    got = got_ref[...].reshape(-1, width)
    fetched = jnp.dot(route_t_ref[...], got, preferred_element_type=f32).astype(bf16)
    proj[...] = jnp.dot(fetched, w_in_ref[...], preferred_element_type=f32)
    carried = state_ref[...].astype(f32)
    n, width = carried.shape
    for h in range(hops):
        p_h = proj[h * n : (h + 1) * n, :]
        renewed = gated_update(p_h, carried, w_hid_ref[...])
        carried = jnp.where(live_ref[:, h : h + 1] >= 0, renewed, carried)
        msgs[h * n : (h + 1) * n, :] = carried.astype(bf16)
    final = carried.astype(bf16)
    final_ref[...] = final
    out_ref[...] = jnp.dot(route_ref[...], msgs[...], preferred_element_type=f32).astype(bf16).reshape(out_ref.shape)
    cot_t = jnp.transpose(cot_t_ref[...].astype(f32)).astype(bf16)
    term = jnp.dot(cot_t, final, preferred_element_type=f32)
    share = term_ref.shape[1]
    for q in range(term_ref.shape[0]):
        term_ref[q] = term[q * share : (q + 1) * share, :]


def run_hops(dcol, got, w_path_in, w_path_hid, state, live, drow, cot_t, n_path):
    entries = dcol.shape[1]
    slots = got.shape[0]
    n, width = state.shape
    hops = entries // n
    return pl.pallas_call(
        lambda *refs: _hop_kernel(hops, *refs),
        out_shape=(jax.ShapeDtypeStruct((n, width), jnp.bfloat16),
                   jax.ShapeDtypeStruct((slots, width), jnp.bfloat16),
                   jax.ShapeDtypeStruct((n_path, cot_t.shape[1] // n_path, width), jnp.float32)),
        in_specs=[pl.BlockSpec(memory_space=pltpu.VMEM)] * 8,
        out_specs=(pl.BlockSpec(memory_space=pltpu.VMEM),) * 3,
        scratch_shapes=[
            pltpu.VMEM((entries, w_path_in.shape[1]), jnp.float32),
            pltpu.VMEM((entries, width), jnp.bfloat16),
        ],
    )(dcol, got, w_path_in, w_path_hid, state, live, drow, cot_t)


def _all_kernel(n_grp, n_path, req_ref, links_ref, w_in_ref, w_hid_ref, state_ref, live_ref,
                drow_ref, cot_ref, w_lin_ref, w_lhid_ref, final_ref, next_ref, grad_ref,
                reqin, want, served, gotbuf, gotv, rsend, rrecv, asend, arecv,
                proj, msgs, outbuf, termbuf, recur_buf, route_t_buf, route_buf,
                inbuf, recv1, recv2, mid, msend, mrecv, send1, got1, send2, got2):
    f32 = jnp.float32
    g = lax.axis_index("grp")
    p = lax.axis_index("path")
    _greet(pltpu.get_barrier_semaphore(), g, p, n_grp, n_path, True)

    def link_recur():
        recur_buf[...] = jnp.dot(links_ref[...], w_lhid_ref[...], preferred_element_type=f32)
        route_t, route = _route_mats(drow_ref[...], route_buf.shape[0])
        route_t_buf[...] = route_t
        route_buf[...] = route

    def link_update():
        width = links_ref.shape[1]
        incoming = inbuf[...].reshape(-1, width)
        link_sum = lax.dot_general(want[...], incoming, (((0,), (0,)), ((), ())), preferred_element_type=f32)
        link_proj = jnp.dot(link_sum.astype(jnp.bfloat16), w_lin_ref[...], preferred_element_type=f32)
        recur = recur_buf[...]
        own = links_ref[...].astype(f32)
        reset = jax.nn.sigmoid(link_proj[:, :width] + recur[:, :width])
        update = jax.nn.sigmoid(link_proj[:, width : 2 * width] + recur[:, width : 2 * width])
        candidate = jnp.tanh(link_proj[:, 2 * width :] + reset * recur[:, 2 * width :])
        next_ref[...] = ((1.0 - update) * candidate + update * own).astype(next_ref.dtype)

    _fetch_kernel(n_grp, n_path, req_ref, links_ref, None, None,
                  reqin, want, served, gotbuf, rsend, rrecv, asend, arecv, greet=False, during=link_recur)
    hops = drow_ref.shape[1] // state_ref.shape[0]
    _hop_kernel(hops, route_t_buf, gotbuf, w_in_ref, w_hid_ref, state_ref, live_ref, route_buf, cot_ref,
                final_ref, outbuf, termbuf, proj, msgs)
    _message_kernel(n_grp, n_path, outbuf, termbuf, None, grad_ref,
                    inbuf, recv1, recv2, mid, msend, mrecv, send1, got1, send2, got2, greet=False,
                    after_msgs=link_update)


def run_all(req, own_links, w_path_in, w_path_hid, state, live, drow1, cot, w_link_in, w_link_hid,
            cap, n_grp, n_path):
    n_k, rows, lanes = req.shape
    link_dev, width = own_links.shape
    entries = drow1.shape[1]
    n = state.shape[0]
    share = cot.shape[1] // n_path
    vmem = pltpu.VMEM
    dma = pltpu.SemaphoreType.DMA
    return pl.pallas_call(
        lambda *refs: _all_kernel(n_grp, n_path, *refs),
        out_shape=(jax.ShapeDtypeStruct((n, width), jnp.bfloat16),
                   jax.ShapeDtypeStruct((link_dev, width), jnp.bfloat16),
                   jax.ShapeDtypeStruct((share, width), jnp.float32)),
        in_specs=[pl.BlockSpec(memory_space=vmem)] * 10,
        out_specs=(pl.BlockSpec(memory_space=vmem),) * 3,
        scratch_shapes=[
            vmem((n_k, rows, lanes), jnp.int32),
            vmem((n_k * cap, link_dev), jnp.bfloat16),
            vmem((n_k, cap, width), jnp.bfloat16),
            vmem((n_k, cap, width), jnp.bfloat16),
            vmem((n_k, cap, width), jnp.bfloat16),
            dma((n_path - 1,)), dma((n_path - 1,)), dma((n_path - 1,)), dma((n_path - 1,)),
            vmem((entries, w_path_in.shape[1]), jnp.float32),
            vmem((entries, width), jnp.bfloat16),
            vmem((n_k, cap, width), jnp.bfloat16),
            vmem((n_path, share, width), jnp.float32),
            vmem((link_dev, w_link_hid.shape[1]), jnp.float32),
            vmem((entries, n_k * cap), jnp.bfloat16),
            vmem((n_k * cap, entries), jnp.bfloat16),
            vmem((n_k, cap, width), jnp.bfloat16),
            vmem((n_path - 1, share, width), jnp.float32),
            vmem((n_grp - 1, share, width), jnp.float32),
            vmem((share, width), jnp.float32),
            dma((n_path - 1,)), dma((n_path - 1,)), dma((n_path - 1,)), dma((n_path - 1,)),
            dma((n_grp - 1,)), dma((n_grp - 1,)),
        ],
        compiler_params=pltpu.CompilerParams(collective_id=0, has_side_effects=True),
    )(req, own_links, w_path_in, w_path_hid, state, live, drow1, cot, w_link_in, w_link_hid)


def shards(
    link_state, path_state, path_links, w_path_in, w_path_hid, w_link_in, w_link_hid, cotangent
):
    bf16, f32 = jnp.bfloat16, jnp.float32
    own_links = link_state[0]
    link_dev, width = own_links.shape
    n_grp = lax.axis_size("grp")
    peer_count = lax.axis_size("path")
    me = lax.axis_index("path")
    path_count, hop_count = path_links.shape
    entries = path_count * hop_count
    capacity = entries // peer_count
    slots = peer_count * capacity
    flat_ids = path_links.reshape(-1)
    is_live = flat_ids >= 0
    owner_id = jnp.where(is_live, flat_ids // link_dev, peer_count)
    local_id = jnp.where(is_live, flat_ids % link_dev, 0)
    marks = (owner_id[:, None] == jnp.arange(peer_count)[None, :]).astype(bf16)
    order = jnp.arange(entries)
    earlier = (order[None, :] < order[:, None]).astype(bf16)
    before = jnp.dot(earlier, marks, preferred_element_type=f32)
    slot_id = jnp.sum(before * marks.astype(f32), axis=1).astype(jnp.int32)
    offset = lax.rem(owner_id - me + peer_count, peer_count)
    dest = jnp.where(is_live, offset * capacity + slot_id, -1)
    dest = dest.reshape(path_count, hop_count).T.reshape(-1)
    local_id = local_id.reshape(path_count, hop_count).T.reshape(-1)
    slot_ids = jnp.arange(slots)
    route = dest[None, :] == slot_ids[:, None]
    requests = jnp.sum(jnp.where(route, local_id[None, :] + 1, 0), axis=1) - 1
    req = jnp.full((peer_count, 8, 128), -1, jnp.int32)
    req = lax.dynamic_update_slice(req, requests.reshape(peer_count, 1, capacity), (0, 0, 0))
    path_final, link_next, read_grad = run_all(
        req, own_links, w_path_in, w_path_hid, path_state[0], path_links, dest[None, :],
        cotangent[0], w_link_in, w_link_hid, capacity, n_grp, peer_count)
    return (link_next[None], path_final[None], read_grad)


def solution(mesh):
    return jax.shard_map(
        shards,
        mesh=mesh,
        in_specs=(
            P("grp", "path", None),
            P("grp", "path", None),
            P("path", None),
            P(),
            P(),
            P(),
            P(),
            P("grp", "path", None),
        ),
        out_specs=(P("grp", "path", None), P("grp", "path", None), P("path", None)),
        check_vma=False,
    )
```

```python
import jax
import jax.numpy as jnp
from jax import lax
from jax.experimental import pallas as pl
from jax.experimental.pallas import tpu as pltpu
from jax.sharding import PartitionSpec as P

MESH = pl.DeviceIdType.MESH


def gated_update(projected, carried, w_hidden):
    width = carried.shape[1]
    recur = jnp.dot(carried.astype(jnp.bfloat16), w_hidden, preferred_element_type=jnp.float32)
    reset = jax.nn.sigmoid(projected[:, :width] + recur[:, :width])
    update = jax.nn.sigmoid(projected[:, width : 2 * width] + recur[:, width : 2 * width])
    candidate = jnp.tanh(projected[:, 2 * width :] + reset * recur[:, 2 * width :])
    return (1.0 - update) * candidate + update * carried


def _greet(barrier, g, p, n_grp, n_path, with_grp):
    def greet_path(k, c):
        pl.semaphore_signal(barrier, inc=1, device_id=(g, lax.rem(p + k, n_path)), device_id_type=MESH)
        return c

    def greet_grp(k, c):
        pl.semaphore_signal(barrier, inc=1, device_id=(lax.rem(g + k, n_grp), p), device_id_type=MESH)
        return c

    lax.fori_loop(1, n_path, greet_path, 0)
    count = n_path - 1
    if with_grp:
        lax.fori_loop(1, n_grp, greet_grp, 0)
        count += n_grp - 1
    pl.semaphore_wait(barrier, count)


def _ring_copies(src, dst, send, recv, g, p, n_path, sign):
    def make(k):
        return pltpu.make_async_remote_copy(
            src_ref=src.at[k], dst_ref=dst.at[k], send_sem=send.at[k - 1], recv_sem=recv.at[k - 1],
            device_id=(g, lax.rem(p + sign * k + n_path, n_path)), device_id_type=MESH)

    def start(k, c):
        make(k).start()
        return c

    def finish(k, c):
        copy = make(k)
        copy.wait_send()
        copy.wait_recv()
        return c

    return start, finish


def _fetch_kernel(n_grp, n_path, req_ref, links_ref, got_ref, ids_ref,
                  reqin, want, served, gotbuf, rsend, rrecv, asend, arecv, greet=True, during=None):
    g = lax.axis_index("grp")
    p = lax.axis_index("path")
    if greet:
        _greet(pltpu.get_barrier_semaphore(), g, p, n_grp, n_path, False)
    start_req, finish_req = _ring_copies(req_ref, reqin, rsend, rrecv, g, p, n_path, 1)
    lax.fori_loop(1, n_path, start_req, 0)
    reqin[0] = req_ref[0]
    n_k, cap = served.shape[0], served.shape[1]
    link_dev = links_ref.shape[0]
    lanes = lax.broadcasted_iota(jnp.int32, (1, link_dev), 1)
    start_ans, finish_ans = _ring_copies(served, gotbuf, asend, arecv, g, p, n_path, -1)
    part = n_k // 4
    for lo, hi in ((0, part), (part, 2 * part), (2 * part, 3 * part), (3 * part, n_k)):
        lax.fori_loop(max(lo, 1), hi, finish_req, 0)
        ids_t = jnp.transpose(reqin[lo:hi, 0, :])
        for k in range(lo, hi):
            want[k * cap : (k + 1) * cap, :] = (ids_t[0:cap, k - lo : k - lo + 1] == lanes).astype(jnp.bfloat16)
        rows = jnp.dot(want[lo * cap : hi * cap, :], links_ref[...], preferred_element_type=jnp.float32)
        served[lo:hi] = rows.astype(jnp.bfloat16).reshape(hi - lo, cap, rows.shape[-1])
        lax.fori_loop(max(lo, 1), hi, start_ans, 0)
    gotbuf[0] = served[0]
    if ids_ref is not None:
        ids_ref[...] = reqin[...]
    if during is not None:
        during()
    lax.fori_loop(1, n_path, finish_ans, 0)
    if got_ref is not None:
        got_ref[...] = gotbuf[...]


def fetch_rows(req, own_links, cap, n_grp, n_path):
    n_k, rows, lanes = req.shape
    width = own_links.shape[1]
    return pl.pallas_call(
        lambda *refs: _fetch_kernel(n_grp, n_path, *refs),
        out_shape=(jax.ShapeDtypeStruct((n_k, cap, width), jnp.bfloat16),
                   jax.ShapeDtypeStruct((n_k, rows, lanes), jnp.int32)),
        in_specs=[pl.BlockSpec(memory_space=pltpu.VMEM)] * 2,
        out_specs=(pl.BlockSpec(memory_space=pltpu.VMEM),) * 2,
        scratch_shapes=[
            pltpu.VMEM((n_k, rows, lanes), jnp.int32),
            pltpu.VMEM((n_k * cap, own_links.shape[0]), jnp.bfloat16),
            pltpu.VMEM((n_k, cap, width), jnp.bfloat16),
            pltpu.VMEM((n_k, cap, width), jnp.bfloat16),
            pltpu.SemaphoreType.DMA((n_path - 1,)),
            pltpu.SemaphoreType.DMA((n_path - 1,)),
            pltpu.SemaphoreType.DMA((n_path - 1,)),
            pltpu.SemaphoreType.DMA((n_path - 1,)),
        ],
        compiler_params=pltpu.CompilerParams(collective_id=0, has_side_effects=True),
    )(req, own_links)


def _message_kernel(n_grp, n_path, out_ref, term_ref, inc_ref, grad_ref,
                    inbuf, recv1, recv2, mid, msend, mrecv, send1, got1, send2, got2, greet=True,
                    after_msgs=None):
    g = lax.axis_index("grp")
    p = lax.axis_index("path")
    if greet:
        _greet(pltpu.get_barrier_semaphore(), g, p, n_grp, n_path, True)
    start_msg, finish_msg = _ring_copies(out_ref, inbuf, msend, mrecv, g, p, n_path, 1)

    def path_copy(k, q):
        return pltpu.make_async_remote_copy(
            src_ref=term_ref.at[q], dst_ref=recv1.at[k - 1], send_sem=send1.at[k - 1],
            recv_sem=got1.at[k - 1], device_id=(g, q), device_id_type=MESH)

    def start1(k, c):
        path_copy(k, lax.rem(p + k, n_path)).start()
        return c

    def finish1(k, c):
        copy = path_copy(k, lax.rem(p + k, n_path))
        copy.wait_send()
        copy.wait_recv()
        return c

    lax.fori_loop(1, n_path, start1, 0)
    lax.fori_loop(1, n_path, start_msg, 0)
    inbuf[0] = out_ref[0]
    lax.fori_loop(1, n_path, finish1, 0)
    mid[...] = term_ref[p] + jnp.sum(recv1[...], axis=0)

    def grp_copy(k, h):
        return pltpu.make_async_remote_copy(
            src_ref=mid, dst_ref=recv2.at[k - 1], send_sem=send2.at[k - 1],
            recv_sem=got2.at[k - 1], device_id=(h, p), device_id_type=MESH)

    def start2(k, c):
        grp_copy(k, lax.rem(g + k, n_grp)).start()
        return c

    def finish2(k, c):
        copy = grp_copy(k, lax.rem(g + k, n_grp))
        copy.wait_send()
        copy.wait_recv()
        return c

    lax.fori_loop(1, n_grp, start2, 0)
    lax.fori_loop(1, n_path, finish_msg, 0)
    if inc_ref is not None:
        inc_ref[...] = inbuf[...]
    if after_msgs is not None:
        after_msgs()
    lax.fori_loop(1, n_grp, finish2, 0)
    grad_ref[...] = mid[...] + jnp.sum(recv2[...], axis=0)


def exchange_messages(outgoing, term, n_grp, n_path):
    n_k, cap, width = outgoing.shape
    _, rows, gwidth = term.shape
    return pl.pallas_call(
        lambda *refs: _message_kernel(n_grp, n_path, *refs),
        out_shape=(jax.ShapeDtypeStruct((n_k, cap, width), jnp.bfloat16),
                   jax.ShapeDtypeStruct((rows, gwidth), jnp.float32)),
        in_specs=[pl.BlockSpec(memory_space=pltpu.VMEM)] * 2,
        out_specs=(pl.BlockSpec(memory_space=pltpu.VMEM),) * 2,
        scratch_shapes=[
            pltpu.VMEM((n_k, cap, width), jnp.bfloat16),
            pltpu.VMEM((n_path - 1, rows, gwidth), jnp.float32),
            pltpu.VMEM((n_grp - 1, rows, gwidth), jnp.float32),
            pltpu.VMEM((rows, gwidth), jnp.float32),
            pltpu.SemaphoreType.DMA((n_path - 1,)),
            pltpu.SemaphoreType.DMA((n_path - 1,)),
            pltpu.SemaphoreType.DMA((n_path - 1,)),
            pltpu.SemaphoreType.DMA((n_path - 1,)),
            pltpu.SemaphoreType.DMA((n_grp - 1,)),
            pltpu.SemaphoreType.DMA((n_grp - 1,)),
        ],
        compiler_params=pltpu.CompilerParams(collective_id=1, has_side_effects=True),
    )(outgoing, term)


def _route_mats(drow, slots):
    dcol = jnp.transpose(jnp.broadcast_to(drow, (8, drow.shape[1])))[:, 0:1]
    route_t = (dcol == lax.broadcasted_iota(jnp.int32, (1, slots), 1)).astype(jnp.bfloat16)
    route = (lax.broadcasted_iota(jnp.int32, (slots, 1), 0) == drow).astype(jnp.bfloat16)
    return route_t, route


def _hop_kernel(hops, route_t_ref, got_ref, w_in_ref, w_hid_ref, state_ref, live_ref, route_ref, cot_t_ref,
                final_ref, out_ref, term_ref, proj, msgs):
    bf16, f32 = jnp.bfloat16, jnp.float32
    width = got_ref.shape[-1]
    got = got_ref[...].reshape(-1, width)
    fetched = jnp.dot(route_t_ref[...], got, preferred_element_type=f32).astype(bf16)
    proj[...] = jnp.dot(fetched, w_in_ref[...], preferred_element_type=f32)
    carried = state_ref[...].astype(f32)
    n, width = carried.shape
    for h in range(hops):
        p_h = proj[h * n : (h + 1) * n, :]
        renewed = gated_update(p_h, carried, w_hid_ref[...])
        carried = jnp.where(live_ref[:, h : h + 1] >= 0, renewed, carried)
        msgs[h * n : (h + 1) * n, :] = carried.astype(bf16)
    final = carried.astype(bf16)
    final_ref[...] = final
    out_ref[...] = jnp.dot(route_ref[...], msgs[...], preferred_element_type=f32).astype(bf16).reshape(out_ref.shape)
    cot_t = jnp.transpose(cot_t_ref[...].astype(f32)).astype(bf16)
    term = jnp.dot(cot_t, final, preferred_element_type=f32)
    share = term_ref.shape[1]
    for q in range(term_ref.shape[0]):
        term_ref[q] = term[q * share : (q + 1) * share, :]


def run_hops(dcol, got, w_path_in, w_path_hid, state, live, drow, cot_t, n_path):
    entries = dcol.shape[1]
    slots = got.shape[0]
    n, width = state.shape
    hops = entries // n
    return pl.pallas_call(
        lambda *refs: _hop_kernel(hops, *refs),
        out_shape=(jax.ShapeDtypeStruct((n, width), jnp.bfloat16),
                   jax.ShapeDtypeStruct((slots, width), jnp.bfloat16),
                   jax.ShapeDtypeStruct((n_path, cot_t.shape[1] // n_path, width), jnp.float32)),
        in_specs=[pl.BlockSpec(memory_space=pltpu.VMEM)] * 8,
        out_specs=(pl.BlockSpec(memory_space=pltpu.VMEM),) * 3,
        scratch_shapes=[
            pltpu.VMEM((entries, w_path_in.shape[1]), jnp.float32),
            pltpu.VMEM((entries, width), jnp.bfloat16),
        ],
    )(dcol, got, w_path_in, w_path_hid, state, live, drow, cot_t)


def _all_kernel(n_grp, n_path, req_ref, links_ref, w_in_ref, w_hid_ref, state_ref, live_ref,
                drow_ref, cot_ref, w_lin_ref, w_lhid_ref, final_ref, next_ref, grad_ref,
                reqin, want, served, gotbuf, gotv, rsend, rrecv, asend, arecv,
                proj, msgs, outbuf, termbuf, recur_buf, route_t_buf, route_buf,
                inbuf, recv1, recv2, mid, msend, mrecv, send1, got1, send2, got2):
    f32 = jnp.float32
    g = lax.axis_index("grp")
    p = lax.axis_index("path")
    _greet(pltpu.get_barrier_semaphore(), g, p, n_grp, n_path, True)

    def link_recur():
        recur_buf[...] = jnp.dot(links_ref[...], w_lhid_ref[...], preferred_element_type=f32)
        route_t, route = _route_mats(drow_ref[...], route_buf.shape[0])
        route_t_buf[...] = route_t
        route_buf[...] = route

    def link_update():
        width = links_ref.shape[1]
        incoming = inbuf[...].reshape(-1, width)
        link_sum = lax.dot_general(want[...], incoming, (((0,), (0,)), ((), ())), preferred_element_type=f32)
        link_proj = jnp.dot(link_sum.astype(jnp.bfloat16), w_lin_ref[...], preferred_element_type=f32)
        recur = recur_buf[...]
        own = links_ref[...].astype(f32)
        reset = jax.nn.sigmoid(link_proj[:, :width] + recur[:, :width])
        update = jax.nn.sigmoid(link_proj[:, width : 2 * width] + recur[:, width : 2 * width])
        candidate = jnp.tanh(link_proj[:, 2 * width :] + reset * recur[:, 2 * width :])
        next_ref[...] = ((1.0 - update) * candidate + update * own).astype(next_ref.dtype)

    _fetch_kernel(n_grp, n_path, req_ref, links_ref, None, None,
                  reqin, want, served, gotbuf, rsend, rrecv, asend, arecv, greet=False, during=link_recur)
    hops = drow_ref.shape[1] // state_ref.shape[0]
    _hop_kernel(hops, route_t_buf, gotbuf, w_in_ref, w_hid_ref, state_ref, live_ref, route_buf, cot_ref,
                final_ref, outbuf, termbuf, proj, msgs)
    _message_kernel(n_grp, n_path, outbuf, termbuf, None, grad_ref,
                    inbuf, recv1, recv2, mid, msend, mrecv, send1, got1, send2, got2, greet=False,
                    after_msgs=link_update)


def run_all(req, own_links, w_path_in, w_path_hid, state, live, drow1, cot, w_link_in, w_link_hid,
            cap, n_grp, n_path):
    n_k, rows, lanes = req.shape
    link_dev, width = own_links.shape
    entries = drow1.shape[1]
    n = state.shape[0]
    share = cot.shape[1] // n_path
    vmem = pltpu.VMEM
    dma = pltpu.SemaphoreType.DMA
    return pl.pallas_call(
        lambda *refs: _all_kernel(n_grp, n_path, *refs),
        out_shape=(jax.ShapeDtypeStruct((n, width), jnp.bfloat16),
                   jax.ShapeDtypeStruct((link_dev, width), jnp.bfloat16),
                   jax.ShapeDtypeStruct((share, width), jnp.float32)),
        in_specs=[pl.BlockSpec(memory_space=vmem)] * 10,
        out_specs=(pl.BlockSpec(memory_space=vmem),) * 3,
        scratch_shapes=[
            vmem((n_k, rows, lanes), jnp.int32),
            vmem((n_k * cap, link_dev), jnp.bfloat16),
            vmem((n_k, cap, width), jnp.bfloat16),
            vmem((n_k, cap, width), jnp.bfloat16),
            vmem((n_k, cap, width), jnp.bfloat16),
            dma((n_path - 1,)), dma((n_path - 1,)), dma((n_path - 1,)), dma((n_path - 1,)),
            vmem((entries, w_path_in.shape[1]), jnp.float32),
            vmem((entries, width), jnp.bfloat16),
            vmem((n_k, cap, width), jnp.bfloat16),
            vmem((n_path, share, width), jnp.float32),
            vmem((link_dev, w_link_hid.shape[1]), jnp.float32),
            vmem((entries, n_k * cap), jnp.bfloat16),
            vmem((n_k * cap, entries), jnp.bfloat16),
            vmem((n_k, cap, width), jnp.bfloat16),
            vmem((n_path - 1, share, width), jnp.float32),
            vmem((n_grp - 1, share, width), jnp.float32),
            vmem((share, width), jnp.float32),
            dma((n_path - 1,)), dma((n_path - 1,)), dma((n_path - 1,)), dma((n_path - 1,)),
            dma((n_grp - 1,)), dma((n_grp - 1,)),
        ],
        compiler_params=pltpu.CompilerParams(collective_id=0, has_side_effects=True),
    )(req, own_links, w_path_in, w_path_hid, state, live, drow1, cot, w_link_in, w_link_hid)


def shards(
    link_state, path_state, path_links, w_path_in, w_path_hid, w_link_in, w_link_hid, cotangent
):
    bf16, f32 = jnp.bfloat16, jnp.float32
    own_links = link_state[0]
    link_dev, width = own_links.shape
    n_grp = lax.axis_size("grp")
    peer_count = lax.axis_size("path")
    me = lax.axis_index("path")
    path_count, hop_count = path_links.shape
    entries = path_count * hop_count
    capacity = entries // peer_count
    slots = peer_count * capacity
    flat_ids = path_links.reshape(-1)
    is_live = flat_ids >= 0
    owner_id = jnp.where(is_live, flat_ids // link_dev, peer_count)
    local_id = jnp.where(is_live, flat_ids % link_dev, 0)
    marks = (owner_id[:, None] == jnp.arange(peer_count)[None, :]).astype(bf16)
    order = jnp.arange(entries)
    earlier = (order[None, :] < order[:, None]).astype(bf16)
    before = jnp.dot(earlier, marks, preferred_element_type=f32)
    slot_id = jnp.sum(before * marks.astype(f32), axis=1).astype(jnp.int32)
    offset = lax.rem(owner_id - me + peer_count, peer_count)
    dest = jnp.where(is_live, offset * capacity + slot_id, -1)
    dest = dest.reshape(path_count, hop_count).T.reshape(-1)
    local_id = local_id.reshape(path_count, hop_count).T.reshape(-1)
    slot_ids = jnp.arange(slots)
    route = dest[None, :] == slot_ids[:, None]
    requests = jnp.sum(jnp.where(route, local_id[None, :] + 1, 0), axis=1) - 1
    req = jnp.full((peer_count, 8, 128), -1, jnp.int32)
    req = lax.dynamic_update_slice(req, requests.reshape(peer_count, 1, capacity), (0, 0, 0))
    path_final, link_next, read_grad = run_all(
        req, own_links, w_path_in, w_path_hid, path_state[0], path_links, dest[None, :],
        cotangent[0], w_link_in, w_link_hid, capacity, n_grp, peer_count)
    return (link_next[None], path_final[None], read_grad)


def solution(mesh):
    return jax.shard_map(
        shards,
        mesh=mesh,
        in_specs=(
            P("grp", "path", None),
            P("grp", "path", None),
            P("path", None),
            P(),
            P(),
            P(),
            P(),
            P("grp", "path", None),
        ),
        out_specs=(P("grp", "path", None), P("grp", "path", None), P("path", None)),
        check_vma=False,
    )
```

```python
import jax
import jax.numpy as jnp
from jax import lax
from jax.experimental import pallas as pl
from jax.experimental.pallas import tpu as pltpu
from jax.sharding import PartitionSpec as P

MESH = pl.DeviceIdType.MESH


def gated_update(projected, carried, w_hidden):
    width = carried.shape[1]
    recur = jnp.dot(carried.astype(jnp.bfloat16), w_hidden, preferred_element_type=jnp.float32)
    reset = jax.nn.sigmoid(projected[:, :width] + recur[:, :width])
    update = jax.nn.sigmoid(projected[:, width : 2 * width] + recur[:, width : 2 * width])
    candidate = jnp.tanh(projected[:, 2 * width :] + reset * recur[:, 2 * width :])
    return (1.0 - update) * candidate + update * carried


def _greet(barrier, g, p, n_grp, n_path, with_grp):
    def greet_path(k, c):
        pl.semaphore_signal(barrier, inc=1, device_id=(g, lax.rem(p + k, n_path)), device_id_type=MESH)
        return c

    def greet_grp(k, c):
        pl.semaphore_signal(barrier, inc=1, device_id=(lax.rem(g + k, n_grp), p), device_id_type=MESH)
        return c

    lax.fori_loop(1, n_path, greet_path, 0)
    count = n_path - 1
    if with_grp:
        lax.fori_loop(1, n_grp, greet_grp, 0)
        count += n_grp - 1
    pl.semaphore_wait(barrier, count)


def _ring_copies(src, dst, send, recv, g, p, n_path, sign):
    def make(k):
        return pltpu.make_async_remote_copy(
            src_ref=src.at[k], dst_ref=dst.at[k], send_sem=send.at[k - 1], recv_sem=recv.at[k - 1],
            device_id=(g, lax.rem(p + sign * k + n_path, n_path)), device_id_type=MESH)

    def start(k, c):
        make(k).start()
        return c

    def finish(k, c):
        copy = make(k)
        copy.wait_send()
        copy.wait_recv()
        return c

    return start, finish


def _fetch_kernel(n_grp, n_path, req_ref, links_ref, got_ref, ids_ref,
                  reqin, want, served, gotbuf, rsend, rrecv, asend, arecv, greet=True, during=None):
    g = lax.axis_index("grp")
    p = lax.axis_index("path")
    if greet:
        _greet(pltpu.get_barrier_semaphore(), g, p, n_grp, n_path, False)
    start_req, finish_req = _ring_copies(req_ref, reqin, rsend, rrecv, g, p, n_path, 1)
    lax.fori_loop(1, n_path, start_req, 0)
    reqin[0] = req_ref[0]
    n_k, cap = served.shape[0], served.shape[1]
    link_dev = links_ref.shape[0]
    lanes = lax.broadcasted_iota(jnp.int32, (1, link_dev), 1)
    start_ans, finish_ans = _ring_copies(served, gotbuf, asend, arecv, g, p, n_path, -1)
    part = n_k // 4
    for lo, hi in ((0, part), (part, 2 * part), (2 * part, 3 * part), (3 * part, n_k)):
        lax.fori_loop(max(lo, 1), hi, finish_req, 0)
        ids_t = jnp.transpose(reqin[lo:hi, 0, :])
        for k in range(lo, hi):
            want[k * cap : (k + 1) * cap, :] = (ids_t[0:cap, k - lo : k - lo + 1] == lanes).astype(jnp.bfloat16)
        rows = jnp.dot(want[lo * cap : hi * cap, :], links_ref[...], preferred_element_type=jnp.float32)
        served[lo:hi] = rows.astype(jnp.bfloat16).reshape(hi - lo, cap, rows.shape[-1])
        lax.fori_loop(max(lo, 1), hi, start_ans, 0)
    gotbuf[0] = served[0]
    if ids_ref is not None:
        ids_ref[...] = reqin[...]
    if during is not None:
        during()
    lax.fori_loop(1, n_path, finish_ans, 0)
    if got_ref is not None:
        got_ref[...] = gotbuf[...]


def fetch_rows(req, own_links, cap, n_grp, n_path):
    n_k, rows, lanes = req.shape
    width = own_links.shape[1]
    return pl.pallas_call(
        lambda *refs: _fetch_kernel(n_grp, n_path, *refs),
        out_shape=(jax.ShapeDtypeStruct((n_k, cap, width), jnp.bfloat16),
                   jax.ShapeDtypeStruct((n_k, rows, lanes), jnp.int32)),
        in_specs=[pl.BlockSpec(memory_space=pltpu.VMEM)] * 2,
        out_specs=(pl.BlockSpec(memory_space=pltpu.VMEM),) * 2,
        scratch_shapes=[
            pltpu.VMEM((n_k, rows, lanes), jnp.int32),
            pltpu.VMEM((n_k * cap, own_links.shape[0]), jnp.bfloat16),
            pltpu.VMEM((n_k, cap, width), jnp.bfloat16),
            pltpu.VMEM((n_k, cap, width), jnp.bfloat16),
            pltpu.SemaphoreType.DMA((n_path - 1,)),
            pltpu.SemaphoreType.DMA((n_path - 1,)),
            pltpu.SemaphoreType.DMA((n_path - 1,)),
            pltpu.SemaphoreType.DMA((n_path - 1,)),
        ],
        compiler_params=pltpu.CompilerParams(collective_id=0, has_side_effects=True),
    )(req, own_links)


def _message_kernel(n_grp, n_path, out_ref, term_ref, inc_ref, grad_ref,
                    inbuf, recv1, recv2, mid, msend, mrecv, send1, got1, send2, got2, greet=True,
                    after_msgs=None, send_msgs=None):
    g = lax.axis_index("grp")
    p = lax.axis_index("path")
    if greet:
        _greet(pltpu.get_barrier_semaphore(), g, p, n_grp, n_path, True)
    start_msg, finish_msg = _ring_copies(out_ref, inbuf, msend, mrecv, g, p, n_path, 1)

    def path_copy(k, q):
        return pltpu.make_async_remote_copy(
            src_ref=term_ref.at[q], dst_ref=recv1.at[k - 1], send_sem=send1.at[k - 1],
            recv_sem=got1.at[k - 1], device_id=(g, q), device_id_type=MESH)

    def start1(k, c):
        path_copy(k, lax.rem(p + k, n_path)).start()
        return c

    def finish1(k, c):
        copy = path_copy(k, lax.rem(p + k, n_path))
        copy.wait_send()
        copy.wait_recv()
        return c

    lax.fori_loop(1, n_path, start1, 0)
    if send_msgs is None:
        lax.fori_loop(1, n_path, start_msg, 0)
    else:
        send_msgs(start_msg)
    inbuf[0] = out_ref[0]
    lax.fori_loop(1, n_path, finish1, 0)
    mid[...] = term_ref[p] + jnp.sum(recv1[...], axis=0)

    def grp_copy(k, h):
        return pltpu.make_async_remote_copy(
            src_ref=mid, dst_ref=recv2.at[k - 1], send_sem=send2.at[k - 1],
            recv_sem=got2.at[k - 1], device_id=(h, p), device_id_type=MESH)

    def start2(k, c):
        grp_copy(k, lax.rem(g + k, n_grp)).start()
        return c

    def finish2(k, c):
        copy = grp_copy(k, lax.rem(g + k, n_grp))
        copy.wait_send()
        copy.wait_recv()
        return c

    lax.fori_loop(1, n_grp, start2, 0)
    lax.fori_loop(1, n_path, finish_msg, 0)
    if inc_ref is not None:
        inc_ref[...] = inbuf[...]
    if after_msgs is not None:
        after_msgs()
    lax.fori_loop(1, n_grp, finish2, 0)
    grad_ref[...] = mid[...] + jnp.sum(recv2[...], axis=0)


def exchange_messages(outgoing, term, n_grp, n_path):
    n_k, cap, width = outgoing.shape
    _, rows, gwidth = term.shape
    return pl.pallas_call(
        lambda *refs: _message_kernel(n_grp, n_path, *refs),
        out_shape=(jax.ShapeDtypeStruct((n_k, cap, width), jnp.bfloat16),
                   jax.ShapeDtypeStruct((rows, gwidth), jnp.float32)),
        in_specs=[pl.BlockSpec(memory_space=pltpu.VMEM)] * 2,
        out_specs=(pl.BlockSpec(memory_space=pltpu.VMEM),) * 2,
        scratch_shapes=[
            pltpu.VMEM((n_k, cap, width), jnp.bfloat16),
            pltpu.VMEM((n_path - 1, rows, gwidth), jnp.float32),
            pltpu.VMEM((n_grp - 1, rows, gwidth), jnp.float32),
            pltpu.VMEM((rows, gwidth), jnp.float32),
            pltpu.SemaphoreType.DMA((n_path - 1,)),
            pltpu.SemaphoreType.DMA((n_path - 1,)),
            pltpu.SemaphoreType.DMA((n_path - 1,)),
            pltpu.SemaphoreType.DMA((n_path - 1,)),
            pltpu.SemaphoreType.DMA((n_grp - 1,)),
            pltpu.SemaphoreType.DMA((n_grp - 1,)),
        ],
        compiler_params=pltpu.CompilerParams(collective_id=1, has_side_effects=True),
    )(outgoing, term)


def _route_mats(drow, slots):
    dcol = jnp.transpose(jnp.broadcast_to(drow, (8, drow.shape[1])))[:, 0:1]
    route_t = (dcol == lax.broadcasted_iota(jnp.int32, (1, slots), 1)).astype(jnp.bfloat16)
    route = (lax.broadcasted_iota(jnp.int32, (slots, 1), 0) == drow).astype(jnp.bfloat16)
    return route_t, route


def _hop_kernel(hops, route_t_ref, got_ref, w_in_ref, w_hid_ref, state_ref, live_ref, route_ref, cot_t_ref,
                final_ref, out_ref, term_ref, proj, msgs):
    bf16, f32 = jnp.bfloat16, jnp.float32
    width = got_ref.shape[-1]
    got = got_ref[...].reshape(-1, width)
    fetched = jnp.dot(route_t_ref[...], got, preferred_element_type=f32).astype(bf16)
    proj[...] = jnp.dot(fetched, w_in_ref[...], preferred_element_type=f32)
    carried = state_ref[...].astype(f32)
    n, width = carried.shape
    for h in range(hops):
        p_h = proj[h * n : (h + 1) * n, :]
        renewed = gated_update(p_h, carried, w_hid_ref[...])
        carried = jnp.where(live_ref[:, h : h + 1] >= 0, renewed, carried)
        msgs[h * n : (h + 1) * n, :] = carried.astype(bf16)
    final = carried.astype(bf16)
    final_ref[...] = final
    if out_ref is not None:
        out_ref[...] = jnp.dot(route_ref[...], msgs[...], preferred_element_type=f32).astype(bf16).reshape(out_ref.shape)
    cot_t = jnp.transpose(cot_t_ref[...].astype(f32)).astype(bf16)
    term = jnp.dot(cot_t, final, preferred_element_type=f32)
    share = term_ref.shape[1]
    for q in range(term_ref.shape[0]):
        term_ref[q] = term[q * share : (q + 1) * share, :]


def run_hops(dcol, got, w_path_in, w_path_hid, state, live, drow, cot_t, n_path):
    entries = dcol.shape[1]
    slots = got.shape[0]
    n, width = state.shape
    hops = entries // n
    return pl.pallas_call(
        lambda *refs: _hop_kernel(hops, *refs),
        out_shape=(jax.ShapeDtypeStruct((n, width), jnp.bfloat16),
                   jax.ShapeDtypeStruct((slots, width), jnp.bfloat16),
                   jax.ShapeDtypeStruct((n_path, cot_t.shape[1] // n_path, width), jnp.float32)),
        in_specs=[pl.BlockSpec(memory_space=pltpu.VMEM)] * 8,
        out_specs=(pl.BlockSpec(memory_space=pltpu.VMEM),) * 3,
        scratch_shapes=[
            pltpu.VMEM((entries, w_path_in.shape[1]), jnp.float32),
            pltpu.VMEM((entries, width), jnp.bfloat16),
        ],
    )(dcol, got, w_path_in, w_path_hid, state, live, drow, cot_t)


def _all_kernel(n_grp, n_path, req_ref, links_ref, w_in_ref, w_hid_ref, state_ref, live_ref,
                drow_ref, cot_ref, w_lin_ref, w_lhid_ref, final_ref, next_ref, grad_ref,
                reqin, want, served, gotbuf, gotv, rsend, rrecv, asend, arecv,
                proj, msgs, outbuf, termbuf, recur_buf, route_t_buf, route_buf,
                inbuf, recv1, recv2, mid, msend, mrecv, send1, got1, send2, got2):
    f32 = jnp.float32
    g = lax.axis_index("grp")
    p = lax.axis_index("path")
    _greet(pltpu.get_barrier_semaphore(), g, p, n_grp, n_path, True)

    def link_recur():
        recur_buf[...] = jnp.dot(links_ref[...], w_lhid_ref[...], preferred_element_type=f32)
        route_t, route = _route_mats(drow_ref[...], route_buf.shape[0])
        route_t_buf[...] = route_t
        route_buf[...] = route

    def link_update():
        width = links_ref.shape[1]
        incoming = inbuf[...].reshape(-1, width)
        link_sum = lax.dot_general(want[...], incoming, (((0,), (0,)), ((), ())), preferred_element_type=f32)
        link_proj = jnp.dot(link_sum.astype(jnp.bfloat16), w_lin_ref[...], preferred_element_type=f32)
        recur = recur_buf[...]
        own = links_ref[...].astype(f32)
        reset = jax.nn.sigmoid(link_proj[:, :width] + recur[:, :width])
        update = jax.nn.sigmoid(link_proj[:, width : 2 * width] + recur[:, width : 2 * width])
        candidate = jnp.tanh(link_proj[:, 2 * width :] + reset * recur[:, 2 * width :])
        next_ref[...] = ((1.0 - update) * candidate + update * own).astype(next_ref.dtype)

    _fetch_kernel(n_grp, n_path, req_ref, links_ref, None, None,
                  reqin, want, served, gotbuf, rsend, rrecv, asend, arecv, greet=False, during=link_recur)
    hops = drow_ref.shape[1] // state_ref.shape[0]
    _hop_kernel(hops, route_t_buf, gotbuf, w_in_ref, w_hid_ref, state_ref, live_ref, route_buf, cot_ref,
                final_ref, None, termbuf, proj, msgs)

    def send_msgs(start_msg):
        n_k, cap, width = outbuf.shape
        half = n_k // 2
        for lo, hi in ((0, half), (half, n_k)):
            part = jnp.dot(route_buf[lo * cap : hi * cap, :], msgs[...], preferred_element_type=f32)
            outbuf[lo:hi] = part.astype(jnp.bfloat16).reshape(hi - lo, cap, width)
            lax.fori_loop(max(lo, 1), hi, start_msg, 0)
    _message_kernel(n_grp, n_path, outbuf, termbuf, None, grad_ref,
                    inbuf, recv1, recv2, mid, msend, mrecv, send1, got1, send2, got2, greet=False,
                    after_msgs=link_update, send_msgs=send_msgs)


def run_all(req, own_links, w_path_in, w_path_hid, state, live, drow1, cot, w_link_in, w_link_hid,
            cap, n_grp, n_path):
    n_k, rows, lanes = req.shape
    link_dev, width = own_links.shape
    entries = drow1.shape[1]
    n = state.shape[0]
    share = cot.shape[1] // n_path
    vmem = pltpu.VMEM
    dma = pltpu.SemaphoreType.DMA
    return pl.pallas_call(
        lambda *refs: _all_kernel(n_grp, n_path, *refs),
        out_shape=(jax.ShapeDtypeStruct((n, width), jnp.bfloat16),
                   jax.ShapeDtypeStruct((link_dev, width), jnp.bfloat16),
                   jax.ShapeDtypeStruct((share, width), jnp.float32)),
        in_specs=[pl.BlockSpec(memory_space=vmem)] * 10,
        out_specs=(pl.BlockSpec(memory_space=vmem),) * 3,
        scratch_shapes=[
            vmem((n_k, rows, lanes), jnp.int32),
            vmem((n_k * cap, link_dev), jnp.bfloat16),
            vmem((n_k, cap, width), jnp.bfloat16),
            vmem((n_k, cap, width), jnp.bfloat16),
            vmem((n_k, cap, width), jnp.bfloat16),
            dma((n_path - 1,)), dma((n_path - 1,)), dma((n_path - 1,)), dma((n_path - 1,)),
            vmem((entries, w_path_in.shape[1]), jnp.float32),
            vmem((entries, width), jnp.bfloat16),
            vmem((n_k, cap, width), jnp.bfloat16),
            vmem((n_path, share, width), jnp.float32),
            vmem((link_dev, w_link_hid.shape[1]), jnp.float32),
            vmem((entries, n_k * cap), jnp.bfloat16),
            vmem((n_k * cap, entries), jnp.bfloat16),
            vmem((n_k, cap, width), jnp.bfloat16),
            vmem((n_path - 1, share, width), jnp.float32),
            vmem((n_grp - 1, share, width), jnp.float32),
            vmem((share, width), jnp.float32),
            dma((n_path - 1,)), dma((n_path - 1,)), dma((n_path - 1,)), dma((n_path - 1,)),
            dma((n_grp - 1,)), dma((n_grp - 1,)),
        ],
        compiler_params=pltpu.CompilerParams(collective_id=0, has_side_effects=True),
    )(req, own_links, w_path_in, w_path_hid, state, live, drow1, cot, w_link_in, w_link_hid)


def shards(
    link_state, path_state, path_links, w_path_in, w_path_hid, w_link_in, w_link_hid, cotangent
):
    bf16, f32 = jnp.bfloat16, jnp.float32
    own_links = link_state[0]
    link_dev, width = own_links.shape
    n_grp = lax.axis_size("grp")
    peer_count = lax.axis_size("path")
    me = lax.axis_index("path")
    path_count, hop_count = path_links.shape
    entries = path_count * hop_count
    capacity = entries // peer_count
    slots = peer_count * capacity
    flat_ids = path_links.reshape(-1)
    is_live = flat_ids >= 0
    owner_id = jnp.where(is_live, flat_ids // link_dev, peer_count)
    local_id = jnp.where(is_live, flat_ids % link_dev, 0)
    marks = (owner_id[:, None] == jnp.arange(peer_count)[None, :]).astype(bf16)
    order = jnp.arange(entries)
    earlier = (order[None, :] < order[:, None]).astype(bf16)
    before = jnp.dot(earlier, marks, preferred_element_type=f32)
    slot_id = jnp.sum(before * marks.astype(f32), axis=1).astype(jnp.int32)
    offset = lax.rem(owner_id - me + peer_count, peer_count)
    dest = jnp.where(is_live, offset * capacity + slot_id, -1)
    dest = dest.reshape(path_count, hop_count).T.reshape(-1)
    local_id = local_id.reshape(path_count, hop_count).T.reshape(-1)
    slot_ids = jnp.arange(slots)
    route = dest[None, :] == slot_ids[:, None]
    requests = jnp.sum(jnp.where(route, local_id[None, :] + 1, 0), axis=1) - 1
    req = jnp.full((peer_count, 8, 128), -1, jnp.int32)
    req = lax.dynamic_update_slice(req, requests.reshape(peer_count, 1, capacity), (0, 0, 0))
    path_final, link_next, read_grad = run_all(
        req, own_links, w_path_in, w_path_hid, path_state[0], path_links, dest[None, :],
        cotangent[0], w_link_in, w_link_hid, capacity, n_grp, peer_count)
    return (link_next[None], path_final[None], read_grad)


def solution(mesh):
    return jax.shard_map(
        shards,
        mesh=mesh,
        in_specs=(
            P("grp", "path", None),
            P("grp", "path", None),
            P("path", None),
            P(),
            P(),
            P(),
            P(),
            P("grp", "path", None),
        ),
        out_specs=(P("grp", "path", None), P("grp", "path", None), P("path", None)),
        check_vma=False,
    )
```

```python
import jax
import jax.numpy as jnp
from jax import lax
from jax.experimental import pallas as pl
from jax.experimental.pallas import tpu as pltpu
from jax.sharding import PartitionSpec as P

MESH = pl.DeviceIdType.MESH


def gated_update(projected, carried, w_hidden):
    width = carried.shape[1]
    recur = jnp.dot(carried.astype(jnp.bfloat16), w_hidden, preferred_element_type=jnp.float32)
    reset = jax.nn.sigmoid(projected[:, :width] + recur[:, :width])
    update = jax.nn.sigmoid(projected[:, width : 2 * width] + recur[:, width : 2 * width])
    candidate = jnp.tanh(projected[:, 2 * width :] + reset * recur[:, 2 * width :])
    return (1.0 - update) * candidate + update * carried


def _greet(barrier, g, p, n_grp, n_path, with_grp):
    def greet_path(k, c):
        pl.semaphore_signal(barrier, inc=1, device_id=(g, lax.rem(p + k, n_path)), device_id_type=MESH)
        return c

    def greet_grp(k, c):
        pl.semaphore_signal(barrier, inc=1, device_id=(lax.rem(g + k, n_grp), p), device_id_type=MESH)
        return c

    lax.fori_loop(1, n_path, greet_path, 0)
    count = n_path - 1
    if with_grp:
        lax.fori_loop(1, n_grp, greet_grp, 0)
        count += n_grp - 1
    pl.semaphore_wait(barrier, count)


def _ring_copies(src, dst, send, recv, g, p, n_path, sign):
    def make(k):
        return pltpu.make_async_remote_copy(
            src_ref=src.at[k], dst_ref=dst.at[k], send_sem=send.at[k - 1], recv_sem=recv.at[k - 1],
            device_id=(g, lax.rem(p + sign * k + n_path, n_path)), device_id_type=MESH)

    def start(k, c):
        make(k).start()
        return c

    def finish(k, c):
        copy = make(k)
        copy.wait_send()
        copy.wait_recv()
        return c

    return start, finish


def _fetch_kernel(n_grp, n_path, req_ref, links_ref, got_ref, ids_ref,
                  reqin, want, served, gotbuf, rsend, rrecv, asend, arecv, greet=True, during=None):
    g = lax.axis_index("grp")
    p = lax.axis_index("path")
    if greet:
        _greet(pltpu.get_barrier_semaphore(), g, p, n_grp, n_path, False)
    start_req, finish_req = _ring_copies(req_ref, reqin, rsend, rrecv, g, p, n_path, 1)
    lax.fori_loop(1, n_path, start_req, 0)
    reqin[0] = req_ref[0]
    n_k, cap = served.shape[0], served.shape[1]
    link_dev = links_ref.shape[0]
    lanes = lax.broadcasted_iota(jnp.int32, (1, link_dev), 1)
    start_ans, finish_ans = _ring_copies(served, gotbuf, asend, arecv, g, p, n_path, -1)
    part = n_k // 4
    for lo, hi in ((0, part), (part, 2 * part), (2 * part, 3 * part), (3 * part, n_k)):
        lax.fori_loop(max(lo, 1), hi, finish_req, 0)
        ids_t = jnp.transpose(reqin[lo:hi, 0, :])
        for k in range(lo, hi):
            want[k * cap : (k + 1) * cap, :] = (ids_t[0:cap, k - lo : k - lo + 1] == lanes).astype(jnp.bfloat16)
        rows = jnp.dot(want[lo * cap : hi * cap, :], links_ref[...], preferred_element_type=jnp.float32)
        served[lo:hi] = rows.astype(jnp.bfloat16).reshape(hi - lo, cap, rows.shape[-1])
        lax.fori_loop(max(lo, 1), hi, start_ans, 0)
    gotbuf[0] = served[0]
    if ids_ref is not None:
        ids_ref[...] = reqin[...]
    if during is not None:
        during()
    lax.fori_loop(1, n_path, finish_ans, 0)
    if got_ref is not None:
        got_ref[...] = gotbuf[...]


def fetch_rows(req, own_links, cap, n_grp, n_path):
    n_k, rows, lanes = req.shape
    width = own_links.shape[1]
    return pl.pallas_call(
        lambda *refs: _fetch_kernel(n_grp, n_path, *refs),
        out_shape=(jax.ShapeDtypeStruct((n_k, cap, width), jnp.bfloat16),
                   jax.ShapeDtypeStruct((n_k, rows, lanes), jnp.int32)),
        in_specs=[pl.BlockSpec(memory_space=pltpu.VMEM)] * 2,
        out_specs=(pl.BlockSpec(memory_space=pltpu.VMEM),) * 2,
        scratch_shapes=[
            pltpu.VMEM((n_k, rows, lanes), jnp.int32),
            pltpu.VMEM((n_k * cap, own_links.shape[0]), jnp.bfloat16),
            pltpu.VMEM((n_k, cap, width), jnp.bfloat16),
            pltpu.VMEM((n_k, cap, width), jnp.bfloat16),
            pltpu.SemaphoreType.DMA((n_path - 1,)),
            pltpu.SemaphoreType.DMA((n_path - 1,)),
            pltpu.SemaphoreType.DMA((n_path - 1,)),
            pltpu.SemaphoreType.DMA((n_path - 1,)),
        ],
        compiler_params=pltpu.CompilerParams(collective_id=0, has_side_effects=True),
    )(req, own_links)


def _message_kernel(n_grp, n_path, out_ref, term_ref, inc_ref, grad_ref,
                    inbuf, recv1, recv2, mid, msend, mrecv, send1, got1, send2, got2, greet=True,
                    after_msgs=None):
    g = lax.axis_index("grp")
    p = lax.axis_index("path")
    if greet:
        _greet(pltpu.get_barrier_semaphore(), g, p, n_grp, n_path, True)
    start_msg, finish_msg = _ring_copies(out_ref, inbuf, msend, mrecv, g, p, n_path, 1)

    def path_copy(k, q):
        return pltpu.make_async_remote_copy(
            src_ref=term_ref.at[q], dst_ref=recv1.at[k - 1], send_sem=send1.at[k - 1],
            recv_sem=got1.at[k - 1], device_id=(g, q), device_id_type=MESH)

    def start1(k, c):
        path_copy(k, lax.rem(p + k, n_path)).start()
        return c

    def finish1(k, c):
        copy = path_copy(k, lax.rem(p + k, n_path))
        copy.wait_send()
        copy.wait_recv()
        return c

    lax.fori_loop(1, n_path, start1, 0)
    lax.fori_loop(1, n_path, start_msg, 0)
    inbuf[0] = out_ref[0]
    lax.fori_loop(1, n_path, finish1, 0)
    mid[...] = term_ref[p] + jnp.sum(recv1[...], axis=0)

    def grp_copy(k, h):
        return pltpu.make_async_remote_copy(
            src_ref=mid, dst_ref=recv2.at[k - 1], send_sem=send2.at[k - 1],
            recv_sem=got2.at[k - 1], device_id=(h, p), device_id_type=MESH)

    def start2(k, c):
        grp_copy(k, lax.rem(g + k, n_grp)).start()
        return c

    def finish2(k, c):
        copy = grp_copy(k, lax.rem(g + k, n_grp))
        copy.wait_send()
        copy.wait_recv()
        return c

    lax.fori_loop(1, n_grp, start2, 0)
    lax.fori_loop(1, n_path, finish_msg, 0)
    if inc_ref is not None:
        inc_ref[...] = inbuf[...]
    if after_msgs is not None:
        after_msgs()
    lax.fori_loop(1, n_grp, finish2, 0)
    grad_ref[...] = mid[...] + jnp.sum(recv2[...], axis=0)


def exchange_messages(outgoing, term, n_grp, n_path):
    n_k, cap, width = outgoing.shape
    _, rows, gwidth = term.shape
    return pl.pallas_call(
        lambda *refs: _message_kernel(n_grp, n_path, *refs),
        out_shape=(jax.ShapeDtypeStruct((n_k, cap, width), jnp.bfloat16),
                   jax.ShapeDtypeStruct((rows, gwidth), jnp.float32)),
        in_specs=[pl.BlockSpec(memory_space=pltpu.VMEM)] * 2,
        out_specs=(pl.BlockSpec(memory_space=pltpu.VMEM),) * 2,
        scratch_shapes=[
            pltpu.VMEM((n_k, cap, width), jnp.bfloat16),
            pltpu.VMEM((n_path - 1, rows, gwidth), jnp.float32),
            pltpu.VMEM((n_grp - 1, rows, gwidth), jnp.float32),
            pltpu.VMEM((rows, gwidth), jnp.float32),
            pltpu.SemaphoreType.DMA((n_path - 1,)),
            pltpu.SemaphoreType.DMA((n_path - 1,)),
            pltpu.SemaphoreType.DMA((n_path - 1,)),
            pltpu.SemaphoreType.DMA((n_path - 1,)),
            pltpu.SemaphoreType.DMA((n_grp - 1,)),
            pltpu.SemaphoreType.DMA((n_grp - 1,)),
        ],
        compiler_params=pltpu.CompilerParams(collective_id=1, has_side_effects=True),
    )(outgoing, term)


def _route_mats(drow, slots):
    dcol = jnp.transpose(jnp.broadcast_to(drow, (8, drow.shape[1])))[:, 0:1]
    route_t = (dcol == lax.broadcasted_iota(jnp.int32, (1, slots), 1)).astype(jnp.bfloat16)
    route = (lax.broadcasted_iota(jnp.int32, (slots, 1), 0) == drow).astype(jnp.bfloat16)
    return route_t, route


def _hop_kernel(hops, route_t_ref, got_ref, w_in_ref, w_hid_ref, state_ref, live_ref, route_ref, cot_t_ref,
                final_ref, out_ref, term_ref, proj, msgs):
    bf16, f32 = jnp.bfloat16, jnp.float32
    width = got_ref.shape[-1]
    got = got_ref[...].reshape(-1, width)
    fetched = jnp.dot(route_t_ref[...], got, preferred_element_type=f32).astype(bf16)
    proj[...] = jnp.dot(fetched, w_in_ref[...], preferred_element_type=f32)
    carried = state_ref[...].astype(f32)
    n, width = carried.shape
    for h in range(hops):
        p_h = proj[h * n : (h + 1) * n, :]
        renewed = gated_update(p_h, carried, w_hid_ref[...])
        carried = jnp.where(live_ref[:, h : h + 1] >= 0, renewed, carried)
        msgs[h * n : (h + 1) * n, :] = carried.astype(bf16)
    final = carried.astype(bf16)
    final_ref[...] = final
    out_ref[...] = jnp.dot(route_ref[...], msgs[...], preferred_element_type=f32).astype(bf16).reshape(out_ref.shape)
    cot_t = jnp.transpose(cot_t_ref[...].astype(f32)).astype(bf16)
    term = jnp.dot(cot_t, final, preferred_element_type=f32)
    share = term_ref.shape[1]
    for q in range(term_ref.shape[0]):
        term_ref[q] = term[q * share : (q + 1) * share, :]


def run_hops(dcol, got, w_path_in, w_path_hid, state, live, drow, cot_t, n_path):
    entries = dcol.shape[1]
    slots = got.shape[0]
    n, width = state.shape
    hops = entries // n
    return pl.pallas_call(
        lambda *refs: _hop_kernel(hops, *refs),
        out_shape=(jax.ShapeDtypeStruct((n, width), jnp.bfloat16),
                   jax.ShapeDtypeStruct((slots, width), jnp.bfloat16),
                   jax.ShapeDtypeStruct((n_path, cot_t.shape[1] // n_path, width), jnp.float32)),
        in_specs=[pl.BlockSpec(memory_space=pltpu.VMEM)] * 8,
        out_specs=(pl.BlockSpec(memory_space=pltpu.VMEM),) * 3,
        scratch_shapes=[
            pltpu.VMEM((entries, w_path_in.shape[1]), jnp.float32),
            pltpu.VMEM((entries, width), jnp.bfloat16),
        ],
    )(dcol, got, w_path_in, w_path_hid, state, live, drow, cot_t)


def _all_kernel(n_grp, n_path, req_ref, links_ref, w_in_ref, w_hid_ref, state_ref, live_ref,
                drow_ref, cot_ref, w_lin_ref, w_lhid_ref, final_ref, next_ref, grad_ref,
                reqin, want, served, gotbuf, gotv, rsend, rrecv, asend, arecv,
                proj, msgs, outbuf, termbuf, recur_buf, route_t_buf, route_buf,
                inbuf, recv1, recv2, mid, msend, mrecv, send1, got1, send2, got2):
    f32 = jnp.float32
    g = lax.axis_index("grp")
    p = lax.axis_index("path")
    _greet(pltpu.get_barrier_semaphore(), g, p, n_grp, n_path, True)

    def link_recur():
        recur_buf[...] = jnp.dot(links_ref[...], w_lhid_ref[...], preferred_element_type=f32)
        route_t, route = _route_mats(drow_ref[...], route_buf.shape[0])
        route_t_buf[...] = route_t
        route_buf[...] = route

    def link_update():
        width = links_ref.shape[1]
        incoming = inbuf[...].reshape(-1, width)
        link_sum = lax.dot_general(want[...], incoming, (((0,), (0,)), ((), ())), preferred_element_type=f32)
        link_proj = jnp.dot(link_sum.astype(jnp.bfloat16), w_lin_ref[...], preferred_element_type=f32)
        recur = recur_buf[...]
        own = links_ref[...].astype(f32)
        reset = jax.nn.sigmoid(link_proj[:, :width] + recur[:, :width])
        update = jax.nn.sigmoid(link_proj[:, width : 2 * width] + recur[:, width : 2 * width])
        candidate = jnp.tanh(link_proj[:, 2 * width :] + reset * recur[:, 2 * width :])
        next_ref[...] = ((1.0 - update) * candidate + update * own).astype(next_ref.dtype)

    _fetch_kernel(n_grp, n_path, req_ref, links_ref, None, None,
                  reqin, want, served, gotbuf, rsend, rrecv, asend, arecv, greet=False, during=link_recur)
    hops = drow_ref.shape[1] // state_ref.shape[0]
    _hop_kernel(hops, route_t_buf, gotbuf, w_in_ref, w_hid_ref, state_ref, live_ref, route_buf, cot_ref,
                final_ref, outbuf, termbuf, proj, msgs)
    _message_kernel(n_grp, n_path, outbuf, termbuf, None, grad_ref,
                    inbuf, recv1, recv2, mid, msend, mrecv, send1, got1, send2, got2, greet=False,
                    after_msgs=link_update)


def run_all(req, own_links, w_path_in, w_path_hid, state, live, drow1, cot, w_link_in, w_link_hid,
            cap, n_grp, n_path):
    n_k, rows, lanes = req.shape
    link_dev, width = own_links.shape
    entries = drow1.shape[1]
    n = state.shape[0]
    share = cot.shape[1] // n_path
    vmem = pltpu.VMEM
    dma = pltpu.SemaphoreType.DMA
    return pl.pallas_call(
        lambda *refs: _all_kernel(n_grp, n_path, *refs),
        out_shape=(jax.ShapeDtypeStruct((n, width), jnp.bfloat16),
                   jax.ShapeDtypeStruct((link_dev, width), jnp.bfloat16),
                   jax.ShapeDtypeStruct((share, width), jnp.float32)),
        in_specs=[pl.BlockSpec(memory_space=vmem)] * 10,
        out_specs=(pl.BlockSpec(memory_space=vmem),) * 3,
        scratch_shapes=[
            vmem((n_k, rows, lanes), jnp.int32),
            vmem((n_k * cap, link_dev), jnp.bfloat16),
            vmem((n_k, cap, width), jnp.bfloat16),
            vmem((n_k, cap, width), jnp.bfloat16),
            vmem((n_k, cap, width), jnp.bfloat16),
            dma((n_path - 1,)), dma((n_path - 1,)), dma((n_path - 1,)), dma((n_path - 1,)),
            vmem((entries, w_path_in.shape[1]), jnp.float32),
            vmem((entries, width), jnp.bfloat16),
            vmem((n_k, cap, width), jnp.bfloat16),
            vmem((n_path, share, width), jnp.float32),
            vmem((link_dev, w_link_hid.shape[1]), jnp.float32),
            vmem((entries, n_k * cap), jnp.bfloat16),
            vmem((n_k * cap, entries), jnp.bfloat16),
            vmem((n_k, cap, width), jnp.bfloat16),
            vmem((n_path - 1, share, width), jnp.float32),
            vmem((n_grp - 1, share, width), jnp.float32),
            vmem((share, width), jnp.float32),
            dma((n_path - 1,)), dma((n_path - 1,)), dma((n_path - 1,)), dma((n_path - 1,)),
            dma((n_grp - 1,)), dma((n_grp - 1,)),
        ],
        compiler_params=pltpu.CompilerParams(collective_id=0, has_side_effects=True),
    )(req, own_links, w_path_in, w_path_hid, state, live, drow1, cot, w_link_in, w_link_hid)


def shards(
    link_state, path_state, path_links, w_path_in, w_path_hid, w_link_in, w_link_hid, cotangent
):
    bf16, f32 = jnp.bfloat16, jnp.float32
    own_links = link_state[0]
    link_dev, width = own_links.shape
    n_grp = lax.axis_size("grp")
    peer_count = lax.axis_size("path")
    me = lax.axis_index("path")
    path_count, hop_count = path_links.shape
    entries = path_count * hop_count
    capacity = entries // peer_count
    slots = peer_count * capacity
    flat_ids = path_links.T.reshape(-1)
    is_live = flat_ids >= 0
    owner_id = jnp.where(is_live, flat_ids // link_dev, peer_count)
    local_id = jnp.where(is_live, flat_ids % link_dev, 0)
    marks = (owner_id[:, None] == jnp.arange(peer_count)[None, :]).astype(bf16)
    order = jnp.arange(entries)
    earlier = (order[None, :] < order[:, None]).astype(bf16)
    before = jnp.dot(earlier, marks, preferred_element_type=f32)
    slot_id = jnp.sum(before * marks.astype(f32), axis=1).astype(jnp.int32)
    offset = lax.rem(owner_id - me + peer_count, peer_count)
    dest = jnp.where(is_live, offset * capacity + slot_id, -1)
    slot_ids = jnp.arange(slots)
    route = dest[None, :] == slot_ids[:, None]
    requests = jnp.sum(jnp.where(route, local_id[None, :] + 1, 0), axis=1) - 1
    req = jnp.full((peer_count, 8, 128), -1, jnp.int32)
    req = lax.dynamic_update_slice(req, requests.reshape(peer_count, 1, capacity), (0, 0, 0))
    path_final, link_next, read_grad = run_all(
        req, own_links, w_path_in, w_path_hid, path_state[0], path_links, dest[None, :],
        cotangent[0], w_link_in, w_link_hid, capacity, n_grp, peer_count)
    return (link_next[None], path_final[None], read_grad)


def solution(mesh):
    return jax.shard_map(
        shards,
        mesh=mesh,
        in_specs=(
            P("grp", "path", None),
            P("grp", "path", None),
            P("path", None),
            P(),
            P(),
            P(),
            P(),
            P("grp", "path", None),
        ),
        out_specs=(P("grp", "path", None), P("grp", "path", None), P("path", None)),
        check_vma=False,
    )
```
